32 devices in a mesh: req: 4 (over y, x), head: 8 (over z, core).
Axes of the slice: x: 2, y: 2, z: 4, core: 2. Of those that a mesh axis runs over, the one named last changes fastest.
Arguments:
- hidden: bfloat16 [4, 256, 5120], P('req', 'head'), may hold values from -6 to 6
- cached_len: int32 [4], P('req'), may hold values from 2 to 4096, as said below
- attn_gain: float32 [5120], replicated, may hold values from 0.5 to 1.5
- query_key_value_weight: bfloat16 [5120, 6144], P(None, 'head'), may hold values from -0.078125 to 0.078125
- b_qkv: bfloat16 [6144], P('head'), may hold values from -1.5 to 1.5
- key_cache: bfloat16 [4, 4096, 1024], P('req', 'head'), may hold values from -4000 to 4000
- value_cache: bfloat16 [4, 4096, 1024], P('req', 'head'), may hold values from -6 to 6
- w_out: bfloat16 [4096, 5120], P('head'), may hold values from -0.09375 to 0.09375
- ffn_gain: float32 [5120], replicated, may hold values from 0.5 to 1.5
- w_gate: bfloat16 [5120, 13824], P(None, 'head'), may hold values from -0.078125 to 0.078125
- w_up: bfloat16 [5120, 13824], P(None, 'head'), may hold values from -0.078125 to 0.078125
- w_down: bfloat16 [13824, 5120], P('head'), may hold values from -0.0546875 to 0.0546875
Outputs:
- layer_out: bfloat16 [4, 256, 5120], P('req', 'head')
- new_keys: bfloat16 [4, 256, 1024], P('req', 'head')
- new_values: bfloat16 [4, 256, 1024], P('req', 'head')
The draws below stay inside these ranges and needn't reach their ends.
Inputs may be any that keep to these rules, and one draw needn't show every extreme that they name: `cached_len`: about half of the requests have nearly full caches, within 512 of 4096, one of them exactly 4096; the others hold fewer than 512 positions; which requests are which is drawn.
All inputs are finite; a program needn't handle non-finite values.
Results may differ from the reference program's by a relative error of at most 0.015.
Values may be sent and summed in bfloat16 or wider, within the bound.
A program may use at most 256 MiB of HBM per device.

```python
import math
import jax
import jax.numpy as jnp
from jax import lax

MODEL_WIDTH = 5120
QUERY_HEADS = 32
KEY_VALUE_HEADS = 8
HEAD_WIDTH = 128
FF = 13824
FRESH_TOKENS = 256
CACHE_DEV = 512
CACHE_SLOTS = 4096
REQUEST_COUNT = 4


def bias_lookup(key):
    random_noise = 0.5 * jax.random.normal(jax.random.fold_in(key, 7), ((QUERY_HEADS + 2 * KEY_VALUE_HEADS) * HEAD_WIDTH,), jnp.float32)
    return jnp.clip(random_noise, -1.5, 1.5)


def draw_b_qkv(key, part):
    return bias_lookup(key).astype(jnp.bfloat16)


def draw_cached_len(key, part):
    ranking = jax.random.permutation(jax.random.fold_in(key, 3), REQUEST_COUNT)
    longer = CACHE_SLOTS - jax.random.randint(jax.random.fold_in(key, 4), (REQUEST_COUNT,), 0, CACHE_DEV)
    longer = jnp.where(ranking == 0, CACHE_SLOTS, longer)
    shorter = jax.random.randint(jax.random.fold_in(key, 5), (REQUEST_COUNT,), 2, CACHE_DEV)
    return jnp.where(ranking < max(REQUEST_COUNT // 2, 1), longer, shorter).astype(jnp.int32)


def draw_key_cache(key, part):
    array_shape = (REQUEST_COUNT, CACHE_SLOTS, KEY_VALUE_HEADS * HEAD_WIDTH)
    start_vals = jnp.clip(jax.random.normal(jax.random.fold_in(key, 11), array_shape, jnp.float32), -6.0, 6.0)
    return start_vals.astype(jnp.bfloat16)


def levels(rng, dims, cuts, low, largest):
    loudness = 1.0
    for dim, blocks in cuts:
        draws = jax.random.uniform(jax.random.fold_in(jax.random.fold_in(rng, 6), dim), (blocks,), jnp.float32, low / len(cuts), largest / len(cuts))
        loudness = loudness * jnp.repeat(jnp.exp(draws), dims[dim] // blocks).reshape((-1,) + (1,) * (len(dims) - 1 - dim))
    return loudness


def noise(key, extent, scale, limit, shards=(), kind=jnp.bfloat16):
    array = jax.random.normal(key, extent, jnp.float32) * scale
    if len(shards) > 0:
        array = levels(key, extent, shards, -0.22, 0.18) * array
    return jnp.clip(array, min=-limit, max=limit).astype(kind)


def setup_inputs(seed: int = 0) -> dict:
    splits = jax.random.split(jax.random.key(seed), 13)
    return {
        "hidden": noise(splits[0], (REQUEST_COUNT, FRESH_TOKENS, MODEL_WIDTH), 1.0, 6.0, ((0, 4), (1, 8))),
        "cached_len": draw_cached_len(jax.random.fold_in(splits[12], 71), 0),
        "attn_gain": jnp.clip(1.0 + 0.1 * jax.random.normal(splits[2], (MODEL_WIDTH,), jnp.float32), 0.5, 1.5),
        "query_key_value_weight": noise(splits[3], (MODEL_WIDTH, (QUERY_HEADS + 2 * KEY_VALUE_HEADS) * HEAD_WIDTH), MODEL_WIDTH ** -0.5, 0.078125, ((1, 8),)),
        "b_qkv": draw_b_qkv(jax.random.fold_in(splits[12], 71), 0),
        "key_cache": draw_key_cache(jax.random.fold_in(splits[12], 71), 0),
        "value_cache": noise(splits[6], (REQUEST_COUNT, CACHE_SLOTS, KEY_VALUE_HEADS * HEAD_WIDTH), 1.0, 6.0, ((0, 4), (1, 8))),
        "w_out": noise(splits[7], (QUERY_HEADS * HEAD_WIDTH, MODEL_WIDTH), (QUERY_HEADS * HEAD_WIDTH) ** -0.5, 0.09375, ((0, 8),)),
        "ffn_gain": jnp.clip(1.0 + 0.1 * jax.random.normal(splits[8], (MODEL_WIDTH,), jnp.float32), 0.5, 1.5),
        "w_gate": noise(splits[9], (MODEL_WIDTH, FF), MODEL_WIDTH ** -0.5, 0.078125, ((1, 8),)),
        "w_up": noise(splits[10], (MODEL_WIDTH, FF), MODEL_WIDTH ** -0.5, 0.078125, ((1, 8),)),
        "w_down": noise(splits[11], (FF, MODEL_WIDTH), FF ** -0.5, 0.0546875, ((0, 8),)),
    }


rope_base = 1000000.0

def rms_norm(values, gain):
    data = values.astype(jnp.float32)
    spread = lax.optimization_barrier(jnp.mean(data * data, axis=-1, keepdims=True))
    return (data * lax.rsqrt(spread + 1e-06) * gain.astype(jnp.float32)).astype(jnp.bfloat16)

def rope_apply(values, positions):
    half_dim = HEAD_WIDTH // 2
    inverse = rope_base ** (-(jnp.arange(half_dim, dtype=jnp.float32) * 2.0 / HEAD_WIDTH))
    angles = positions.astype(jnp.float32)[:, None] * inverse[None, :]
    cosine = jnp.concatenate([jnp.cos(angles), jnp.cos(angles)], axis=-1)[:, None, :]
    sine = jnp.concatenate([jnp.sin(angles), jnp.sin(angles)], axis=-1)[:, None, :]
    data = values.astype(jnp.float32)
    rotated = jnp.concatenate([-data[..., half_dim:], data[..., :half_dim]], axis=-1)
    return (data * cosine + rotated * sine).astype(jnp.bfloat16)

def reference(hidden, cached_len, attn_gain, query_key_value_weight, b_qkv, key_cache, value_cache, w_out, ffn_gain, w_gate, w_up, w_down):
    head_group = QUERY_HEADS // KEY_VALUE_HEADS
    scale = 1.0 / math.sqrt(HEAD_WIDTH)
    outputs = []
    key_pieces = []
    value_pieces = []
    for request_index in range(REQUEST_COUNT):
        inputs = hidden[request_index]
        normed = rms_norm(inputs, attn_gain)
        query_key_value = (jnp.dot(normed, query_key_value_weight, preferred_element_type=jnp.float32) + b_qkv.astype(jnp.float32)).astype(jnp.bfloat16)
        query_rows = query_key_value[:, :QUERY_HEADS * HEAD_WIDTH].reshape(FRESH_TOKENS, QUERY_HEADS, HEAD_WIDTH)
        fresh_keys = query_key_value[:, QUERY_HEADS * HEAD_WIDTH:(QUERY_HEADS + KEY_VALUE_HEADS) * HEAD_WIDTH].reshape(FRESH_TOKENS, KEY_VALUE_HEADS, HEAD_WIDTH)
        fresh_values = query_key_value[:, (QUERY_HEADS + KEY_VALUE_HEADS) * HEAD_WIDTH:].reshape(FRESH_TOKENS, KEY_VALUE_HEADS, HEAD_WIDTH)
        positions = cached_len[request_index] + jnp.arange(FRESH_TOKENS, dtype=jnp.int32)
        query_rows = rope_apply(query_rows, positions)
        fresh_keys = rope_apply(fresh_keys, positions)
        key_pieces.append(fresh_keys.reshape(FRESH_TOKENS, KEY_VALUE_HEADS * HEAD_WIDTH))
        value_pieces.append(fresh_values.reshape(FRESH_TOKENS, KEY_VALUE_HEADS * HEAD_WIDTH))
        cache_ok = jnp.arange(CACHE_SLOTS, dtype=jnp.int32) < cached_len[request_index]
        token_ids = jnp.arange(FRESH_TOKENS, dtype=jnp.int32)
        new_ok = token_ids[None, :] <= token_ids[:, None]
        allowed = jnp.concatenate([jnp.broadcast_to(cache_ok[None, :], (FRESH_TOKENS, CACHE_SLOTS)), new_ok], axis=1)
        query_head_rows = query_rows.reshape(FRESH_TOKENS, KEY_VALUE_HEADS, head_group, HEAD_WIDTH).transpose(1, 0, 2, 3)
        stored_keys = key_cache[request_index].reshape(CACHE_SLOTS, KEY_VALUE_HEADS, HEAD_WIDTH).transpose(1, 0, 2)
        stored_values = value_cache[request_index].reshape(CACHE_SLOTS, KEY_VALUE_HEADS, HEAD_WIDTH).transpose(1, 0, 2)

        def one_head(items):
            query_h, ckeys, cvalues, nkeys, nvalues = items
            joined_keys = jnp.concatenate([ckeys, nkeys], axis=0).astype(jnp.float32)
            joined_values = jnp.concatenate([cvalues, nvalues], axis=0).astype(jnp.float32)
            scores = jnp.einsum('tjd,sd->jts', query_h.astype(jnp.float32), joined_keys) * scale
            scores = jnp.where(allowed[None], scores, -1e+30)
            top = lax.optimization_barrier(jnp.max(scores, axis=-1, keepdims=True))
            expo = jnp.where(allowed[None], jnp.exp(scores - top), 0.0)
            total = lax.optimization_barrier(jnp.sum(expo, axis=-1))
            weights = expo.astype(jnp.bfloat16).astype(jnp.float32)
            mixed = jnp.einsum('jts,sd->tjd', weights, joined_values)
            return (mixed / jnp.transpose(total)[:, :, None]).astype(jnp.bfloat16)
        attended = lax.map(one_head, (query_head_rows, stored_keys, stored_values, fresh_keys.transpose(1, 0, 2), fresh_values.transpose(1, 0, 2)))
        attn = attended.transpose(1, 0, 2, 3).reshape(FRESH_TOKENS, QUERY_HEADS * HEAD_WIDTH)
        projected = jnp.dot(attn, w_out, preferred_element_type=jnp.float32)
        middle = (inputs.astype(jnp.float32) + projected).astype(jnp.bfloat16)
        normed_two = rms_norm(middle, ffn_gain)
        gate = jnp.dot(normed_two, w_gate, preferred_element_type=jnp.float32)
        upward = jnp.dot(normed_two, w_up, preferred_element_type=jnp.float32)
        active = (jax.nn.silu(gate) * upward).astype(jnp.bfloat16)
        result = middle.astype(jnp.float32) + jnp.dot(active, w_down, preferred_element_type=jnp.float32)
        outputs.append(result.astype(jnp.bfloat16))
    return (jnp.stack(outputs), jnp.stack(key_pieces), jnp.stack(value_pieces))
```

```python
import functools
import math

import jax
import jax.numpy as jnp
from jax import lax
from jax.experimental import pallas as pl
from jax.experimental.pallas import tpu as pltpu
from jax.sharding import PartitionSpec as P

QUERY_HEADS = 32
KEY_VALUE_HEADS = 8
HEAD_WIDTH = 128
GROUP = QUERY_HEADS // KEY_VALUE_HEADS
SCALE = 1.0 / math.sqrt(HEAD_WIDTH)
TAIL = 16
FEED_TILE = 432
FEED_COLUMNS = 1024
TAIL_CHUNK = 512

rope_base = 1000000.0
MESH = pl.DeviceIdType.MESH


def rms_norm(values, gain):
    data = values.astype(jnp.float32)
    spread = jnp.mean(data * data, axis=-1, keepdims=True)
    return (data * lax.rsqrt(spread + 1e-06) * gain).astype(jnp.bfloat16)


def rope_tables(positions):
    half_dim = HEAD_WIDTH // 2
    inverse = rope_base ** (-(jnp.arange(half_dim, dtype=jnp.float32) * 2.0 / HEAD_WIDTH))
    angles = positions.astype(jnp.float32)[:, None] * inverse[None, :]
    cosine = jnp.cos(angles)
    sine = jnp.sin(angles)
    return (
        jnp.concatenate([cosine, cosine], axis=-1),
        jnp.concatenate([-sine, sine], axis=-1),
    )


def chain_barrier(chips, me, chip, partner):
    barrier = pltpu.get_barrier_semaphore()
    pl.semaphore_signal(barrier, inc=1, device_id={"head": partner}, device_id_type=MESH)

    @pl.when(chip > 0)
    def _():
        pl.semaphore_signal(barrier, inc=1, device_id={"head": me - 2}, device_id_type=MESH)

    @pl.when(chip < chips - 1)
    def _():
        pl.semaphore_signal(barrier, inc=1, device_id={"head": me + 2}, device_id_type=MESH)

    below = (chip + chips - 1) // chips
    above = (2 * chips - 2 - chip) // chips
    pl.semaphore_wait(barrier, 1 + below + above)


def gather_kernel(
    chips, pieces, x_ref, out_ref, own_sem, up_send, down_send, chip_recv, pair_send, pair_recv
):
    me = lax.axis_index("head")
    chip = me // 2
    core = me % 2
    partner = chip * 2 + (1 - core)
    chain_barrier(chips, me, chip, partner)

    def to_up(src, owner, c):
        return pltpu.make_async_remote_copy(
            src_ref=src,
            dst_ref=out_ref.at[owner * 2 + core, c],
            send_sem=up_send.at[owner, c],
            recv_sem=chip_recv.at[owner, c],
            device_id={"head": me + 2},
            device_id_type=MESH,
        )

    def to_down(src, owner, c):
        return pltpu.make_async_remote_copy(
            src_ref=src,
            dst_ref=out_ref.at[owner * 2 + core, c],
            send_sem=down_send.at[owner, c],
            recv_sem=chip_recv.at[owner, c],
            device_id={"head": me - 2},
            device_id_type=MESH,
        )

    def to_partner(src, owner, c):
        return pltpu.make_async_remote_copy(
            src_ref=src,
            dst_ref=out_ref.at[owner * 2 + core, c],
            send_sem=pair_send.at[owner, c],
            recv_sem=pair_recv.at[owner, c],
            device_id={"head": partner},
            device_id_type=MESH,
        )

    def begin(c, carry):
        @pl.when(chip < chips - 1)
        def _():
            to_up(x_ref.at[c], chip, c).start()

        @pl.when(chip > 0)
        def _():
            to_down(x_ref.at[c], chip, c).start()

        to_partner(x_ref.at[c], chip, c).start()
        return carry

    lax.fori_loop(0, pieces, begin, 0)
    own = pltpu.make_async_copy(x_ref, out_ref.at[me], own_sem)
    own.start()

    def step(t, carry):
        s = 1 + t // pieces
        c = t % pieces

        @pl.when(chip - s >= 0)
        def _():
            owner = chip - s
            held = out_ref.at[owner * 2 + core, c]
            to_up(held, owner, c).wait_recv()

            @pl.when(chip < chips - 1)
            def _():
                to_up(held, owner, c).start()

            to_partner(held, owner, c).start()

        @pl.when(chip + s <= chips - 1)
        def _():
            owner = chip + s
            held = out_ref.at[owner * 2 + core, c]
            to_down(held, owner, c).wait_recv()

            @pl.when(chip > 0)
            def _():
                to_down(held, owner, c).start()

            to_partner(held, owner, c).start()

        return carry

    lax.fori_loop(0, (chips - 1) * pieces, step, 0)
    own.wait()

    def finish(t, carry):
        owner = t // pieces
        c = t % pieces
        to_partner(x_ref.at[c], owner, c).wait()

        @pl.when((chip < chips - 1) & (owner <= chip))
        def _():
            to_up(x_ref.at[c], owner, c).wait_send()

        @pl.when((chip > 0) & (owner >= chip))
        def _():
            to_down(x_ref.at[c], owner, c).wait_send()

        return carry

    lax.fori_loop(0, chips * pieces, finish, 0)


def gather(x, size, pieces, collective_id):
    chips = size // 2
    rows, width = x.shape
    x = x.reshape(pieces, rows // pieces, width)
    return pl.pallas_call(
        functools.partial(gather_kernel, chips, pieces),
        out_shape=jax.ShapeDtypeStruct((size,) + x.shape, x.dtype),
        in_specs=[pl.BlockSpec(memory_space=pltpu.VMEM)],
        out_specs=pl.BlockSpec(memory_space=pltpu.VMEM),
        scratch_shapes=[pltpu.SemaphoreType.DMA(())]
        + [pltpu.SemaphoreType.DMA((chips, pieces))] * 5,
        compiler_params=pltpu.CompilerParams(
            collective_id=collective_id, has_side_effects=True, vmem_limit_bytes=16 << 20
        ),
        name="gather%d" % collective_id,
    )(x).reshape(size, rows, width)


def add_blocks(a, b):
    return a.astype(jnp.float32) + b.astype(jnp.float32)


def pack_sums(sums, total, top):
    def narrow(v):
        return v.astype(jnp.bfloat16).astype(jnp.float32)

    total_high = narrow(total)
    top_high = narrow(top)
    top_middle = narrow(top - top_high)
    rows = [total_high, total - total_high, top_high, top_middle, top - top_high - top_middle]
    index = lax.broadcasted_iota(jnp.int32, (TAIL, sums.shape[1]), 0)
    tail = jnp.zeros((TAIL, sums.shape[1]), jnp.float32)
    for place, row in enumerate(rows):
        tail = jnp.where(index == place, row, tail)
    return jnp.concatenate([sums, tail], axis=0)


def join_sums(a, b):
    def unpack(block):
        block = block.astype(jnp.float32)
        tail = block[HEAD_WIDTH:]
        return block[:HEAD_WIDTH], tail[0:1] + tail[1:2], (tail[2:3] + tail[3:4]) + tail[4:5]

    sums_a, total_a, top_a = unpack(a)
    sums_b, total_b, top_b = unpack(b)
    top = jnp.maximum(top_a, top_b)
    scale_a = jnp.exp((top_a - top) * SCALE)
    scale_b = jnp.exp((top_b - top) * SCALE)
    return pack_sums(
        sums_a * scale_a + sums_b * scale_b, total_a * scale_a + total_b * scale_b, top
    )


def scatter_kernel(
    join,
    chips,
    pieces,
    x_ref,
    out_ref,
    pair,
    up,
    down,
    pair_send,
    pair_recv,
    up_send,
    up_recv,
    down_send,
    down_recv,
):
    me = lax.axis_index("head")
    chip = me // 2
    core = me % 2
    partner = chip * 2 + (1 - core)
    half = chip // (chips // 2)
    chain_barrier(chips, me, chip, partner)

    def to_partner(j, c):
        return pltpu.make_async_remote_copy(
            src_ref=x_ref.at[2 * j + (1 - core), c],
            dst_ref=pair.at[j, c],
            send_sem=pair_send.at[j, c],
            recv_sem=pair_recv.at[j, c],
            device_id={"head": partner},
            device_id_type=MESH,
        )

    def to_up(src, j, c):
        return pltpu.make_async_remote_copy(
            src_ref=src.at[j, c],
            dst_ref=up.at[j, c],
            send_sem=up_send.at[j, c],
            recv_sem=up_recv.at[j, c],
            device_id={"head": me + 2},
            device_id_type=MESH,
        )

    def to_down(src, j, c):
        return pltpu.make_async_remote_copy(
            src_ref=src.at[j, c],
            dst_ref=down.at[j, c],
            send_sem=down_send.at[j, c],
            recv_sem=down_recv.at[j, c],
            device_id={"head": me - 2},
            device_id_type=MESH,
        )

    def order(k):
        return (1 - half) * (chips - 1 - k) + half * k

    def first(t, carry):
        to_partner(order(t // pieces), t % pieces).start()
        return carry

    lax.fori_loop(0, chips * pieces, first, 0)

    def second(t, carry):
        j = order(t // pieces)
        c = t % pieces
        to_partner(j, c).wait_recv()
        pair[j, c] = join(pair[j, c], x_ref[2 * j + core, c]).astype(pair.dtype)

        @pl.when((chip == 0) & (j > 0))
        def _():
            to_up(pair, j, c).start()

        @pl.when((chip == chips - 1) & (j < chips - 1))
        def _():
            to_down(pair, j, c).start()

        return carry

    lax.fori_loop(0, chips * pieces, second, 0)

    def move_up(j, c):
        @pl.when((chip > 0) & (j > chip))
        def _():
            to_up(up, j, c).wait_recv()
            up[j, c] = join(up[j, c], pair[j, c]).astype(up.dtype)
            to_up(up, j, c).start()

    def move_down(j, c):
        @pl.when((chip < chips - 1) & (j < chip))
        def _():
            to_down(down, j, c).wait_recv()
            down[j, c] = join(down[j, c], pair[j, c]).astype(down.dtype)
            to_down(down, j, c).start()

    def third(t, carry):
        s = t // pieces
        c = t % pieces

        @pl.when(half == 0)
        def _():
            move_up(chips - 1 - s, c)

        move_down(s, c)

        @pl.when(half == 1)
        def _():
            move_up(chips - 1 - s, c)

        return carry

    lax.fori_loop(0, (chips - 1) * pieces, third, 0)

    def total(c, carry):
        out_ref[c] = pair[chip, c].astype(jnp.float32)

        @pl.when(chip > 0)
        def _():
            to_up(up, chip, c).wait_recv()
            out_ref[c] = join(out_ref[c], up[chip, c])

        @pl.when(chip < chips - 1)
        def _():
            to_down(down, chip, c).wait_recv()
            out_ref[c] = join(out_ref[c], down[chip, c])

        return carry

    lax.fori_loop(0, pieces, total, 0)

    def finish(t, carry):
        j = t // pieces
        c = t % pieces
        to_partner(j, c).wait_send()

        @pl.when(j > chip)
        def _():
            to_up(pair, j, c).wait_send()

        @pl.when(j < chip)
        def _():
            to_down(pair, j, c).wait_send()

        return carry

    lax.fori_loop(0, chips * pieces, finish, 0)


def scatter(x, size, join, collective_id):
    chips = size // 2
    shape = x.shape[1:]
    pieces = shape[0]
    return pl.pallas_call(
        functools.partial(scatter_kernel, join, chips, pieces),
        out_shape=jax.ShapeDtypeStruct(shape, jnp.float32),
        in_specs=[pl.BlockSpec(memory_space=pltpu.VMEM)],
        out_specs=pl.BlockSpec(memory_space=pltpu.VMEM),
        scratch_shapes=[pltpu.VMEM((chips,) + shape, x.dtype)] * 3
        + [pltpu.SemaphoreType.DMA((chips, pieces))] * 6,
        compiler_params=pltpu.CompilerParams(
            collective_id=collective_id, has_side_effects=True, vmem_limit_bytes=24 << 20
        ),
        name="scatter%d" % collective_id,
    )(x)


def attend_kernel(info_ref, q_ref, kc_ref, vc_ref, kn_ref, vn_ref, cos_ref, sin_ref, sum_ref):
    tokens = q_ref.shape[0]
    length = kc_ref.shape[0]
    fresh = kn_ref.shape[0]
    width = GROUP * tokens
    cosine = cos_ref[...]
    sine = sin_ref[...]
    parts = []
    for j in range(GROUP):
        data = q_ref[:, j * HEAD_WIDTH : (j + 1) * HEAD_WIDTH].astype(jnp.float32)
        turned = pltpu.roll(data, HEAD_WIDTH // 2, 1)
        parts.append((data * cosine + turned * sine).astype(jnp.bfloat16))
    query = jnp.concatenate(parts, axis=0)
    last = (((1,), (1,)), ((), ()))
    first = (((0,), (0,)), ((), ()))
    old = lax.dot_general(kc_ref[...], query, last, preferred_element_type=jnp.float32)
    new = lax.dot_general(kn_ref[...], query, last, preferred_element_type=jnp.float32)
    old_ids = lax.broadcasted_iota(jnp.int32, (length, 1), 0)
    old = jnp.where(old_ids < info_ref[0], old, -1e30)
    new_ids = lax.broadcasted_iota(jnp.int32, (fresh, width), 0) + info_ref[1]
    token_ids = lax.broadcasted_iota(jnp.int32, (fresh, width), 1) % tokens
    new = jnp.where(new_ids <= token_ids, new, -1e30)
    top = jnp.maximum(jnp.max(old, axis=0, keepdims=True), jnp.max(new, axis=0, keepdims=True))
    top = jnp.maximum(top, -1e29)
    old = jnp.exp((old - top) * SCALE)
    new = jnp.exp((new - top) * SCALE)
    total = jnp.sum(old, axis=0, keepdims=True) + jnp.sum(new, axis=0, keepdims=True)
    sums = lax.dot_general(
        vc_ref[...], old.astype(jnp.bfloat16), first, preferred_element_type=jnp.float32
    ) + lax.dot_general(
        vn_ref[...], new.astype(jnp.bfloat16), first, preferred_element_type=jnp.float32
    )
    packed = pack_sums(sums, total, top).astype(jnp.bfloat16)
    for j in range(GROUP):
        sum_ref[0, j] = packed[:, j * tokens : (j + 1) * tokens]


def attend(info, qkv, key_cache, value_cache, new_keys, new_values, cosine, sine):
    tokens = qkv.shape[0]
    length = key_cache.shape[0]
    fresh = new_keys.shape[0]

    def head_block(rows):
        return pl.BlockSpec((rows, HEAD_WIDTH), lambda g, info: (0, g))

    def whole_block(shape):
        return pl.BlockSpec(shape, lambda g, info: (0, 0))

    return pl.pallas_call(
        attend_kernel,
        grid_spec=pltpu.PrefetchScalarGridSpec(
            num_scalar_prefetch=1,
            grid=(KEY_VALUE_HEADS,),
            in_specs=[
                pl.BlockSpec((tokens, GROUP * HEAD_WIDTH), lambda g, info: (0, g)),
                head_block(length),
                head_block(length),
                head_block(fresh),
                head_block(fresh),
                whole_block((tokens, HEAD_WIDTH)),
                whole_block((tokens, HEAD_WIDTH)),
            ],
            out_specs=pl.BlockSpec(
                (1, GROUP, HEAD_WIDTH + TAIL, tokens), lambda g, info: (g, 0, 0, 0)
            ),
        ),
        out_shape=jax.ShapeDtypeStruct(
            (KEY_VALUE_HEADS, GROUP, HEAD_WIDTH + TAIL, tokens), jnp.bfloat16
        ),
        compiler_params=pltpu.CompilerParams(
            dimension_semantics=("arbitrary",), vmem_limit_bytes=32 << 20
        ),
        name="attend",
    )(info, qkv, key_cache, value_cache, new_keys, new_values, cosine, sine)


def feed_kernel(steps, x_ref, gate_ref, up_ref, down_ref, out_ref, turned, active):
    step = pl.program_id(0)
    tile = gate_ref.shape[0]

    @pl.when(step == 0)
    def _():
        turned[...] = jnp.transpose(x_ref[...])

    @pl.when(step < steps)
    def _():
        x = turned[...]
        gate = jnp.dot(gate_ref[...], x, preferred_element_type=jnp.float32)
        upward = jnp.dot(up_ref[...], x, preferred_element_type=jnp.float32)
        active[pl.ds(pl.multiple_of(step * tile, tile), tile), :] = (
            gate / (1.0 + jnp.exp(-gate)) * upward
        ).astype(jnp.bfloat16)

    @pl.when(step >= steps)
    def _():
        out_ref[...] = lax.dot_general(
            active[...],
            down_ref[...],
            (((0,), (0,)), ((), ())),
            preferred_element_type=jnp.float32,
        ).astype(jnp.bfloat16)


def feed(x, w_gate, w_up, w_down):
    tokens, model = x.shape
    units = w_down.shape[0]
    steps = units // FEED_TILE
    tile = units // steps
    weight = pl.BlockSpec((tile, model), lambda i: (jnp.minimum(i, steps - 1), 0))
    return pl.pallas_call(
        functools.partial(feed_kernel, steps),
        grid=(steps + model // FEED_COLUMNS,),
        in_specs=[
            pl.BlockSpec((tokens, model), lambda i: (0, 0)),
            weight,
            weight,
            pl.BlockSpec((units, FEED_COLUMNS), lambda i: (0, jnp.maximum(i - steps, 0))),
        ],
        out_specs=pl.BlockSpec((tokens, FEED_COLUMNS), lambda i: (0, jnp.maximum(i - steps, 0))),
        out_shape=jax.ShapeDtypeStruct((tokens, model), jnp.bfloat16),
        scratch_shapes=[
            pltpu.VMEM((model, tokens), jnp.bfloat16),
            pltpu.VMEM((units, tokens), jnp.bfloat16),
        ],
        compiler_params=pltpu.CompilerParams(
            dimension_semantics=("arbitrary",), vmem_limit_bytes=48 << 20
        ),
        name="feed",
    )(x, jnp.transpose(w_gate), jnp.transpose(w_up), w_down)


def tail_kernel(
    n_chunks,
    attn_ref,
    hidden_ref,
    gain_ref,
    w_out_hbm,
    gate_hbm,
    up_hbm,
    w_down_hbm,
    out_ref,
    w_out,
    gate_w,
    up_w,
    w_down,
    product,
    own,
    pair_out,
    pair_in,
    outer_out,
    outer_in,
    cross_out,
    cross_in,
    middle,
    squares,
    x,
    spread,
    gate_sum,
    up_sum,
    active,
    rows_own,
    rows_pair_out,
    rows_pair_in,
    rows_outer_out,
    rows_outer_in,
    rows_cross_out,
    rows_cross_in,
    rows_last_out,
    rows_last_in,
    weight_sem,
    pair_sem,
    outer_sem,
    cross_sem,
    near_sem,
    far_sem,
    far_out_sem,
    near_pair_sem,
    far_pair_sem,
    rows_pair_sem,
    rows_outer_sem,
    rows_cross_sem,
    rows_last_sem,
):
    me = lax.axis_index("head")
    chip = me // 2
    core = me % 2
    side = chip // 2
    partner = chip * 2 + (1 - core)
    inner = (chip == 1) | (chip == 2)
    outer = (chip == 0) | (chip == 3)
    toward = 2 - 4 * side
    near_device = me + toward
    outer_device = me - toward
    tokens = attn_ref.shape[0]
    half = tokens // 2
    part = half // 2
    own_rows = hidden_ref.shape[0]
    chunk = w_out.shape[2]
    slots = gate_w.shape[0]
    near_start = pl.multiple_of(side * half + core * part, part)
    far_start = pl.multiple_of((1 - side) * half + core * part, part)

    def columns(j):
        return pl.ds(pl.multiple_of(j * chunk, chunk), chunk)

    def load_out(j):
        return pltpu.make_async_copy(w_out_hbm.at[:, columns(j)], w_out.at[j], weight_sem.at[0, j])

    def load_gate(j):
        return pltpu.make_async_copy(
            gate_hbm.at[:, columns(j)], gate_w.at[j % slots], weight_sem.at[1, j]
        )

    def load_up(j):
        return pltpu.make_async_copy(
            up_hbm.at[:, columns(j)], up_w.at[j % slots], weight_sem.at[2, j]
        )

    def load_down(j):
        return pltpu.make_async_copy(
            w_down_hbm.at[:, columns(j)], w_down.at[j], weight_sem.at[3, j]
        )

    def remote(src, dst, sems, j, device):
        return pltpu.make_async_remote_copy(
            src_ref=src,
            dst_ref=dst,
            send_sem=sems.at[0, j],
            recv_sem=sems.at[1, j],
            device_id={"head": device},
            device_id_type=MESH,
        )

    def pair_copy(j):
        return remote(pair_out.at[j], pair_in.at[j], pair_sem, j, partner)

    def outer_copy(j):
        return remote(outer_out.at[j], outer_in.at[j], outer_sem, j, near_device)

    def cross_copy(j):
        return remote(cross_out.at[j], cross_in.at[j], cross_sem, j, near_device)

    def x_copy(j, start, sems, device):
        ref = x.at[j, pl.ds(start, part)]
        return remote(ref, ref, sems, j, device)

    def spread_copy(start, sems, device):
        ref = spread.at[pl.ds(start, part)]
        return remote(ref, ref, sems, n_chunks, device)

    def begin_out(j, carry):
        load_out(j).start()
        return carry

    def begin_feed(j, carry):
        load_gate(j).start()
        load_up(j).start()
        return carry

    lax.fori_loop(0, n_chunks, begin_out, 0)
    lax.fori_loop(0, slots, begin_feed, 0)
    chain_barrier(4, me, chip, partner)
    squares[...] = jnp.zeros_like(squares)
    gate_sum[...] = jnp.zeros_like(gate_sum)
    up_sum[...] = jnp.zeros_like(up_sum)

    def stage(t, lag, also=None):
        j = t - lag
        ready = (j >= 0) & (j < n_chunks)
        return ready if also is None else ready & also

    def step(t, carry):
        @pl.when(stage(t, 5, outer))
        def _():
            j = t - 5
            x_copy(j, far_start, far_out_sem, near_device).wait_recv()
            x_copy(j, far_start, far_pair_sem, partner).start()

            @pl.when(j == n_chunks - 1)
            def _():
                spread_copy(far_start, far_out_sem, near_device).wait_recv()
                spread_copy(far_start, far_pair_sem, partner).start()

        @pl.when(stage(t, 4, inner))
        def _():
            j = t - 4
            x_copy(j, far_start, far_sem, near_device).wait_recv()
            x_copy(j, far_start, far_out_sem, outer_device).start()
            x_copy(j, far_start, far_pair_sem, partner).start()

            @pl.when(j == n_chunks - 1)
            def _():
                spread_copy(far_start, far_sem, near_device).wait_recv()
                spread_copy(far_start, far_out_sem, outer_device).start()
                spread_copy(far_start, far_pair_sem, partner).start()

        @pl.when(stage(t, 4, outer))
        def _():
            j = t - 4
            x_copy(j, near_start, near_sem, near_device).wait_recv()
            x_copy(j, near_start, near_pair_sem, partner).start()

            @pl.when(j == n_chunks - 1)
            def _():
                spread_copy(near_start, near_sem, near_device).wait_recv()
                spread_copy(near_start, near_pair_sem, partner).start()

        @pl.when(stage(t, 3, inner))
        def _():
            j = t - 3
            cross_copy(j).wait_recv()
            mid = (own[j, side] + cross_in[j].astype(jnp.float32)).astype(jnp.bfloat16)
            middle[j] = mid
            data = mid.astype(jnp.float32)
            square = data * data
            folded = square[:, :HEAD_WIDTH]
            for k in range(1, chunk // HEAD_WIDTH):
                folded = folded + square[:, k * HEAD_WIDTH : (k + 1) * HEAD_WIDTH]
            squares[...] += folded
            x[j, pl.ds(near_start, part)] = (data * gain_ref[:, columns(j)]).astype(jnp.bfloat16)
            x_copy(j, near_start, near_sem, outer_device).start()
            x_copy(j, near_start, far_sem, near_device).start()
            x_copy(j, near_start, near_pair_sem, partner).start()

            @pl.when(j == n_chunks - 1)
            def _():
                mean = jnp.sum(squares[...], axis=1, keepdims=True) / (n_chunks * chunk)
                spread[pl.ds(near_start, part)] = jnp.broadcast_to(
                    lax.rsqrt(mean + 1e-06), (part, HEAD_WIDTH)
                )
                spread_copy(near_start, near_sem, outer_device).start()
                spread_copy(near_start, far_sem, near_device).start()
                spread_copy(near_start, near_pair_sem, partner).start()

        @pl.when(stage(t, 2, inner))
        def _():
            j = t - 2
            outer_copy(j).wait_recv()
            cross_out[j] = (own[j, 1 - side] + outer_in[j, 1 - side].astype(jnp.float32)).astype(
                jnp.bfloat16
            )
            cross_copy(j).start()
            own[j, side] += outer_in[j, side].astype(jnp.float32)

        @pl.when(stage(t, 1))
        def _():
            j = t - 1
            pair_copy(j).wait_recv()
            total = own[j] + pair_in[j].astype(jnp.float32)

            @pl.when(outer)
            def _():
                outer_out[j] = total.astype(jnp.bfloat16)
                outer_copy(j).start()

            @pl.when(inner)
            def _():
                own[j] = total

        @pl.when(t < n_chunks)
        def _():
            load_out(t).wait()
            product[...] = jnp.dot(attn_ref[...], w_out[t], preferred_element_type=jnp.float32)
            mine = pl.ds(pl.multiple_of(me * own_rows, own_rows), own_rows)
            product[mine] += hidden_ref[:, columns(t)].astype(jnp.float32)
            for f in range(2):
                keep = pl.ds(pl.multiple_of(f * half + core * part, part), part)
                give = pl.ds(pl.multiple_of(f * half + (1 - core) * part, part), part)
                own[t, f] = product[keep]
                pair_out[t, f] = product[give].astype(jnp.bfloat16)
            pair_copy(t).start()
            load_down(t).start()

        @pl.when(stage(t, 6))
        def _():
            j = t - 6
            x_copy(j, near_start, near_pair_sem, partner).wait_recv()
            x_copy(j, far_start, far_pair_sem, partner).wait_recv()
            load_gate(j).wait()
            load_up(j).wait()
            gate_sum[...] += lax.dot_general(
                gate_w[j % slots], x[j], (((1,), (1,)), ((), ())), preferred_element_type=jnp.float32
            )
            up_sum[...] += lax.dot_general(
                up_w[j % slots], x[j], (((1,), (1,)), ((), ())), preferred_element_type=jnp.float32
            )

            @pl.when(j + slots < n_chunks)
            def _():
                load_gate(j + slots).start()
                load_up(j + slots).start()

        return carry

    lax.fori_loop(0, n_chunks + 6, step, 0)
    spread_copy(near_start, near_pair_sem, partner).wait_recv()
    spread_copy(far_start, far_pair_sem, partner).wait_recv()
    scale = jnp.transpose(spread[...])[0:1]
    units = gate_sum.shape[0]
    for start in range(0, units, HEAD_WIDTH):
        stop = min(start + HEAD_WIDTH, units)
        gate = gate_sum[start:stop] * scale
        upward = up_sum[start:stop] * scale
        block = gate / (1.0 + jnp.exp(-gate)) * upward
        active[:, start:stop] = jnp.transpose(block).astype(jnp.bfloat16)

    near_chip = chip + 1 - 2 * side
    outer_chip = 3 * side
    other_outer = 3 - outer_chip
    other_inner = 3 - chip

    def rows_pair_copy(j):
        return remote(rows_pair_out.at[j], rows_pair_in.at[j], rows_pair_sem, j, partner)

    def rows_outer_copy(j):
        return remote(rows_outer_out.at[j], rows_outer_in.at[j], rows_outer_sem, j, near_device)

    def rows_cross_copy(j):
        return remote(rows_cross_out.at[j], rows_cross_in.at[j], rows_cross_sem, j, near_device)

    def rows_last_copy(j, device):
        return remote(rows_last_out.at[j], rows_last_in.at[j], rows_last_sem, j, device)

    def rows_step(t, carry):
        @pl.when(stage(t, 4, outer))
        def _():
            j = t - 4
            rows_last_copy(j, near_device).wait_recv()
            out_ref[:, columns(j)] = (
                rows_own[j, chip] + rows_last_in[j].astype(jnp.float32)
            ).astype(jnp.bfloat16)

        @pl.when(stage(t, 3, inner))
        def _():
            j = t - 3
            rows_cross_copy(j).wait_recv()
            rows_last_out[j] = (
                rows_own[j, outer_chip] + rows_cross_in[j, 1].astype(jnp.float32)
            ).astype(jnp.bfloat16)
            rows_last_copy(j, outer_device).start()
            out_ref[:, columns(j)] = (
                rows_own[j, chip] + rows_cross_in[j, 0].astype(jnp.float32)
            ).astype(jnp.bfloat16)

        @pl.when(stage(t, 2, inner))
        def _():
            j = t - 2
            rows_outer_copy(j).wait_recv()
            rows_cross_out[j, 0] = (
                rows_own[j, other_inner] + rows_outer_in[j, 1].astype(jnp.float32)
            ).astype(jnp.bfloat16)
            rows_cross_out[j, 1] = (
                rows_own[j, other_outer] + rows_outer_in[j, 2].astype(jnp.float32)
            ).astype(jnp.bfloat16)
            rows_cross_copy(j).start()
            rows_own[j, chip] += rows_outer_in[j, 0].astype(jnp.float32)

        @pl.when(stage(t, 1))
        def _():
            j = t - 1
            rows_pair_copy(j).wait_recv()
            for k in range(4):
                rows_own[j, k] += rows_pair_in[j, k].astype(jnp.float32)

            @pl.when(outer)
            def _():
                for k in range(3):
                    target = (1 - side) * (1 + k) + side * (2 - k)
                    rows_outer_out[j, k] = rows_own[j, target].astype(jnp.bfloat16)
                rows_outer_copy(j).start()

        @pl.when(t < n_chunks)
        def _():
            load_down(t).wait()
            product[...] = jnp.dot(active[...], w_down[t], preferred_element_type=jnp.float32)

            @pl.when(inner)
            def _():
                product[pl.ds(near_start, part)] += middle[t].astype(jnp.float32)

            for k in range(4):
                keep = pl.ds(pl.multiple_of((2 * k + core) * own_rows, own_rows), own_rows)
                give = pl.ds(pl.multiple_of((2 * k + 1 - core) * own_rows, own_rows), own_rows)
                rows_own[t, k] = product[keep]
                rows_pair_out[t, k] = product[give].astype(jnp.bfloat16)
            rows_pair_copy(t).start()

        return carry

    lax.fori_loop(0, n_chunks + 4, rows_step, 0)

    def finish(j, carry):
        pair_copy(j).wait_send()
        rows_pair_copy(j).wait_send()
        x_copy(j, near_start, near_pair_sem, partner).wait_send()
        x_copy(j, far_start, far_pair_sem, partner).wait_send()

        @pl.when(outer)
        def _():
            outer_copy(j).wait_send()
            rows_outer_copy(j).wait_send()

        @pl.when(inner)
        def _():
            cross_copy(j).wait_send()
            x_copy(j, near_start, near_sem, outer_device).wait_send()
            x_copy(j, near_start, far_sem, near_device).wait_send()
            x_copy(j, far_start, far_out_sem, outer_device).wait_send()
            rows_cross_copy(j).wait_send()
            rows_last_copy(j, outer_device).wait_send()

        return carry

    lax.fori_loop(0, n_chunks, finish, 0)
    spread_copy(near_start, near_pair_sem, partner).wait_send()
    spread_copy(far_start, far_pair_sem, partner).wait_send()

    @pl.when(inner)
    def _():
        spread_copy(near_start, near_sem, outer_device).wait_send()
        spread_copy(near_start, far_sem, near_device).wait_send()
        spread_copy(far_start, far_out_sem, outer_device).wait_send()


def tail(attn, hidden, gain, w_out, w_gate, w_up, w_down, collective_id):
    tokens, inner = attn.shape
    own_rows, model = hidden.shape
    units = w_down.shape[0]
    chunk = TAIL_CHUNK
    n_chunks = model // chunk
    slots = 3
    part = tokens // 4
    bf16, f32 = jnp.bfloat16, jnp.float32
    vmem = pl.BlockSpec(memory_space=pltpu.VMEM)
    hbm = pl.BlockSpec(memory_space=pl.ANY)

    def remote_sem(count):
        return pltpu.SemaphoreType.DMA((2, count))

    return pl.pallas_call(
        functools.partial(tail_kernel, n_chunks),
        out_shape=jax.ShapeDtypeStruct((own_rows, model), bf16),
        in_specs=[vmem, vmem, vmem, hbm, hbm, hbm, hbm],
        out_specs=vmem,
        scratch_shapes=[
            pltpu.VMEM((n_chunks, inner, chunk), bf16),
            pltpu.VMEM((slots, units, chunk), bf16),
            pltpu.VMEM((slots, units, chunk), bf16),
            pltpu.VMEM((n_chunks, units, chunk), bf16),
            pltpu.VMEM((tokens, chunk), f32),
            pltpu.VMEM((n_chunks, 2, part, chunk), f32),
            pltpu.VMEM((n_chunks, 2, part, chunk), bf16),
            pltpu.VMEM((n_chunks, 2, part, chunk), bf16),
            pltpu.VMEM((n_chunks, 2, part, chunk), bf16),
            pltpu.VMEM((n_chunks, 2, part, chunk), bf16),
            pltpu.VMEM((n_chunks, part, chunk), bf16),
            pltpu.VMEM((n_chunks, part, chunk), bf16),
            pltpu.VMEM((n_chunks, part, chunk), bf16),
            pltpu.VMEM((part, HEAD_WIDTH), f32),
            pltpu.VMEM((n_chunks, tokens, chunk), bf16),
            pltpu.VMEM((tokens, HEAD_WIDTH), f32),
            pltpu.VMEM((units, tokens), f32),
            pltpu.VMEM((units, tokens), f32),
            pltpu.VMEM((tokens, units), bf16),
            pltpu.VMEM((n_chunks, 4, own_rows, chunk), f32),
            pltpu.VMEM((n_chunks, 4, own_rows, chunk), bf16),
            pltpu.VMEM((n_chunks, 4, own_rows, chunk), bf16),
            pltpu.VMEM((n_chunks, 3, own_rows, chunk), bf16),
            pltpu.VMEM((n_chunks, 3, own_rows, chunk), bf16),
            pltpu.VMEM((n_chunks, 2, own_rows, chunk), bf16),
            pltpu.VMEM((n_chunks, 2, own_rows, chunk), bf16),
            pltpu.VMEM((n_chunks, own_rows, chunk), bf16),
            pltpu.VMEM((n_chunks, own_rows, chunk), bf16),
            pltpu.SemaphoreType.DMA((4, n_chunks)),
        ]
        + [remote_sem(n_chunks)] * 3
        + [remote_sem(n_chunks + 1)] * 5
        + [remote_sem(n_chunks)] * 4,
        compiler_params=pltpu.CompilerParams(
            collective_id=collective_id, has_side_effects=True, vmem_limit_bytes=62 << 20
        ),
        name="tail%d" % collective_id,
    )(
        attn,
        hidden,
        gain.reshape(1, model),
        w_out,
        jnp.transpose(w_gate),
        jnp.transpose(w_up),
        w_down,
    )


def on_device(
    hidden,
    cached_len,
    attn_gain,
    query_key_value_weight,
    b_qkv,
    key_cache,
    value_cache,
    w_out,
    ffn_gain,
    w_gate,
    w_up,
    w_down,
):
    size = lax.axis_size("head")
    index_here = lax.axis_index("head")
    own_rows = hidden[0]
    fresh, model = own_rows.shape
    tokens = fresh * size
    heads_here = QUERY_HEADS // size
    row_start = index_here * fresh
    cache_length = key_cache.shape[1]
    key_start = QUERY_HEADS * HEAD_WIDTH
    coarse = max(fresh // 16, 1)

    cosine, sine = rope_tables(cached_len[0] + jnp.arange(tokens, dtype=jnp.int32))
    own_cosine = lax.dynamic_slice_in_dim(cosine, row_start, fresh, 0)[:, None, :]
    own_sine = lax.dynamic_slice_in_dim(sine, row_start, fresh, 0)[:, None, :]

    normed = gather(rms_norm(own_rows, attn_gain), size, coarse, 0).reshape(tokens, model)
    qkv_part = (
        jnp.dot(normed, query_key_value_weight, preferred_element_type=jnp.float32)
        + b_qkv.astype(jnp.float32)
    ).astype(jnp.bfloat16)
    qkv = jnp.transpose(gather(qkv_part, size, 4, 1), (1, 0, 2)).reshape(tokens, -1)
    own = lax.dynamic_slice(
        qkv, (row_start, key_start), (fresh, 2 * KEY_VALUE_HEADS * HEAD_WIDTH)
    )
    key_data = own[:, : KEY_VALUE_HEADS * HEAD_WIDTH].astype(jnp.float32)
    key_data = key_data.reshape(fresh, KEY_VALUE_HEADS, HEAD_WIDTH)
    turned = jnp.roll(key_data, HEAD_WIDTH // 2, axis=-1)
    new_keys = (key_data * own_cosine + turned * own_sine).astype(jnp.bfloat16)
    new_keys = new_keys.reshape(fresh, KEY_VALUE_HEADS * HEAD_WIDTH)
    new_values = own[:, KEY_VALUE_HEADS * HEAD_WIDTH :]

    info = jnp.stack([cached_len[0] - index_here * cache_length, row_start]).astype(jnp.int32)
    sums = attend(info, qkv, key_cache[0], value_cache[0], new_keys, new_values, cosine, sine)
    sums = sums.reshape(size, heads_here, HEAD_WIDTH + TAIL, tokens)
    mixed = scatter(sums, size, join_sums, 3)
    total = mixed[:, HEAD_WIDTH : HEAD_WIDTH + 1] + mixed[:, HEAD_WIDTH + 1 : HEAD_WIDTH + 2]
    attn = (mixed[:, :HEAD_WIDTH] / total).astype(jnp.bfloat16)
    attn = jnp.transpose(attn, (2, 0, 1)).reshape(tokens, heads_here * HEAD_WIDTH)
    if size == 8 and fresh == 32:
        result = tail(attn, own_rows, ffn_gain, w_out, w_gate, w_up, w_down, 7)
    else:
        projected = jnp.dot(attn, w_out, preferred_element_type=jnp.float32).astype(jnp.bfloat16)
        blocks = (size, coarse, fresh // coarse, model)
        projected = scatter(projected.reshape(blocks), size, add_blocks, 4).reshape(fresh, model)
        middle = (own_rows.astype(jnp.float32) + projected).astype(jnp.bfloat16)
        normed_two = gather(rms_norm(middle, ffn_gain), size, coarse, 5).reshape(tokens, model)
        ffn_part = feed(normed_two, w_gate, w_up, w_down)
        ffn_sum = scatter(ffn_part.reshape(blocks), size, add_blocks, 6).reshape(fresh, model)
        result = (middle.astype(jnp.float32) + ffn_sum).astype(jnp.bfloat16)
    return (result[None], new_keys[None], new_values[None])


def solution(mesh):
    in_specs = (
        P("req", "head", None),
        P("req"),
        P(),
        P(None, "head"),
        P("head"),
        P("req", "head", None),
        P("req", "head", None),
        P("head", None),
        P(),
        P(None, "head"),
        P(None, "head"),
        P("head", None),
    )
    out_specs = (P("req", "head", None), P("req", "head", None), P("req", "head", None))
    return jax.shard_map(
        on_device, mesh=mesh, in_specs=in_specs, out_specs=out_specs, check_vma=False
    )
```

```python
import functools
import math

import jax
import jax.numpy as jnp
from jax import lax
from jax.experimental import pallas as pl
from jax.experimental.pallas import tpu as pltpu
from jax.sharding import PartitionSpec as P

QUERY_HEADS = 32
KEY_VALUE_HEADS = 8
HEAD_WIDTH = 128
GROUP = QUERY_HEADS // KEY_VALUE_HEADS
SCALE = 1.0 / math.sqrt(HEAD_WIDTH)
TAIL = 16
FEED_TILE = 432
FEED_COLUMNS = 1024
TAIL_CHUNK = 512
FEED_GROUP = 1
HEAD_CHUNK = 1024
ATTEND_LAG = 4
REDUCE_LAG = 2
PAIR_LAG = 1
HOP_LAG = 2

rope_base = 1000000.0
MESH = pl.DeviceIdType.MESH


def rms_norm(values, gain):
    data = values.astype(jnp.float32)
    spread = jnp.mean(data * data, axis=-1, keepdims=True)
    return (data * lax.rsqrt(spread + 1e-06) * gain).astype(jnp.bfloat16)


def rope_tables(positions):
    half_dim = HEAD_WIDTH // 2
    inverse = rope_base ** (-(jnp.arange(half_dim, dtype=jnp.float32) * 2.0 / HEAD_WIDTH))
    angles = positions.astype(jnp.float32)[:, None] * inverse[None, :]
    cosine = jnp.cos(angles)
    sine = jnp.sin(angles)
    return (
        jnp.concatenate([cosine, cosine], axis=-1),
        jnp.concatenate([-sine, sine], axis=-1),
    )


def chain_barrier(chips, me, chip, partner):
    barrier = pltpu.get_barrier_semaphore()
    pl.semaphore_signal(barrier, inc=1, device_id={"head": partner}, device_id_type=MESH)

    @pl.when(chip > 0)
    def _():
        pl.semaphore_signal(barrier, inc=1, device_id={"head": me - 2}, device_id_type=MESH)

    @pl.when(chip < chips - 1)
    def _():
        pl.semaphore_signal(barrier, inc=1, device_id={"head": me + 2}, device_id_type=MESH)

    below = (chip + chips - 1) // chips
    above = (2 * chips - 2 - chip) // chips
    pl.semaphore_wait(barrier, 1 + below + above)


def gather_kernel(
    chips, pieces, x_ref, out_ref, own_sem, up_send, down_send, chip_recv, pair_send, pair_recv
):
    me = lax.axis_index("head")
    chip = me // 2
    core = me % 2
    partner = chip * 2 + (1 - core)
    chain_barrier(chips, me, chip, partner)

    def to_up(src, owner, c):
        return pltpu.make_async_remote_copy(
            src_ref=src,
            dst_ref=out_ref.at[owner * 2 + core, c],
            send_sem=up_send.at[owner, c],
            recv_sem=chip_recv.at[owner, c],
            device_id={"head": me + 2},
            device_id_type=MESH,
        )

    def to_down(src, owner, c):
        return pltpu.make_async_remote_copy(
            src_ref=src,
            dst_ref=out_ref.at[owner * 2 + core, c],
            send_sem=down_send.at[owner, c],
            recv_sem=chip_recv.at[owner, c],
            device_id={"head": me - 2},
            device_id_type=MESH,
        )

    def to_partner(src, owner, c):
        return pltpu.make_async_remote_copy(
            src_ref=src,
            dst_ref=out_ref.at[owner * 2 + core, c],
            send_sem=pair_send.at[owner, c],
            recv_sem=pair_recv.at[owner, c],
            device_id={"head": partner},
            device_id_type=MESH,
        )

    def begin(c, carry):
        @pl.when(chip < chips - 1)
        def _():
            to_up(x_ref.at[c], chip, c).start()

        @pl.when(chip > 0)
        def _():
            to_down(x_ref.at[c], chip, c).start()

        to_partner(x_ref.at[c], chip, c).start()
        return carry

    lax.fori_loop(0, pieces, begin, 0)
    own = pltpu.make_async_copy(x_ref, out_ref.at[me], own_sem)
    own.start()

    def step(t, carry):
        s = 1 + t // pieces
        c = t % pieces

        @pl.when(chip - s >= 0)
        def _():
            owner = chip - s
            held = out_ref.at[owner * 2 + core, c]
            to_up(held, owner, c).wait_recv()

            @pl.when(chip < chips - 1)
            def _():
                to_up(held, owner, c).start()

            to_partner(held, owner, c).start()

        @pl.when(chip + s <= chips - 1)
        def _():
            owner = chip + s
            held = out_ref.at[owner * 2 + core, c]
            to_down(held, owner, c).wait_recv()

            @pl.when(chip > 0)
            def _():
                to_down(held, owner, c).start()

            to_partner(held, owner, c).start()

        return carry

    lax.fori_loop(0, (chips - 1) * pieces, step, 0)
    own.wait()

    def finish(t, carry):
        owner = t // pieces
        c = t % pieces
        to_partner(x_ref.at[c], owner, c).wait()

        @pl.when((chip < chips - 1) & (owner <= chip))
        def _():
            to_up(x_ref.at[c], owner, c).wait_send()

        @pl.when((chip > 0) & (owner >= chip))
        def _():
            to_down(x_ref.at[c], owner, c).wait_send()

        return carry

    lax.fori_loop(0, chips * pieces, finish, 0)


def gather(x, size, pieces, collective_id):
    chips = size // 2
    rows, width = x.shape
    x = x.reshape(pieces, rows // pieces, width)
    return pl.pallas_call(
        functools.partial(gather_kernel, chips, pieces),
        out_shape=jax.ShapeDtypeStruct((size,) + x.shape, x.dtype),
        in_specs=[pl.BlockSpec(memory_space=pltpu.VMEM)],
        out_specs=pl.BlockSpec(memory_space=pltpu.VMEM),
        scratch_shapes=[pltpu.SemaphoreType.DMA(())]
        + [pltpu.SemaphoreType.DMA((chips, pieces))] * 5,
        compiler_params=pltpu.CompilerParams(
            collective_id=collective_id, has_side_effects=True, vmem_limit_bytes=16 << 20
        ),
        name="gather%d" % collective_id,
    )(x).reshape(size, rows, width)


def add_blocks(a, b):
    return a.astype(jnp.float32) + b.astype(jnp.float32)


def pack_sums(sums, total, top):
    def narrow(v):
        return v.astype(jnp.bfloat16).astype(jnp.float32)

    total_high = narrow(total)
    top_high = narrow(top)
    top_middle = narrow(top - top_high)
    rows = [total_high, total - total_high, top_high, top_middle, top - top_high - top_middle]
    index = lax.broadcasted_iota(jnp.int32, (TAIL, sums.shape[1]), 0)
    tail = jnp.zeros((TAIL, sums.shape[1]), jnp.float32)
    for place, row in enumerate(rows):
        tail = jnp.where(index == place, row, tail)
    return jnp.concatenate([sums, tail], axis=0)


def join_sums(a, b):
    def unpack(block):
        block = block.astype(jnp.float32)
        tail = block[HEAD_WIDTH:]
        return block[:HEAD_WIDTH], tail[0:1] + tail[1:2], (tail[2:3] + tail[3:4]) + tail[4:5]

    sums_a, total_a, top_a = unpack(a)
    sums_b, total_b, top_b = unpack(b)
    top = jnp.maximum(top_a, top_b)
    scale_a = jnp.exp((top_a - top) * SCALE)
    scale_b = jnp.exp((top_b - top) * SCALE)
    return pack_sums(
        sums_a * scale_a + sums_b * scale_b, total_a * scale_a + total_b * scale_b, top
    )


def scatter_kernel(
    join,
    chips,
    pieces,
    x_ref,
    out_ref,
    pair,
    up,
    down,
    pair_send,
    pair_recv,
    up_send,
    up_recv,
    down_send,
    down_recv,
):
    me = lax.axis_index("head")
    chip = me // 2
    core = me % 2
    partner = chip * 2 + (1 - core)
    half = chip // (chips // 2)
    chain_barrier(chips, me, chip, partner)

    def to_partner(j, c):
        return pltpu.make_async_remote_copy(
            src_ref=x_ref.at[2 * j + (1 - core), c],
            dst_ref=pair.at[j, c],
            send_sem=pair_send.at[j, c],
            recv_sem=pair_recv.at[j, c],
            device_id={"head": partner},
            device_id_type=MESH,
        )

    def to_up(src, j, c):
        return pltpu.make_async_remote_copy(
            src_ref=src.at[j, c],
            dst_ref=up.at[j, c],
            send_sem=up_send.at[j, c],
            recv_sem=up_recv.at[j, c],
            device_id={"head": me + 2},
            device_id_type=MESH,
        )

    def to_down(src, j, c):
        return pltpu.make_async_remote_copy(
            src_ref=src.at[j, c],
            dst_ref=down.at[j, c],
            send_sem=down_send.at[j, c],
            recv_sem=down_recv.at[j, c],
            device_id={"head": me - 2},
            device_id_type=MESH,
        )

    def order(k):
        return (1 - half) * (chips - 1 - k) + half * k

    def first(t, carry):
        to_partner(order(t // pieces), t % pieces).start()
        return carry

    lax.fori_loop(0, chips * pieces, first, 0)

    def second(t, carry):
        j = order(t // pieces)
        c = t % pieces
        to_partner(j, c).wait_recv()
        pair[j, c] = join(pair[j, c], x_ref[2 * j + core, c]).astype(pair.dtype)

        @pl.when((chip == 0) & (j > 0))
        def _():
            to_up(pair, j, c).start()

        @pl.when((chip == chips - 1) & (j < chips - 1))
        def _():
            to_down(pair, j, c).start()

        return carry

    lax.fori_loop(0, chips * pieces, second, 0)

    def move_up(j, c):
        @pl.when((chip > 0) & (j > chip))
        def _():
            to_up(up, j, c).wait_recv()
            up[j, c] = join(up[j, c], pair[j, c]).astype(up.dtype)
            to_up(up, j, c).start()

    def move_down(j, c):
        @pl.when((chip < chips - 1) & (j < chip))
        def _():
            to_down(down, j, c).wait_recv()
            down[j, c] = join(down[j, c], pair[j, c]).astype(down.dtype)
            to_down(down, j, c).start()

    def third(t, carry):
        s = t // pieces
        c = t % pieces

        @pl.when(half == 0)
        def _():
            move_up(chips - 1 - s, c)

        move_down(s, c)

        @pl.when(half == 1)
        def _():
            move_up(chips - 1 - s, c)

        return carry

    lax.fori_loop(0, (chips - 1) * pieces, third, 0)

    def total(c, carry):
        out_ref[c] = pair[chip, c].astype(jnp.float32)

        @pl.when(chip > 0)
        def _():
            to_up(up, chip, c).wait_recv()
            out_ref[c] = join(out_ref[c], up[chip, c])

        @pl.when(chip < chips - 1)
        def _():
            to_down(down, chip, c).wait_recv()
            out_ref[c] = join(out_ref[c], down[chip, c])

        return carry

    lax.fori_loop(0, pieces, total, 0)

    def finish(t, carry):
        j = t // pieces
        c = t % pieces
        to_partner(j, c).wait_send()

        @pl.when(j > chip)
        def _():
            to_up(pair, j, c).wait_send()

        @pl.when(j < chip)
        def _():
            to_down(pair, j, c).wait_send()

        return carry

    lax.fori_loop(0, chips * pieces, finish, 0)


def scatter(x, size, join, collective_id):
    chips = size // 2
    shape = x.shape[1:]
    pieces = shape[0]
    return pl.pallas_call(
        functools.partial(scatter_kernel, join, chips, pieces),
        out_shape=jax.ShapeDtypeStruct(shape, jnp.float32),
        in_specs=[pl.BlockSpec(memory_space=pltpu.VMEM)],
        out_specs=pl.BlockSpec(memory_space=pltpu.VMEM),
        scratch_shapes=[pltpu.VMEM((chips,) + shape, x.dtype)] * 3
        + [pltpu.SemaphoreType.DMA((chips, pieces))] * 6,
        compiler_params=pltpu.CompilerParams(
            collective_id=collective_id, has_side_effects=True, vmem_limit_bytes=24 << 20
        ),
        name="scatter%d" % collective_id,
    )(x)


def attend_kernel(info_ref, q_ref, kc_ref, vc_ref, kn_ref, vn_ref, cos_ref, sin_ref, sum_ref):
    tokens = q_ref.shape[0]
    length = kc_ref.shape[0]
    fresh = kn_ref.shape[0]
    width = GROUP * tokens
    cosine = cos_ref[...]
    sine = sin_ref[...]
    parts = []
    for j in range(GROUP):
        data = q_ref[:, j * HEAD_WIDTH : (j + 1) * HEAD_WIDTH].astype(jnp.float32)
        turned = pltpu.roll(data, HEAD_WIDTH // 2, 1)
        parts.append((data * cosine + turned * sine).astype(jnp.bfloat16))
    query = jnp.concatenate(parts, axis=0)
    last = (((1,), (1,)), ((), ()))
    first = (((0,), (0,)), ((), ()))
    old = lax.dot_general(kc_ref[...], query, last, preferred_element_type=jnp.float32)
    new = lax.dot_general(kn_ref[...], query, last, preferred_element_type=jnp.float32)
    old_ids = lax.broadcasted_iota(jnp.int32, (length, 1), 0)
    old = jnp.where(old_ids < info_ref[0], old, -1e30)
    new_ids = lax.broadcasted_iota(jnp.int32, (fresh, width), 0) + info_ref[1]
    token_ids = lax.broadcasted_iota(jnp.int32, (fresh, width), 1) % tokens
    new = jnp.where(new_ids <= token_ids, new, -1e30)
    top = jnp.maximum(jnp.max(old, axis=0, keepdims=True), jnp.max(new, axis=0, keepdims=True))
    top = jnp.maximum(top, -1e29)
    old = jnp.exp((old - top) * SCALE)
    new = jnp.exp((new - top) * SCALE)
    total = jnp.sum(old, axis=0, keepdims=True) + jnp.sum(new, axis=0, keepdims=True)
    sums = lax.dot_general(
        vc_ref[...], old.astype(jnp.bfloat16), first, preferred_element_type=jnp.float32
    ) + lax.dot_general(
        vn_ref[...], new.astype(jnp.bfloat16), first, preferred_element_type=jnp.float32
    )
    packed = pack_sums(sums, total, top).astype(jnp.bfloat16)
    for j in range(GROUP):
        sum_ref[0, j] = packed[:, j * tokens : (j + 1) * tokens]


def attend(info, qkv, key_cache, value_cache, new_keys, new_values, cosine, sine):
    tokens = qkv.shape[0]
    length = key_cache.shape[0]
    fresh = new_keys.shape[0]

    def head_block(rows):
        return pl.BlockSpec((rows, HEAD_WIDTH), lambda g, info: (0, g))

    def whole_block(shape):
        return pl.BlockSpec(shape, lambda g, info: (0, 0))

    return pl.pallas_call(
        attend_kernel,
        grid_spec=pltpu.PrefetchScalarGridSpec(
            num_scalar_prefetch=1,
            grid=(KEY_VALUE_HEADS,),
            in_specs=[
                pl.BlockSpec((tokens, GROUP * HEAD_WIDTH), lambda g, info: (0, g)),
                head_block(length),
                head_block(length),
                head_block(fresh),
                head_block(fresh),
                whole_block((tokens, HEAD_WIDTH)),
                whole_block((tokens, HEAD_WIDTH)),
            ],
            out_specs=pl.BlockSpec(
                (1, GROUP, HEAD_WIDTH + TAIL, tokens), lambda g, info: (g, 0, 0, 0)
            ),
        ),
        out_shape=jax.ShapeDtypeStruct(
            (KEY_VALUE_HEADS, GROUP, HEAD_WIDTH + TAIL, tokens), jnp.bfloat16
        ),
        compiler_params=pltpu.CompilerParams(
            dimension_semantics=("arbitrary",), vmem_limit_bytes=32 << 20
        ),
        name="attend",
    )(info, qkv, key_cache, value_cache, new_keys, new_values, cosine, sine)


def feed_kernel(steps, x_ref, gate_ref, up_ref, down_ref, out_ref, turned, active):
    step = pl.program_id(0)
    tile = gate_ref.shape[0]

    @pl.when(step == 0)
    def _():
        turned[...] = jnp.transpose(x_ref[...])

    @pl.when(step < steps)
    def _():
        x = turned[...]
        gate = jnp.dot(gate_ref[...], x, preferred_element_type=jnp.float32)
        upward = jnp.dot(up_ref[...], x, preferred_element_type=jnp.float32)
        active[pl.ds(pl.multiple_of(step * tile, tile), tile), :] = (
            gate / (1.0 + jnp.exp(-gate)) * upward
        ).astype(jnp.bfloat16)

    @pl.when(step >= steps)
    def _():
        out_ref[...] = lax.dot_general(
            active[...],
            down_ref[...],
            (((0,), (0,)), ((), ())),
            preferred_element_type=jnp.float32,
        ).astype(jnp.bfloat16)


def feed(x, w_gate, w_up, w_down):
    tokens, model = x.shape
    units = w_down.shape[0]
    steps = units // FEED_TILE
    tile = units // steps
    weight = pl.BlockSpec((tile, model), lambda i: (jnp.minimum(i, steps - 1), 0))
    return pl.pallas_call(
        functools.partial(feed_kernel, steps),
        grid=(steps + model // FEED_COLUMNS,),
        in_specs=[
            pl.BlockSpec((tokens, model), lambda i: (0, 0)),
            weight,
            weight,
            pl.BlockSpec((units, FEED_COLUMNS), lambda i: (0, jnp.maximum(i - steps, 0))),
        ],
        out_specs=pl.BlockSpec((tokens, FEED_COLUMNS), lambda i: (0, jnp.maximum(i - steps, 0))),
        out_shape=jax.ShapeDtypeStruct((tokens, model), jnp.bfloat16),
        scratch_shapes=[
            pltpu.VMEM((model, tokens), jnp.bfloat16),
            pltpu.VMEM((units, tokens), jnp.bfloat16),
        ],
        compiler_params=pltpu.CompilerParams(
            dimension_semantics=("arbitrary",), vmem_limit_bytes=48 << 20
        ),
        name="feed",
    )(x, jnp.transpose(w_gate), jnp.transpose(w_up), w_down)


def tail_kernel(
    n_chunks,
    attn_ref,
    hidden_ref,
    gain_ref,
    w_out_hbm,
    gate_hbm,
    up_hbm,
    w_down_hbm,
    out_ref,
    w_out,
    gate_w,
    up_w,
    w_down,
    product,
    own,
    pair_out,
    pair_in,
    outer_out,
    outer_in,
    cross_out,
    cross_in,
    middle,
    squares,
    x,
    spread,
    gate_sum,
    up_sum,
    active,
    rows_own,
    rows_pair_out,
    rows_pair_in,
    rows_outer_out,
    rows_outer_in,
    rows_cross_out,
    rows_cross_in,
    rows_last_out,
    rows_last_in,
    weight_sem,
    pair_sem,
    outer_sem,
    cross_sem,
    near_sem,
    far_sem,
    far_out_sem,
    near_pair_sem,
    far_pair_sem,
    rows_pair_sem,
    rows_outer_sem,
    rows_cross_sem,
    rows_last_sem,
):
    me = lax.axis_index("head")
    chip = me // 2
    core = me % 2
    side = chip // 2
    partner = chip * 2 + (1 - core)
    inner = (chip == 1) | (chip == 2)
    outer = (chip == 0) | (chip == 3)
    toward = 2 - 4 * side
    near_device = me + toward
    outer_device = me - toward
    tokens = attn_ref.shape[0]
    half = tokens // 2
    part = half // 2
    own_rows = hidden_ref.shape[0]
    chunk = w_out.shape[2]
    slots = gate_w.shape[0]
    near_start = pl.multiple_of(side * half + core * part, part)
    far_start = pl.multiple_of((1 - side) * half + core * part, part)

    def columns(j):
        return pl.ds(pl.multiple_of(j * chunk, chunk), chunk)

    def group_columns(j):
        return pl.ds(pl.multiple_of((j % FEED_GROUP) * chunk, chunk), chunk)

    def group_all(j):
        return pl.ds(pl.multiple_of(j * FEED_GROUP * chunk, FEED_GROUP * chunk), FEED_GROUP * chunk)

    def load_out(j):
        return pltpu.make_async_copy(w_out_hbm.at[:, columns(j)], w_out.at[j], weight_sem.at[0, j])

    def load_gate(j):
        return pltpu.make_async_copy(
            gate_hbm.at[:, group_all(j)], gate_w.at[j % slots], weight_sem.at[1, j]
        )

    def load_up(j):
        return pltpu.make_async_copy(
            up_hbm.at[:, group_all(j)], up_w.at[j % slots], weight_sem.at[2, j]
        )

    def load_down(j):
        return pltpu.make_async_copy(
            w_down_hbm.at[:, columns(j)], w_down.at[j], weight_sem.at[3, j]
        )

    def remote(src, dst, sems, j, device):
        return pltpu.make_async_remote_copy(
            src_ref=src,
            dst_ref=dst,
            send_sem=sems.at[0, j],
            recv_sem=sems.at[1, j],
            device_id={"head": device},
            device_id_type=MESH,
        )

    def pair_copy(j):
        return remote(pair_out.at[j], pair_in.at[j], pair_sem, j, partner)

    def outer_copy(j):
        return remote(outer_out.at[j], outer_in.at[j], outer_sem, j, near_device)

    def cross_copy(j):
        return remote(cross_out.at[j], cross_in.at[j], cross_sem, j, near_device)

    def x_copy(j, start, sems, device):
        ref = x.at[j // FEED_GROUP, pl.ds(start, part), group_columns(j)]
        return remote(ref, ref, sems, j, device)

    def spread_copy(start, sems, device):
        ref = spread.at[pl.ds(start, part)]
        return remote(ref, ref, sems, n_chunks, device)

    def begin_out(j, carry):
        load_out(j).start()
        return carry

    def begin_feed(j, carry):
        load_gate(j).start()
        load_up(j).start()
        return carry

    lax.fori_loop(0, n_chunks, begin_out, 0)
    lax.fori_loop(0, slots, begin_feed, 0)
    chain_barrier(4, me, chip, partner)
    squares[...] = jnp.zeros_like(squares)
    gate_sum[...] = jnp.zeros_like(gate_sum)
    up_sum[...] = jnp.zeros_like(up_sum)

    def stage(t, lag, also=None):
        j = t - lag
        ready = (j >= 0) & (j < n_chunks)
        return ready if also is None else ready & also

    lag_outer = PAIR_LAG + HOP_LAG
    lag_cross = lag_outer + HOP_LAG
    lag_near = lag_cross + HOP_LAG
    lag_far = lag_near + HOP_LAG
    lag_feed = lag_far + PAIR_LAG

    def step(t, carry):
        @pl.when(stage(t, lag_far, outer))
        def _():
            j = t - lag_far
            x_copy(j, far_start, far_out_sem, near_device).wait_recv()
            x_copy(j, far_start, far_pair_sem, partner).start()

            @pl.when(j == n_chunks - 1)
            def _():
                spread_copy(far_start, far_out_sem, near_device).wait_recv()
                spread_copy(far_start, far_pair_sem, partner).start()

        @pl.when(stage(t, lag_near, inner))
        def _():
            j = t - lag_near
            x_copy(j, far_start, far_sem, near_device).wait_recv()
            x_copy(j, far_start, far_out_sem, outer_device).start()
            x_copy(j, far_start, far_pair_sem, partner).start()

            @pl.when(j == n_chunks - 1)
            def _():
                spread_copy(far_start, far_sem, near_device).wait_recv()
                spread_copy(far_start, far_out_sem, outer_device).start()
                spread_copy(far_start, far_pair_sem, partner).start()

        @pl.when(stage(t, lag_near, outer))
        def _():
            j = t - lag_near
            x_copy(j, near_start, near_sem, near_device).wait_recv()
            x_copy(j, near_start, near_pair_sem, partner).start()

            @pl.when(j == n_chunks - 1)
            def _():
                spread_copy(near_start, near_sem, near_device).wait_recv()
                spread_copy(near_start, near_pair_sem, partner).start()

        @pl.when(stage(t, lag_cross, inner))
        def _():
            j = t - lag_cross
            cross_copy(j).wait_recv()
            mid = (own[j, side] + cross_in[j].astype(jnp.float32)).astype(jnp.bfloat16)
            middle[j] = mid
            data = mid.astype(jnp.float32)
            square = data * data
            folded = square[:, :HEAD_WIDTH]
            for k in range(1, chunk // HEAD_WIDTH):
                folded = folded + square[:, k * HEAD_WIDTH : (k + 1) * HEAD_WIDTH]
            squares[...] += folded
            x[j // FEED_GROUP, pl.ds(near_start, part), group_columns(j)] = (
                data * gain_ref[:, columns(j)]
            ).astype(jnp.bfloat16)
            x_copy(j, near_start, near_sem, outer_device).start()
            x_copy(j, near_start, far_sem, near_device).start()
            x_copy(j, near_start, near_pair_sem, partner).start()

            @pl.when(j == n_chunks - 1)
            def _():
                mean = jnp.sum(squares[...], axis=1, keepdims=True) / (n_chunks * chunk)
                spread[pl.ds(near_start, part)] = jnp.broadcast_to(
                    lax.rsqrt(mean + 1e-06), (part, HEAD_WIDTH)
                )
                spread_copy(near_start, near_sem, outer_device).start()
                spread_copy(near_start, far_sem, near_device).start()
                spread_copy(near_start, near_pair_sem, partner).start()

        @pl.when(stage(t, lag_outer, inner))
        def _():
            j = t - lag_outer
            outer_copy(j).wait_recv()
            cross_out[j] = (own[j, 1 - side] + outer_in[j, 1 - side].astype(jnp.float32)).astype(
                jnp.bfloat16
            )
            cross_copy(j).start()
            own[j, side] += outer_in[j, side].astype(jnp.float32)

        @pl.when(stage(t, PAIR_LAG))
        def _():
            j = t - PAIR_LAG
            pair_copy(j).wait_recv()
            total = own[j] + pair_in[j].astype(jnp.float32)

            @pl.when(outer)
            def _():
                outer_out[j] = total.astype(jnp.bfloat16)
                outer_copy(j).start()

            @pl.when(inner)
            def _():
                own[j] = total

        @pl.when(t < n_chunks)
        def _():
            load_out(t).wait()
            product[...] = jnp.dot(attn_ref[...], w_out[t], preferred_element_type=jnp.float32)
            mine = pl.ds(pl.multiple_of(me * own_rows, own_rows), own_rows)
            product[mine] += hidden_ref[:, columns(t)].astype(jnp.float32)
            for f in range(2):
                keep = pl.ds(pl.multiple_of(f * half + core * part, part), part)
                give = pl.ds(pl.multiple_of(f * half + (1 - core) * part, part), part)
                own[t, f] = product[keep]
                pair_out[t, f] = product[give].astype(jnp.bfloat16)
            pair_copy(t).start()
            load_down(t).start()

        @pl.when(stage(t, lag_feed))
        def _():
            j = t - lag_feed
            x_copy(j, near_start, near_pair_sem, partner).wait_recv()
            x_copy(j, far_start, far_pair_sem, partner).wait_recv()

            @pl.when(j % FEED_GROUP == FEED_GROUP - 1)
            def _():
                g = j // FEED_GROUP
                load_gate(g).wait()
                load_up(g).wait()
                last = (((1,), (1,)), ((), ()))
                gate_sum[...] += lax.dot_general(
                    gate_w[g % slots], x[g], last, preferred_element_type=jnp.float32
                )
                up_sum[...] += lax.dot_general(
                    up_w[g % slots], x[g], last, preferred_element_type=jnp.float32
                )

                @pl.when(g + slots < n_chunks // FEED_GROUP)
                def _():
                    load_gate(g + slots).start()
                    load_up(g + slots).start()

        return carry

    lax.fori_loop(0, n_chunks + lag_feed, step, 0)
    spread_copy(near_start, near_pair_sem, partner).wait_recv()
    spread_copy(far_start, far_pair_sem, partner).wait_recv()
    scale = jnp.transpose(spread[...])[0:1]
    units = gate_sum.shape[0]
    for start in range(0, units, HEAD_WIDTH):
        stop = min(start + HEAD_WIDTH, units)
        gate = gate_sum[start:stop] * scale
        upward = up_sum[start:stop] * scale
        block = gate / (1.0 + jnp.exp(-gate)) * upward
        active[:, start:stop] = jnp.transpose(block).astype(jnp.bfloat16)

    near_chip = chip + 1 - 2 * side
    outer_chip = 3 * side
    other_outer = 3 - outer_chip
    other_inner = 3 - chip

    def rows_pair_copy(j):
        return remote(rows_pair_out.at[j], rows_pair_in.at[j], rows_pair_sem, j, partner)

    def rows_outer_copy(j):
        return remote(rows_outer_out.at[j], rows_outer_in.at[j], rows_outer_sem, j, near_device)

    def rows_cross_copy(j):
        return remote(rows_cross_out.at[j], rows_cross_in.at[j], rows_cross_sem, j, near_device)

    def rows_last_copy(j, device):
        return remote(rows_last_out.at[j], rows_last_in.at[j], rows_last_sem, j, device)

    lag_last = lag_cross + HOP_LAG

    def rows_step(t, carry):
        @pl.when(stage(t, lag_last, outer))
        def _():
            j = t - lag_last
            rows_last_copy(j, near_device).wait_recv()
            out_ref[:, columns(j)] = (
                rows_own[j, chip] + rows_last_in[j].astype(jnp.float32)
            ).astype(jnp.bfloat16)

        @pl.when(stage(t, lag_cross, inner))
        def _():
            j = t - lag_cross
            rows_cross_copy(j).wait_recv()
            rows_last_out[j] = (
                rows_own[j, outer_chip] + rows_cross_in[j, 1].astype(jnp.float32)
            ).astype(jnp.bfloat16)
            rows_last_copy(j, outer_device).start()
            out_ref[:, columns(j)] = (
                rows_own[j, chip] + rows_cross_in[j, 0].astype(jnp.float32)
            ).astype(jnp.bfloat16)

        @pl.when(stage(t, lag_outer, inner))
        def _():
            j = t - lag_outer
            rows_outer_copy(j).wait_recv()
            rows_cross_out[j, 0] = (
                rows_own[j, other_inner] + rows_outer_in[j, 1].astype(jnp.float32)
            ).astype(jnp.bfloat16)
            rows_cross_out[j, 1] = (
                rows_own[j, other_outer] + rows_outer_in[j, 2].astype(jnp.float32)
            ).astype(jnp.bfloat16)
            rows_cross_copy(j).start()
            rows_own[j, chip] += rows_outer_in[j, 0].astype(jnp.float32)

        @pl.when(stage(t, PAIR_LAG))
        def _():
            j = t - PAIR_LAG
            rows_pair_copy(j).wait_recv()
            for k in range(4):
                rows_own[j, k] += rows_pair_in[j, k].astype(jnp.float32)

            @pl.when(outer)
            def _():
                for k in range(3):
                    target = (1 - side) * (1 + k) + side * (2 - k)
                    rows_outer_out[j, k] = rows_own[j, target].astype(jnp.bfloat16)
                rows_outer_copy(j).start()

        @pl.when(t < n_chunks)
        def _():
            load_down(t).wait()
            product[...] = jnp.dot(active[...], w_down[t], preferred_element_type=jnp.float32)

            @pl.when(inner)
            def _():
                product[pl.ds(near_start, part)] += middle[t].astype(jnp.float32)

            for k in range(4):
                keep = pl.ds(pl.multiple_of((2 * k + core) * own_rows, own_rows), own_rows)
                give = pl.ds(pl.multiple_of((2 * k + 1 - core) * own_rows, own_rows), own_rows)
                rows_own[t, k] = product[keep]
                rows_pair_out[t, k] = product[give].astype(jnp.bfloat16)
            rows_pair_copy(t).start()

        return carry

    lax.fori_loop(0, n_chunks + lag_last, rows_step, 0)

    def finish(j, carry):
        pair_copy(j).wait_send()
        rows_pair_copy(j).wait_send()
        x_copy(j, near_start, near_pair_sem, partner).wait_send()
        x_copy(j, far_start, far_pair_sem, partner).wait_send()

        @pl.when(outer)
        def _():
            outer_copy(j).wait_send()
            rows_outer_copy(j).wait_send()

        @pl.when(inner)
        def _():
            cross_copy(j).wait_send()
            x_copy(j, near_start, near_sem, outer_device).wait_send()
            x_copy(j, near_start, far_sem, near_device).wait_send()
            x_copy(j, far_start, far_out_sem, outer_device).wait_send()
            rows_cross_copy(j).wait_send()
            rows_last_copy(j, outer_device).wait_send()

        return carry

    lax.fori_loop(0, n_chunks, finish, 0)
    spread_copy(near_start, near_pair_sem, partner).wait_send()
    spread_copy(far_start, far_pair_sem, partner).wait_send()

    @pl.when(inner)
    def _():
        spread_copy(near_start, near_sem, outer_device).wait_send()
        spread_copy(near_start, far_sem, near_device).wait_send()
        spread_copy(far_start, far_out_sem, outer_device).wait_send()


def tail(attn, hidden, gain, w_out, w_gate, w_up, w_down, collective_id):
    tokens, inner = attn.shape
    own_rows, model = hidden.shape
    units = w_down.shape[0]
    chunk = TAIL_CHUNK
    n_chunks = model // chunk
    slots = 3
    part = tokens // 4
    bf16, f32 = jnp.bfloat16, jnp.float32
    vmem = pl.BlockSpec(memory_space=pltpu.VMEM)
    hbm = pl.BlockSpec(memory_space=pl.ANY)

    def remote_sem(count):
        return pltpu.SemaphoreType.DMA((2, count))

    return pl.pallas_call(
        functools.partial(tail_kernel, n_chunks),
        out_shape=jax.ShapeDtypeStruct((own_rows, model), bf16),
        in_specs=[vmem, vmem, vmem, hbm, hbm, hbm, hbm],
        out_specs=vmem,
        scratch_shapes=[
            pltpu.VMEM((n_chunks, inner, chunk), bf16),
            pltpu.VMEM((slots, units, FEED_GROUP * chunk), bf16),
            pltpu.VMEM((slots, units, FEED_GROUP * chunk), bf16),
            pltpu.VMEM((n_chunks, units, chunk), bf16),
            pltpu.VMEM((tokens, chunk), f32),
            pltpu.VMEM((n_chunks, 2, part, chunk), f32),
            pltpu.VMEM((n_chunks, 2, part, chunk), bf16),
            pltpu.VMEM((n_chunks, 2, part, chunk), bf16),
            pltpu.VMEM((n_chunks, 2, part, chunk), bf16),
            pltpu.VMEM((n_chunks, 2, part, chunk), bf16),
            pltpu.VMEM((n_chunks, part, chunk), bf16),
            pltpu.VMEM((n_chunks, part, chunk), bf16),
            pltpu.VMEM((n_chunks, part, chunk), bf16),
            pltpu.VMEM((part, HEAD_WIDTH), f32),
            pltpu.VMEM((n_chunks // FEED_GROUP, tokens, FEED_GROUP * chunk), bf16),
            pltpu.VMEM((tokens, HEAD_WIDTH), f32),
            pltpu.VMEM((units, tokens), f32),
            pltpu.VMEM((units, tokens), f32),
            pltpu.VMEM((tokens, units), bf16),
            pltpu.VMEM((n_chunks, 4, own_rows, chunk), f32),
            pltpu.VMEM((n_chunks, 4, own_rows, chunk), bf16),
            pltpu.VMEM((n_chunks, 4, own_rows, chunk), bf16),
            pltpu.VMEM((n_chunks, 3, own_rows, chunk), bf16),
            pltpu.VMEM((n_chunks, 3, own_rows, chunk), bf16),
            pltpu.VMEM((n_chunks, 2, own_rows, chunk), bf16),
            pltpu.VMEM((n_chunks, 2, own_rows, chunk), bf16),
            pltpu.VMEM((n_chunks, own_rows, chunk), bf16),
            pltpu.VMEM((n_chunks, own_rows, chunk), bf16),
            pltpu.SemaphoreType.DMA((4, n_chunks)),
        ]
        + [remote_sem(n_chunks)] * 3
        + [remote_sem(n_chunks + 1)] * 5
        + [remote_sem(n_chunks)] * 4,
        compiler_params=pltpu.CompilerParams(
            collective_id=collective_id, has_side_effects=True, vmem_limit_bytes=62 << 20
        ),
        name="tail%d" % collective_id,
    )(
        attn,
        hidden,
        gain.reshape(1, model),
        w_out,
        jnp.transpose(w_gate),
        jnp.transpose(w_up),
        w_down,
    )


def attend_pair(key, value, new_key, new_value, query, limit, row_start, tokens):
    length = key.shape[0]
    fresh = new_key.shape[0]
    width = query.shape[0]
    last = (((1,), (1,)), ((), ()))
    first = (((0,), (0,)), ((), ()))
    old = lax.dot_general(key, query, last, preferred_element_type=jnp.float32)
    new = lax.dot_general(new_key, query, last, preferred_element_type=jnp.float32)
    old_ids = lax.broadcasted_iota(jnp.int32, (length, 1), 0)
    old = jnp.where(old_ids < limit, old, -1e30)
    new_ids = lax.broadcasted_iota(jnp.int32, (fresh, width), 0) + row_start
    token_ids = lax.broadcasted_iota(jnp.int32, (fresh, width), 1) % tokens
    new = jnp.where(new_ids <= token_ids, new, -1e30)
    top = jnp.maximum(jnp.max(old, axis=0, keepdims=True), jnp.max(new, axis=0, keepdims=True))
    top = jnp.maximum(top, -1e29)
    old = jnp.exp((old - top) * SCALE)
    new = jnp.exp((new - top) * SCALE)
    total = jnp.sum(old, axis=0, keepdims=True) + jnp.sum(new, axis=0, keepdims=True)
    sums = lax.dot_general(
        value, old.astype(jnp.bfloat16), first, preferred_element_type=jnp.float32
    ) + lax.dot_general(
        new_value, new.astype(jnp.bfloat16), first, preferred_element_type=jnp.float32
    )
    return pack_sums(sums, total, top).astype(jnp.bfloat16)


def head_kernel(
    n_chunks,
    info_ref,
    hidden_ref,
    gain_ref,
    bias_ref,
    cos_ref,
    sin_ref,
    weight_hbm,
    key_hbm,
    value_hbm,
    attn_ref,
    new_key_ref,
    new_value_ref,
    weight,
    key_cache,
    value_cache,
    x,
    total,
    pairs,
    query,
    fresh_in,
    sums,
    pair_in,
    up_in,
    down_in,
    load_sem,
    x_up_sem,
    x_down_sem,
    x_recv,
    x_pair_sem,
    q_up_sem,
    q_down_sem,
    q_recv,
    q_pair_sem,
    fresh_send,
    fresh_recv,
    sums_pair_sem,
    sums_up_sem,
    sums_down_sem,
):
    me = lax.axis_index("head")
    chip = me // 2
    core = me % 2
    chips = 4
    size = 8
    partner = chip * 2 + (1 - core)
    tokens = x.shape[1]
    own_rows = hidden_ref.shape[0]
    chunk = x.shape[2]
    length = key_cache.shape[0]
    groups = 3
    n_pairs = QUERY_HEADS // 2
    width = 2 * HEAD_WIDTH
    first_kv = n_pairs // groups
    mine = pl.ds(pl.multiple_of(me * own_rows, own_rows), own_rows)

    def columns(j):
        return pl.ds(pl.multiple_of(j * chunk, chunk), chunk)

    def load_weight(j):
        return pltpu.make_async_copy(weight_hbm.at[columns(j)], weight.at[j], load_sem.at[j])

    def load_key():
        return pltpu.make_async_copy(key_hbm, key_cache, load_sem.at[n_chunks])

    def load_value():
        return pltpu.make_async_copy(value_hbm, value_cache, load_sem.at[n_chunks + 1])

    def remote(src, dst, send, recv, device):
        return pltpu.make_async_remote_copy(
            src_ref=src,
            dst_ref=dst,
            send_sem=send,
            recv_sem=recv,
            device_id={"head": device},
            device_id_type=MESH,
        )

    def begin(j, carry):
        load_weight(j).start()
        return carry

    lax.fori_loop(0, n_chunks, begin, 0)
    load_key().start()
    load_value().start()

    barrier = pltpu.get_barrier_semaphore()

    def greet(k, carry):
        pl.semaphore_signal(
            barrier, inc=1, device_id={"head": (me + k) % size}, device_id_type=MESH
        )
        return carry

    lax.fori_loop(1, size, greet, 0)
    data = hidden_ref[...].astype(jnp.float32)
    mean = jnp.mean(data * data, axis=-1, keepdims=True)
    normed = (data * lax.rsqrt(mean + 1e-06) * gain_ref[...]).astype(jnp.bfloat16)
    for j in range(n_chunks):
        x[j, mine] = normed[:, j * chunk : (j + 1) * chunk]
    total[...] = jnp.zeros_like(total)
    pl.semaphore_wait(barrier, size - 1)

    def x_block(j, owner_device):
        return x.at[j, pl.ds(pl.multiple_of(owner_device * own_rows, own_rows), own_rows)]

    def x_up(j, owner):
        block = x_block(j, owner * 2 + core)
        return remote(block, block, x_up_sem.at[owner, j], x_recv.at[owner, j], me + 2)

    def x_down(j, owner):
        block = x_block(j, owner * 2 + core)
        return remote(block, block, x_down_sem.at[owner, j], x_recv.at[owner, j], me - 2)

    def x_pair(j, owner):
        block = x_block(j, owner * 2 + core)
        return remote(block, block, x_pair_sem.at[0, owner, j], x_pair_sem.at[1, owner, j], partner)

    def send_x(j, carry):
        @pl.when(chip < chips - 1)
        def _():
            x_up(j, chip).start()

        @pl.when(chip > 0)
        def _():
            x_down(j, chip).start()

        x_pair(j, chip).start()
        return carry

    def gather_step(t, carry):
        s = 1 + t // n_chunks
        j = t % n_chunks

        @pl.when(chip - s >= 0)
        def _():
            x_up(j, chip - s).wait_recv()

            @pl.when(chip < chips - 1)
            def _():
                x_up(j, chip - s).start()

            x_pair(j, chip - s).start()

        @pl.when(chip + s <= chips - 1)
        def _():
            x_down(j, chip + s).wait_recv()

            @pl.when(chip > 0)
            def _():
                x_down(j, chip + s).start()

            x_pair(j, chip + s).start()

        done = t - (chips - 2) * n_chunks - 1

        @pl.when(done >= 0)
        def _():
            multiply(done)

        return carry

    def multiply(j):
        for owner in range(chips):
            x_pair(j, owner).wait_recv()
        load_weight(j).wait()
        total[...] += jnp.dot(x[j], weight[j], preferred_element_type=jnp.float32)

    lax.fori_loop(0, n_chunks, send_x, 0)
    lax.fori_loop(0, (chips - 1) * n_chunks, gather_step, 0)
    multiply(n_chunks - 1)

    def q_up(p):
        return remote(query.at[p], query.at[p], q_up_sem.at[p], q_recv.at[p], me + 2)

    def q_down(p):
        return remote(query.at[p], query.at[p], q_down_sem.at[p], q_recv.at[p], me - 2)

    def q_pair(p):
        return remote(query.at[p], query.at[p], q_pair_sem.at[0, p], q_pair_sem.at[1, p], partner)

    def fresh_copy(target):
        rows = pl.ds(pl.multiple_of(target * own_rows, own_rows), own_rows)
        source = me - first_kv
        return remote(
            pairs.at[:, rows], fresh_in.at[source], fresh_send.at[target], fresh_recv.at[source], target
        )

    def fresh_wait(source):
        return remote(
            pairs.at[:, pl.ds(0, own_rows)],
            fresh_in.at[source],
            fresh_send.at[0],
            fresh_recv.at[source],
            partner,
        ).wait_recv()

    def send_own(i):
        p = me * groups + i

        @pl.when(p < n_pairs)
        def _():
            @pl.when(chip < chips - 1)
            def _():
                q_up(p).start()

            @pl.when(chip > 0)
            def _():
                q_down(p).start()

            q_pair(p).start()

    def prepare(i, carry):
        piece = pl.ds(pl.multiple_of(i * width, width), width)
        raw = (total[:, piece] + bias_ref[:, piece].astype(jnp.float32)).astype(jnp.bfloat16)
        pairs[i] = raw

        @pl.when(me * groups + i < n_pairs)
        def _():
            for h in range(2):
                values = raw[:, h * HEAD_WIDTH : (h + 1) * HEAD_WIDTH].astype(jnp.float32)
                turned = pltpu.roll(values, HEAD_WIDTH // 2, 1)
                query[me * groups + i, h * tokens : (h + 1) * tokens] = (
                    values * cos_ref[...] + turned * sin_ref[...]
                ).astype(jnp.bfloat16)

        @pl.when((i == 0) | (chip != 1))
        def _():
            send_own(i)

        return carry

    lax.fori_loop(0, groups, prepare, 0)

    @pl.when(me >= first_kv)
    def _():
        for k in range(1, size):
            fresh_copy((me + k) % size).start()
        fresh_in[me - first_kv] = pairs[:, mine]

    load_key().wait()
    load_value().wait()

    def wait_fresh():
        for source in range(size - first_kv):
            @pl.when(me != first_kv + source)
            def _():
                fresh_wait(source)

        for k in range(n_pairs // 4):
            place = n_pairs + k
            block = fresh_in[place // groups - first_kv, place % groups].astype(jnp.float32)
            for h in range(2):
                values = block[:, h * HEAD_WIDTH : (h + 1) * HEAD_WIDTH]
                turned = pltpu.roll(values, HEAD_WIDTH // 2, 1)
                head = 2 * k + h
                new_key_ref[:, head * HEAD_WIDTH : (head + 1) * HEAD_WIDTH] = (
                    values * cos_ref[mine] + turned * sin_ref[mine]
                ).astype(jnp.bfloat16)
            place = n_pairs + n_pairs // 4 + k
            new_value_ref[:, k * width : (k + 1) * width] = fresh_in[
                place // groups - first_kv, place % groups
            ]

    def sums_pair(p):
        return remote(
            sums.at[p], pair_in.at[p], sums_pair_sem.at[0, p], sums_pair_sem.at[1, p], partner
        )

    def sums_up(src, p):
        return remote(src.at[p], up_in.at[p], sums_up_sem.at[0, p], sums_up_sem.at[1, p], me + 2)

    def sums_down(src, p):
        return remote(
            src.at[p], down_in.at[p], sums_down_sem.at[0, p], sums_down_sem.at[1, p], me - 2
        )

    def compute(p):
        head = pl.ds(pl.multiple_of((p // 2) * HEAD_WIDTH, HEAD_WIDTH), HEAD_WIDTH)
        sums[p] = attend_pair(
            key_cache[:, head],
            value_cache[:, head],
            new_key_ref[:, head],
            new_value_ref[:, head],
            query[p],
            info_ref[0],
            me * own_rows,
            tokens,
        )

        @pl.when((p // 2) % 2 != core)
        def _():
            sums_pair(p).start()

    def unit(k):
        after_two = (k + 5) // 8
        after_three = (k + 4) // 8
        after_six = (k + 1) // 8
        owner = 2 - after_two - after_three + after_six
        return owner, k - 3 * after_two - after_three - 2 * after_six

    def receive(k):
        owner, i = unit(k)
        p = (owner * 2 + core) * groups + i

        @pl.when((p < n_pairs) & (owner < chip))
        def _():
            q_up(p).wait_recv()

            @pl.when(chip < chips - 1)
            def _():
                q_up(p).start()

            q_pair(p).start()

        @pl.when((p < n_pairs) & (owner > chip))
        def _():
            q_down(p).wait_recv()

            @pl.when(chip > 0)
            def _():
                q_down(p).start()

            q_pair(p).start()

        @pl.when((chip == 1) & (k == 6))
        def _():
            send_own(1)
            send_own(2)

    def attend_unit(k):
        owner, i = unit(k)

        def each(c, carry):
            p = (owner * 2 + c) * groups + i

            @pl.when(p < n_pairs)
            def _():
                @pl.when(c != core)
                def _():
                    q_pair(p).wait_recv()

                compute(p)

            return carry

        lax.fori_loop(0, 2, each, 0)

    def reduce(k, stage):
        owner, i = unit(k)

        def each(c, carry):
            p = (owner * 2 + c) * groups + i
            target = p // 4
            held = (p < n_pairs) & ((p // 2) % 2 == core)

            if stage == 0:

                @pl.when(held)
                def _():
                    sums_pair(p).wait_recv()
                    sums[p] = join_sums(sums[p], pair_in[p]).astype(jnp.bfloat16)

                    @pl.when((chip == 0) & (target > 0))
                    def _():
                        sums_up(sums, p).start()

                    @pl.when((chip == chips - 1) & (target < chips - 1))
                    def _():
                        sums_down(sums, p).start()
            else:

                @pl.when(held & (chip == stage) & (chip < target))
                def _():
                    sums_up(up_in, p).wait_recv()
                    up_in[p] = join_sums(up_in[p], sums[p]).astype(jnp.bfloat16)
                    sums_up(up_in, p).start()

                @pl.when(held & (chips - 1 - chip == stage) & (chip > target))
                def _():
                    sums_down(down_in, p).wait_recv()
                    down_in[p] = join_sums(down_in[p], sums[p]).astype(jnp.bfloat16)
                    sums_down(down_in, p).start()

            return carry

        lax.fori_loop(0, 2, each, 0)

    units = chips * groups - groups
    inside = (chip == 1) | (chip == 2)

    def attend_step(t, carry):
        done = t - ATTEND_LAG

        @pl.when((t < units) & inside)
        def _():
            receive(t)

        @pl.when((done >= 0) & (done < units) & (chip != 1) & (chip != 2))
        def _():
            receive(done)

        for stage in (2, 1, 0):
            k = done - 1 - stage * REDUCE_LAG

            @pl.when((k >= 0) & (k < units))
            def _():
                reduce(k, stage)

        @pl.when(done == 0)
        def _():
            wait_fresh()

        @pl.when((done >= 0) & (done < units))
        def _():
            attend_unit(done)

        return carry

    lax.fori_loop(0, units + ATTEND_LAG + 1 + 2 * REDUCE_LAG, attend_step, 0)

    for k in range(2):
        p = me * 2 + k

        @pl.when(chip > 0)
        def _():
            sums_up(up_in, p).wait_recv()
            sums[p] = join_sums(sums[p], up_in[p]).astype(jnp.bfloat16)

        @pl.when(chip < chips - 1)
        def _():
            sums_down(down_in, p).wait_recv()

        @pl.when(chip == chips - 1)
        def _():
            down_in[p] = sums[p]

        block = down_in[p]

        @pl.when(chip < chips - 1)
        def _():
            down_in[p] = join_sums(sums[p], block).astype(jnp.bfloat16)

        mixed = down_in[p].astype(jnp.float32)
        bottom = mixed[HEAD_WIDTH : HEAD_WIDTH + 1] + mixed[HEAD_WIDTH + 1 : HEAD_WIDTH + 2]
        result = jnp.transpose(mixed[:HEAD_WIDTH] / bottom).astype(jnp.bfloat16)
        for h in range(2):
            head = 2 * k + h
            attn_ref[:, head * HEAD_WIDTH : (head + 1) * HEAD_WIDTH] = result[
                h * tokens : (h + 1) * tokens
            ]

    def finish_x(n, carry):
        owner = n // n_chunks
        j = n % n_chunks
        x_pair(j, owner).wait_send()

        @pl.when((chip < chips - 1) & (owner <= chip))
        def _():
            x_up(j, owner).wait_send()

        @pl.when((chip > 0) & (owner >= chip))
        def _():
            x_down(j, owner).wait_send()

        return carry

    lax.fori_loop(0, chips * n_chunks, finish_x, 0)

    def finish_pairs(p, carry):
        device = p // groups
        owner = device // 2

        @pl.when(device % 2 == core)
        def _():
            q_pair(p).wait_send()

            @pl.when((chip < chips - 1) & (owner <= chip))
            def _():
                q_up(p).wait_send()

            @pl.when((chip > 0) & (owner >= chip))
            def _():
                q_down(p).wait_send()

        target = p // 4

        @pl.when((p // 2) % 2 != core)
        def _():
            sums_pair(p).wait_send()

        @pl.when((p // 2) % 2 == core)
        def _():
            @pl.when(chip < target)
            def _():
                sums_up(sums, p).wait_send()

            @pl.when(chip > target)
            def _():
                sums_down(sums, p).wait_send()

        return carry

    lax.fori_loop(0, n_pairs, finish_pairs, 0)

    @pl.when(me >= first_kv)
    def _():
        for k in range(1, size):
            fresh_copy((me + k) % size).wait_send()


def head(info, hidden, gain, bias, cosine, sine, weight, key_cache, value_cache, collective_id):
    own_rows, model = hidden.shape
    tokens = cosine.shape[0]
    columns = weight.shape[1]
    length, cached = key_cache.shape
    chunk = HEAD_CHUNK
    n_chunks = model // chunk
    n_pairs = QUERY_HEADS // 2
    groups = 3
    width = 2 * HEAD_WIDTH
    bf16, f32 = jnp.bfloat16, jnp.float32
    vmem = pl.BlockSpec(memory_space=pltpu.VMEM)
    smem = pl.BlockSpec(memory_space=pltpu.SMEM)
    hbm = pl.BlockSpec(memory_space=pl.ANY)
    dma = pltpu.SemaphoreType.DMA
    block = pltpu.VMEM((n_pairs, HEAD_WIDTH + TAIL, 2 * tokens), bf16)
    return pl.pallas_call(
        functools.partial(head_kernel, n_chunks),
        out_shape=[
            jax.ShapeDtypeStruct((tokens, 4 * HEAD_WIDTH), bf16),
            jax.ShapeDtypeStruct((own_rows, cached), bf16),
            jax.ShapeDtypeStruct((own_rows, cached), bf16),
        ],
        in_specs=[smem, vmem, vmem, vmem, vmem, vmem, hbm, hbm, hbm],
        out_specs=[vmem, vmem, vmem],
        scratch_shapes=[
            pltpu.VMEM((n_chunks, chunk, columns), bf16),
            pltpu.VMEM((length, cached), bf16),
            pltpu.VMEM((length, cached), bf16),
            pltpu.VMEM((n_chunks, tokens, chunk), bf16),
            pltpu.VMEM((tokens, columns), f32),
            pltpu.VMEM((groups, tokens, width), bf16),
            pltpu.VMEM((n_pairs, 2 * tokens, HEAD_WIDTH), bf16),
            pltpu.VMEM((3, groups, own_rows, width), bf16),
            block,
            block,
            block,
            block,
            dma((n_chunks + 2,)),
            dma((4, n_chunks)),
            dma((4, n_chunks)),
            dma((4, n_chunks)),
            dma((2, 4, n_chunks)),
            dma((n_pairs,)),
            dma((n_pairs,)),
            dma((n_pairs,)),
            dma((2, n_pairs)),
            dma((8,)),
            dma((3,)),
            dma((2, n_pairs)),
            dma((2, n_pairs)),
            dma((2, n_pairs)),
        ],
        compiler_params=pltpu.CompilerParams(
            collective_id=collective_id, has_side_effects=True, vmem_limit_bytes=62 << 20
        ),
        name="head%d" % collective_id,
    )(
        info,
        hidden,
        gain.reshape(1, model),
        bias.reshape(1, columns),
        cosine,
        sine,
        weight,
        key_cache,
        value_cache,
    )


def on_device(
    hidden,
    cached_len,
    attn_gain,
    query_key_value_weight,
    b_qkv,
    key_cache,
    value_cache,
    w_out,
    ffn_gain,
    w_gate,
    w_up,
    w_down,
):
    size = lax.axis_size("head")
    index_here = lax.axis_index("head")
    own_rows = hidden[0]
    fresh, model = own_rows.shape
    tokens = fresh * size
    heads_here = QUERY_HEADS // size
    row_start = index_here * fresh
    cache_length = key_cache.shape[1]
    key_start = QUERY_HEADS * HEAD_WIDTH
    coarse = max(fresh // 16, 1)

    cosine, sine = rope_tables(cached_len[0] + jnp.arange(tokens, dtype=jnp.int32))
    own_cosine = lax.dynamic_slice_in_dim(cosine, row_start, fresh, 0)[:, None, :]
    own_sine = lax.dynamic_slice_in_dim(sine, row_start, fresh, 0)[:, None, :]

    if size == 8 and fresh == 32:
        info = jnp.reshape(cached_len[0] - index_here * cache_length, (1,)).astype(jnp.int32)
        attn, new_keys, new_values = head(
            info,
            own_rows,
            attn_gain,
            b_qkv,
            cosine,
            sine,
            query_key_value_weight,
            key_cache[0],
            value_cache[0],
            2,
        )
        result = tail(attn, own_rows, ffn_gain, w_out, w_gate, w_up, w_down, 7)
    else:
        normed = gather(rms_norm(own_rows, attn_gain), size, coarse, 0).reshape(tokens, model)
        qkv_part = (
            jnp.dot(normed, query_key_value_weight, preferred_element_type=jnp.float32)
            + b_qkv.astype(jnp.float32)
        ).astype(jnp.bfloat16)
        qkv = jnp.transpose(gather(qkv_part, size, 4, 1), (1, 0, 2)).reshape(tokens, -1)
        own = lax.dynamic_slice(
            qkv, (row_start, key_start), (fresh, 2 * KEY_VALUE_HEADS * HEAD_WIDTH)
        )
        key_data = own[:, : KEY_VALUE_HEADS * HEAD_WIDTH].astype(jnp.float32)
        key_data = key_data.reshape(fresh, KEY_VALUE_HEADS, HEAD_WIDTH)
        turned = jnp.roll(key_data, HEAD_WIDTH // 2, axis=-1)
        new_keys = (key_data * own_cosine + turned * own_sine).astype(jnp.bfloat16)
        new_keys = new_keys.reshape(fresh, KEY_VALUE_HEADS * HEAD_WIDTH)
        new_values = own[:, KEY_VALUE_HEADS * HEAD_WIDTH :]

        info = jnp.stack([cached_len[0] - index_here * cache_length, row_start]).astype(jnp.int32)
        sums = attend(info, qkv, key_cache[0], value_cache[0], new_keys, new_values, cosine, sine)
        sums = sums.reshape(size, heads_here, HEAD_WIDTH + TAIL, tokens)
        mixed = scatter(sums, size, join_sums, 3)
        total = mixed[:, HEAD_WIDTH : HEAD_WIDTH + 1] + mixed[:, HEAD_WIDTH + 1 : HEAD_WIDTH + 2]
        attn = (mixed[:, :HEAD_WIDTH] / total).astype(jnp.bfloat16)
        attn = jnp.transpose(attn, (2, 0, 1)).reshape(tokens, heads_here * HEAD_WIDTH)
        projected = jnp.dot(attn, w_out, preferred_element_type=jnp.float32).astype(jnp.bfloat16)
        blocks = (size, coarse, fresh // coarse, model)
        projected = scatter(projected.reshape(blocks), size, add_blocks, 4).reshape(fresh, model)
        middle = (own_rows.astype(jnp.float32) + projected).astype(jnp.bfloat16)
        normed_two = gather(rms_norm(middle, ffn_gain), size, coarse, 5).reshape(tokens, model)
        ffn_part = feed(normed_two, w_gate, w_up, w_down)
        ffn_sum = scatter(ffn_part.reshape(blocks), size, add_blocks, 6).reshape(fresh, model)
        result = (middle.astype(jnp.float32) + ffn_sum).astype(jnp.bfloat16)
    return (result[None], new_keys[None], new_values[None])


def solution(mesh):
    in_specs = (
        P("req", "head", None),
        P("req"),
        P(),
        P(None, "head"),
        P("head"),
        P("req", "head", None),
        P("req", "head", None),
        P("head", None),
        P(),
        P(None, "head"),
        P(None, "head"),
        P("head", None),
    )
    out_specs = (P("req", "head", None), P("req", "head", None), P("req", "head", None))
    return jax.shard_map(
        on_device, mesh=mesh, in_specs=in_specs, out_specs=out_specs, check_vma=False
    )
```

```python
import functools
import math

import jax
import jax.numpy as jnp
from jax import lax
from jax.experimental import pallas as pl
from jax.experimental.pallas import tpu as pltpu
from jax.sharding import PartitionSpec as P

QUERY_HEADS = 32
KEY_VALUE_HEADS = 8
HEAD_WIDTH = 128
GROUP = QUERY_HEADS // KEY_VALUE_HEADS
SCALE = 1.0 / math.sqrt(HEAD_WIDTH)
TAIL = 16
FEED_TILE = 432
FEED_COLUMNS = 1024
TAIL_CHUNK = 512
FEED_GROUP = 1
HEAD_CHUNK = 1024
ATTEND_LAG = 2
REDUCE_LAG = 4
PAIR_LAG = 1
HOP_LAG = 2

rope_base = 1000000.0
MESH = pl.DeviceIdType.MESH


def rms_norm(values, gain):
    data = values.astype(jnp.float32)
    spread = jnp.mean(data * data, axis=-1, keepdims=True)
    return (data * lax.rsqrt(spread + 1e-06) * gain).astype(jnp.bfloat16)


def rope_halves(positions):
    half_dim = HEAD_WIDTH // 2
    inverse = rope_base ** (-(jnp.arange(half_dim, dtype=jnp.float32) * 2.0 / HEAD_WIDTH))
    angles = positions.astype(jnp.float32)[:, None] * inverse[None, :]
    return jnp.cos(angles), jnp.sin(angles)


def rope_tables(positions):
    cosine, sine = rope_halves(positions)
    return (
        jnp.concatenate([cosine, cosine], axis=-1),
        jnp.concatenate([-sine, sine], axis=-1),
    )


def chain_barrier(chips, me, chip, partner):
    barrier = pltpu.get_barrier_semaphore()
    pl.semaphore_signal(barrier, inc=1, device_id={"head": partner}, device_id_type=MESH)

    @pl.when(chip > 0)
    def _():
        pl.semaphore_signal(barrier, inc=1, device_id={"head": me - 2}, device_id_type=MESH)

    @pl.when(chip < chips - 1)
    def _():
        pl.semaphore_signal(barrier, inc=1, device_id={"head": me + 2}, device_id_type=MESH)

    below = (chip + chips - 1) // chips
    above = (2 * chips - 2 - chip) // chips
    pl.semaphore_wait(barrier, 1 + below + above)


def gather_kernel(
    chips, pieces, x_ref, out_ref, own_sem, up_send, down_send, chip_recv, pair_send, pair_recv
):
    me = lax.axis_index("head")
    chip = me // 2
    core = me % 2
    partner = chip * 2 + (1 - core)
    chain_barrier(chips, me, chip, partner)

    def to_up(src, owner, c):
        return pltpu.make_async_remote_copy(
            src_ref=src,
            dst_ref=out_ref.at[owner * 2 + core, c],
            send_sem=up_send.at[owner, c],
            recv_sem=chip_recv.at[owner, c],
            device_id={"head": me + 2},
            device_id_type=MESH,
        )

    def to_down(src, owner, c):
        return pltpu.make_async_remote_copy(
            src_ref=src,
            dst_ref=out_ref.at[owner * 2 + core, c],
            send_sem=down_send.at[owner, c],
            recv_sem=chip_recv.at[owner, c],
            device_id={"head": me - 2},
            device_id_type=MESH,
        )

    def to_partner(src, owner, c):
        return pltpu.make_async_remote_copy(
            src_ref=src,
            dst_ref=out_ref.at[owner * 2 + core, c],
            send_sem=pair_send.at[owner, c],
            recv_sem=pair_recv.at[owner, c],
            device_id={"head": partner},
            device_id_type=MESH,
        )

    def begin(c, carry):
        @pl.when(chip < chips - 1)
        def _():
            to_up(x_ref.at[c], chip, c).start()

        @pl.when(chip > 0)
        def _():
            to_down(x_ref.at[c], chip, c).start()

        to_partner(x_ref.at[c], chip, c).start()
        return carry

    lax.fori_loop(0, pieces, begin, 0)
    own = pltpu.make_async_copy(x_ref, out_ref.at[me], own_sem)
    own.start()

    def step(t, carry):
        s = 1 + t // pieces
        c = t % pieces

        @pl.when(chip - s >= 0)
        def _():
            owner = chip - s
            held = out_ref.at[owner * 2 + core, c]
            to_up(held, owner, c).wait_recv()

            @pl.when(chip < chips - 1)
            def _():
                to_up(held, owner, c).start()

            to_partner(held, owner, c).start()

        @pl.when(chip + s <= chips - 1)
        def _():
            owner = chip + s
            held = out_ref.at[owner * 2 + core, c]
            to_down(held, owner, c).wait_recv()

            @pl.when(chip > 0)
            def _():
                to_down(held, owner, c).start()

            to_partner(held, owner, c).start()

        return carry

    lax.fori_loop(0, (chips - 1) * pieces, step, 0)
    own.wait()

    def finish(t, carry):
        owner = t // pieces
        c = t % pieces
        to_partner(x_ref.at[c], owner, c).wait()

        @pl.when((chip < chips - 1) & (owner <= chip))
        def _():
            to_up(x_ref.at[c], owner, c).wait_send()

        @pl.when((chip > 0) & (owner >= chip))
        def _():
            to_down(x_ref.at[c], owner, c).wait_send()

        return carry

    lax.fori_loop(0, chips * pieces, finish, 0)


def gather(x, size, pieces, collective_id):
    chips = size // 2
    rows, width = x.shape
    x = x.reshape(pieces, rows // pieces, width)
    return pl.pallas_call(
        functools.partial(gather_kernel, chips, pieces),
        out_shape=jax.ShapeDtypeStruct((size,) + x.shape, x.dtype),
        in_specs=[pl.BlockSpec(memory_space=pltpu.VMEM)],
        out_specs=pl.BlockSpec(memory_space=pltpu.VMEM),
        scratch_shapes=[pltpu.SemaphoreType.DMA(())]
        + [pltpu.SemaphoreType.DMA((chips, pieces))] * 5,
        compiler_params=pltpu.CompilerParams(
            collective_id=collective_id, has_side_effects=True, vmem_limit_bytes=16 << 20
        ),
        name="gather%d" % collective_id,
    )(x).reshape(size, rows, width)


def add_blocks(a, b):
    return a.astype(jnp.float32) + b.astype(jnp.float32)


def pack_sums(sums, total, top):
    def narrow(v):
        return v.astype(jnp.bfloat16).astype(jnp.float32)

    total_high = narrow(total)
    top_high = narrow(top)
    top_middle = narrow(top - top_high)
    rows = [total_high, total - total_high, top_high, top_middle, top - top_high - top_middle]
    index = lax.broadcasted_iota(jnp.int32, (TAIL, sums.shape[1]), 0)
    tail = jnp.zeros((TAIL, sums.shape[1]), jnp.float32)
    for place, row in enumerate(rows):
        tail = jnp.where(index == place, row, tail)
    return jnp.concatenate([sums, tail], axis=0)


def join_sums(a, b):
    def unpack(block):
        block = block.astype(jnp.float32)
        tail = block[HEAD_WIDTH:]
        return block[:HEAD_WIDTH], tail[0:1] + tail[1:2], (tail[2:3] + tail[3:4]) + tail[4:5]

    sums_a, total_a, top_a = unpack(a)
    sums_b, total_b, top_b = unpack(b)
    top = jnp.maximum(top_a, top_b)
    scale_a = jnp.exp((top_a - top) * SCALE)
    scale_b = jnp.exp((top_b - top) * SCALE)
    return pack_sums(
        sums_a * scale_a + sums_b * scale_b, total_a * scale_a + total_b * scale_b, top
    )


def scatter_kernel(
    join,
    chips,
    pieces,
    x_ref,
    out_ref,
    pair,
    up,
    down,
    pair_send,
    pair_recv,
    up_send,
    up_recv,
    down_send,
    down_recv,
):
    me = lax.axis_index("head")
    chip = me // 2
    core = me % 2
    partner = chip * 2 + (1 - core)
    half = chip // (chips // 2)
    chain_barrier(chips, me, chip, partner)

    def to_partner(j, c):
        return pltpu.make_async_remote_copy(
            src_ref=x_ref.at[2 * j + (1 - core), c],
            dst_ref=pair.at[j, c],
            send_sem=pair_send.at[j, c],
            recv_sem=pair_recv.at[j, c],
            device_id={"head": partner},
            device_id_type=MESH,
        )

    def to_up(src, j, c):
        return pltpu.make_async_remote_copy(
            src_ref=src.at[j, c],
            dst_ref=up.at[j, c],
            send_sem=up_send.at[j, c],
            recv_sem=up_recv.at[j, c],
            device_id={"head": me + 2},
            device_id_type=MESH,
        )

    def to_down(src, j, c):
        return pltpu.make_async_remote_copy(
            src_ref=src.at[j, c],
            dst_ref=down.at[j, c],
            send_sem=down_send.at[j, c],
            recv_sem=down_recv.at[j, c],
            device_id={"head": me - 2},
            device_id_type=MESH,
        )

    def order(k):
        return (1 - half) * (chips - 1 - k) + half * k

    def first(t, carry):
        to_partner(order(t // pieces), t % pieces).start()
        return carry

    lax.fori_loop(0, chips * pieces, first, 0)

    def second(t, carry):
        j = order(t // pieces)
        c = t % pieces
        to_partner(j, c).wait_recv()
        pair[j, c] = join(pair[j, c], x_ref[2 * j + core, c]).astype(pair.dtype)

        @pl.when((chip == 0) & (j > 0))
        def _():
            to_up(pair, j, c).start()

        @pl.when((chip == chips - 1) & (j < chips - 1))
        def _():
            to_down(pair, j, c).start()

        return carry

    lax.fori_loop(0, chips * pieces, second, 0)

    def move_up(j, c):
        @pl.when((chip > 0) & (j > chip))
        def _():
            to_up(up, j, c).wait_recv()
            up[j, c] = join(up[j, c], pair[j, c]).astype(up.dtype)
            to_up(up, j, c).start()

    def move_down(j, c):
        @pl.when((chip < chips - 1) & (j < chip))
        def _():
            to_down(down, j, c).wait_recv()
            down[j, c] = join(down[j, c], pair[j, c]).astype(down.dtype)
            to_down(down, j, c).start()

    def third(t, carry):
        s = t // pieces
        c = t % pieces

        @pl.when(half == 0)
        def _():
            move_up(chips - 1 - s, c)

        move_down(s, c)

        @pl.when(half == 1)
        def _():
            move_up(chips - 1 - s, c)

        return carry

    lax.fori_loop(0, (chips - 1) * pieces, third, 0)

    def total(c, carry):
        out_ref[c] = pair[chip, c].astype(jnp.float32)

        @pl.when(chip > 0)
        def _():
            to_up(up, chip, c).wait_recv()
            out_ref[c] = join(out_ref[c], up[chip, c])

        @pl.when(chip < chips - 1)
        def _():
            to_down(down, chip, c).wait_recv()
            out_ref[c] = join(out_ref[c], down[chip, c])

        return carry

    lax.fori_loop(0, pieces, total, 0)

    def finish(t, carry):
        j = t // pieces
        c = t % pieces
        to_partner(j, c).wait_send()

        @pl.when(j > chip)
        def _():
            to_up(pair, j, c).wait_send()

        @pl.when(j < chip)
        def _():
            to_down(pair, j, c).wait_send()

        return carry

    lax.fori_loop(0, chips * pieces, finish, 0)


def scatter(x, size, join, collective_id):
    chips = size // 2
    shape = x.shape[1:]
    pieces = shape[0]
    return pl.pallas_call(
        functools.partial(scatter_kernel, join, chips, pieces),
        out_shape=jax.ShapeDtypeStruct(shape, jnp.float32),
        in_specs=[pl.BlockSpec(memory_space=pltpu.VMEM)],
        out_specs=pl.BlockSpec(memory_space=pltpu.VMEM),
        scratch_shapes=[pltpu.VMEM((chips,) + shape, x.dtype)] * 3
        + [pltpu.SemaphoreType.DMA((chips, pieces))] * 6,
        compiler_params=pltpu.CompilerParams(
            collective_id=collective_id, has_side_effects=True, vmem_limit_bytes=24 << 20
        ),
        name="scatter%d" % collective_id,
    )(x)


def attend_kernel(info_ref, q_ref, kc_ref, vc_ref, kn_ref, vn_ref, cos_ref, sin_ref, sum_ref):
    tokens = q_ref.shape[0]
    length = kc_ref.shape[0]
    fresh = kn_ref.shape[0]
    width = GROUP * tokens
    cosine = cos_ref[...]
    sine = sin_ref[...]
    parts = []
    for j in range(GROUP):
        data = q_ref[:, j * HEAD_WIDTH : (j + 1) * HEAD_WIDTH].astype(jnp.float32)
        turned = pltpu.roll(data, HEAD_WIDTH // 2, 1)
        parts.append((data * cosine + turned * sine).astype(jnp.bfloat16))
    query = jnp.concatenate(parts, axis=0)
    last = (((1,), (1,)), ((), ()))
    first = (((0,), (0,)), ((), ()))
    old = lax.dot_general(kc_ref[...], query, last, preferred_element_type=jnp.float32)
    new = lax.dot_general(kn_ref[...], query, last, preferred_element_type=jnp.float32)
    old_ids = lax.broadcasted_iota(jnp.int32, (length, 1), 0)
    old = jnp.where(old_ids < info_ref[0], old, -1e30)
    new_ids = lax.broadcasted_iota(jnp.int32, (fresh, width), 0) + info_ref[1]
    token_ids = lax.broadcasted_iota(jnp.int32, (fresh, width), 1) % tokens
    new = jnp.where(new_ids <= token_ids, new, -1e30)
    top = jnp.maximum(jnp.max(old, axis=0, keepdims=True), jnp.max(new, axis=0, keepdims=True))
    top = jnp.maximum(top, -1e29)
    old = jnp.exp((old - top) * SCALE)
    new = jnp.exp((new - top) * SCALE)
    total = jnp.sum(old, axis=0, keepdims=True) + jnp.sum(new, axis=0, keepdims=True)
    sums = lax.dot_general(
        vc_ref[...], old.astype(jnp.bfloat16), first, preferred_element_type=jnp.float32
    ) + lax.dot_general(
        vn_ref[...], new.astype(jnp.bfloat16), first, preferred_element_type=jnp.float32
    )
    packed = pack_sums(sums, total, top).astype(jnp.bfloat16)
    for j in range(GROUP):
        sum_ref[0, j] = packed[:, j * tokens : (j + 1) * tokens]


def attend(info, qkv, key_cache, value_cache, new_keys, new_values, cosine, sine):
    tokens = qkv.shape[0]
    length = key_cache.shape[0]
    fresh = new_keys.shape[0]

    def head_block(rows):
        return pl.BlockSpec((rows, HEAD_WIDTH), lambda g, info: (0, g))

    def whole_block(shape):
        return pl.BlockSpec(shape, lambda g, info: (0, 0))

    return pl.pallas_call(
        attend_kernel,
        grid_spec=pltpu.PrefetchScalarGridSpec(
            num_scalar_prefetch=1,
            grid=(KEY_VALUE_HEADS,),
            in_specs=[
                pl.BlockSpec((tokens, GROUP * HEAD_WIDTH), lambda g, info: (0, g)),
                head_block(length),
                head_block(length),
                head_block(fresh),
                head_block(fresh),
                whole_block((tokens, HEAD_WIDTH)),
                whole_block((tokens, HEAD_WIDTH)),
            ],
            out_specs=pl.BlockSpec(
                (1, GROUP, HEAD_WIDTH + TAIL, tokens), lambda g, info: (g, 0, 0, 0)
            ),
        ),
        out_shape=jax.ShapeDtypeStruct(
            (KEY_VALUE_HEADS, GROUP, HEAD_WIDTH + TAIL, tokens), jnp.bfloat16
        ),
        compiler_params=pltpu.CompilerParams(
            dimension_semantics=("arbitrary",), vmem_limit_bytes=32 << 20
        ),
        name="attend",
    )(info, qkv, key_cache, value_cache, new_keys, new_values, cosine, sine)


def feed_kernel(steps, x_ref, gate_ref, up_ref, down_ref, out_ref, turned, active):
    step = pl.program_id(0)
    tile = gate_ref.shape[0]

    @pl.when(step == 0)
    def _():
        turned[...] = jnp.transpose(x_ref[...])

    @pl.when(step < steps)
    def _():
        x = turned[...]
        gate = jnp.dot(gate_ref[...], x, preferred_element_type=jnp.float32)
        upward = jnp.dot(up_ref[...], x, preferred_element_type=jnp.float32)
        active[pl.ds(pl.multiple_of(step * tile, tile), tile), :] = (
            gate / (1.0 + jnp.exp(-gate)) * upward
        ).astype(jnp.bfloat16)

    @pl.when(step >= steps)
    def _():
        out_ref[...] = lax.dot_general(
            active[...],
            down_ref[...],
            (((0,), (0,)), ((), ())),
            preferred_element_type=jnp.float32,
        ).astype(jnp.bfloat16)


def feed(x, w_gate, w_up, w_down):
    tokens, model = x.shape
    units = w_down.shape[0]
    steps = units // FEED_TILE
    tile = units // steps
    weight = pl.BlockSpec((tile, model), lambda i: (jnp.minimum(i, steps - 1), 0))
    return pl.pallas_call(
        functools.partial(feed_kernel, steps),
        grid=(steps + model // FEED_COLUMNS,),
        in_specs=[
            pl.BlockSpec((tokens, model), lambda i: (0, 0)),
            weight,
            weight,
            pl.BlockSpec((units, FEED_COLUMNS), lambda i: (0, jnp.maximum(i - steps, 0))),
        ],
        out_specs=pl.BlockSpec((tokens, FEED_COLUMNS), lambda i: (0, jnp.maximum(i - steps, 0))),
        out_shape=jax.ShapeDtypeStruct((tokens, model), jnp.bfloat16),
        scratch_shapes=[
            pltpu.VMEM((model, tokens), jnp.bfloat16),
            pltpu.VMEM((units, tokens), jnp.bfloat16),
        ],
        compiler_params=pltpu.CompilerParams(
            dimension_semantics=("arbitrary",), vmem_limit_bytes=48 << 20
        ),
        name="feed",
    )(x, jnp.transpose(w_gate), jnp.transpose(w_up), w_down)


def tail_kernel(
    n_chunks,
    attn_ref,
    hidden_ref,
    gain_ref,
    w_out_hbm,
    gate_hbm,
    up_hbm,
    w_down_hbm,
    out_ref,
    w_out,
    gate_w,
    up_w,
    w_down,
    product,
    own,
    pair_out,
    pair_in,
    outer_out,
    outer_in,
    cross_out,
    cross_in,
    middle,
    squares,
    x,
    spread,
    gate_sum,
    up_sum,
    active,
    rows_own,
    rows_pair_out,
    rows_pair_in,
    rows_outer_out,
    rows_outer_in,
    rows_cross_out,
    rows_cross_in,
    rows_last_out,
    rows_last_in,
    weight_sem,
    pair_sem,
    outer_sem,
    cross_sem,
    near_sem,
    far_sem,
    far_out_sem,
    near_pair_sem,
    far_pair_sem,
    rows_pair_sem,
    rows_outer_sem,
    rows_cross_sem,
    rows_last_sem,
):
    me = lax.axis_index("head")
    chip = me // 2
    core = me % 2
    side = chip // 2
    partner = chip * 2 + (1 - core)
    inner = (chip == 1) | (chip == 2)
    outer = (chip == 0) | (chip == 3)
    toward = 2 - 4 * side
    near_device = me + toward
    outer_device = me - toward
    tokens = attn_ref.shape[0]
    half = tokens // 2
    part = half // 2
    own_rows = hidden_ref.shape[0]
    chunk = w_out.shape[2]
    slots = gate_w.shape[0]
    near_start = pl.multiple_of(side * half + core * part, part)
    far_start = pl.multiple_of((1 - side) * half + core * part, part)

    def columns(j):
        return pl.ds(pl.multiple_of(j * chunk, chunk), chunk)

    def group_columns(j):
        return pl.ds(pl.multiple_of((j % FEED_GROUP) * chunk, chunk), chunk)

    def group_all(j):
        return pl.ds(pl.multiple_of(j * FEED_GROUP * chunk, FEED_GROUP * chunk), FEED_GROUP * chunk)

    def load_out(j):
        return pltpu.make_async_copy(w_out_hbm.at[:, columns(j)], w_out.at[j], weight_sem.at[0, j])

    def load_gate(j):
        return pltpu.make_async_copy(
            gate_hbm.at[:, group_all(j)], gate_w.at[j % slots], weight_sem.at[1, j]
        )

    def load_up(j):
        return pltpu.make_async_copy(
            up_hbm.at[:, group_all(j)], up_w.at[j % slots], weight_sem.at[2, j]
        )

    def load_down(j):
        return pltpu.make_async_copy(
            w_down_hbm.at[:, columns(j)], w_down.at[j], weight_sem.at[3, j]
        )

    def remote(src, dst, sems, j, device):
        return pltpu.make_async_remote_copy(
            src_ref=src,
            dst_ref=dst,
            send_sem=sems.at[0, j],
            recv_sem=sems.at[1, j],
            device_id={"head": device},
            device_id_type=MESH,
        )

    def pair_copy(j):
        return remote(pair_out.at[j], pair_in.at[j], pair_sem, j, partner)

    def outer_copy(j):
        return remote(outer_out.at[j], outer_in.at[j], outer_sem, j, near_device)

    def cross_copy(j):
        return remote(cross_out.at[j], cross_in.at[j], cross_sem, j, near_device)

    def x_copy(j, start, sems, device):
        ref = x.at[j // FEED_GROUP, pl.ds(start, part), group_columns(j)]
        return remote(ref, ref, sems, j, device)

    def spread_copy(start, sems, device):
        ref = spread.at[pl.ds(start, part)]
        return remote(ref, ref, sems, n_chunks, device)

    def begin_out(j, carry):
        load_out(j).start()
        return carry

    def begin_feed(j, carry):
        load_gate(j).start()
        load_up(j).start()
        return carry

    lax.fori_loop(0, n_chunks, begin_out, 0)
    lax.fori_loop(0, slots, begin_feed, 0)
    chain_barrier(4, me, chip, partner)
    squares[...] = jnp.zeros_like(squares)
    gate_sum[...] = jnp.zeros_like(gate_sum)
    up_sum[...] = jnp.zeros_like(up_sum)

    def stage(t, lag, also=None):
        j = t - lag
        ready = (j >= 0) & (j < n_chunks)
        return ready if also is None else ready & also

    lag_outer = PAIR_LAG + HOP_LAG
    lag_cross = lag_outer + HOP_LAG
    lag_near = lag_cross + HOP_LAG
    lag_far = lag_near + HOP_LAG
    lag_feed = lag_far + PAIR_LAG

    def step(t, carry):
        @pl.when(stage(t, lag_far, outer))
        def _():
            j = t - lag_far
            x_copy(j, far_start, far_out_sem, near_device).wait_recv()
            x_copy(j, far_start, far_pair_sem, partner).start()

            @pl.when(j == n_chunks - 1)
            def _():
                spread_copy(far_start, far_out_sem, near_device).wait_recv()
                spread_copy(far_start, far_pair_sem, partner).start()

        @pl.when(stage(t, lag_near, inner))
        def _():
            j = t - lag_near
            x_copy(j, far_start, far_sem, near_device).wait_recv()
            x_copy(j, far_start, far_out_sem, outer_device).start()
            x_copy(j, far_start, far_pair_sem, partner).start()

            @pl.when(j == n_chunks - 1)
            def _():
                spread_copy(far_start, far_sem, near_device).wait_recv()
                spread_copy(far_start, far_out_sem, outer_device).start()
                spread_copy(far_start, far_pair_sem, partner).start()

        @pl.when(stage(t, lag_near, outer))
        def _():
            j = t - lag_near
            x_copy(j, near_start, near_sem, near_device).wait_recv()
            x_copy(j, near_start, near_pair_sem, partner).start()

            @pl.when(j == n_chunks - 1)
            def _():
                spread_copy(near_start, near_sem, near_device).wait_recv()
                spread_copy(near_start, near_pair_sem, partner).start()

        @pl.when(stage(t, lag_cross, inner))
        def _():
            j = t - lag_cross
            cross_copy(j).wait_recv()
            mid = (own[j, side] + cross_in[j].astype(jnp.float32)).astype(jnp.bfloat16)
            middle[j] = mid
            data = mid.astype(jnp.float32)
            square = data * data
            folded = square[:, :HEAD_WIDTH]
            for k in range(1, chunk // HEAD_WIDTH):
                folded = folded + square[:, k * HEAD_WIDTH : (k + 1) * HEAD_WIDTH]
            squares[...] += folded
            x[j // FEED_GROUP, pl.ds(near_start, part), group_columns(j)] = (
                data * gain_ref[:, columns(j)]
            ).astype(jnp.bfloat16)
            x_copy(j, near_start, near_sem, outer_device).start()
            x_copy(j, near_start, far_sem, near_device).start()
            x_copy(j, near_start, near_pair_sem, partner).start()

            @pl.when(j == n_chunks - 1)
            def _():
                mean = jnp.sum(squares[...], axis=1, keepdims=True) / (n_chunks * chunk)
                spread[pl.ds(near_start, part)] = jnp.broadcast_to(
                    lax.rsqrt(mean + 1e-06), (part, HEAD_WIDTH)
                )
                spread_copy(near_start, near_sem, outer_device).start()
                spread_copy(near_start, far_sem, near_device).start()
                spread_copy(near_start, near_pair_sem, partner).start()

        @pl.when(stage(t, lag_outer, inner))
        def _():
            j = t - lag_outer
            outer_copy(j).wait_recv()
            cross_out[j] = (own[j, 1 - side] + outer_in[j, 1 - side].astype(jnp.float32)).astype(
                jnp.bfloat16
            )
            cross_copy(j).start()
            own[j, side] += outer_in[j, side].astype(jnp.float32)

        @pl.when(stage(t, PAIR_LAG))
        def _():
            j = t - PAIR_LAG
            pair_copy(j).wait_recv()
            total = own[j] + pair_in[j].astype(jnp.float32)

            @pl.when(outer)
            def _():
                outer_out[j] = total.astype(jnp.bfloat16)
                outer_copy(j).start()

            @pl.when(inner)
            def _():
                own[j] = total

        @pl.when(t < n_chunks)
        def _():
            load_out(t).wait()
            product[...] = jnp.dot(attn_ref[...], w_out[t], preferred_element_type=jnp.float32)
            mine = pl.ds(pl.multiple_of(me * own_rows, own_rows), own_rows)
            product[mine] += hidden_ref[:, columns(t)].astype(jnp.float32)
            for f in range(2):
                keep = pl.ds(pl.multiple_of(f * half + core * part, part), part)
                give = pl.ds(pl.multiple_of(f * half + (1 - core) * part, part), part)
                own[t, f] = product[keep]
                pair_out[t, f] = product[give].astype(jnp.bfloat16)
            pair_copy(t).start()
            load_down(t).start()

        @pl.when(stage(t, lag_feed))
        def _():
            j = t - lag_feed
            x_copy(j, near_start, near_pair_sem, partner).wait_recv()
            x_copy(j, far_start, far_pair_sem, partner).wait_recv()

            @pl.when(j % FEED_GROUP == FEED_GROUP - 1)
            def _():
                g = j // FEED_GROUP
                load_gate(g).wait()
                load_up(g).wait()
                last = (((1,), (1,)), ((), ()))
                gate_sum[...] += lax.dot_general(
                    gate_w[g % slots], x[g], last, preferred_element_type=jnp.float32
                )
                up_sum[...] += lax.dot_general(
                    up_w[g % slots], x[g], last, preferred_element_type=jnp.float32
                )

                @pl.when(g + slots < n_chunks // FEED_GROUP)
                def _():
                    load_gate(g + slots).start()
                    load_up(g + slots).start()

        return carry

    lax.fori_loop(0, n_chunks + lag_feed, step, 0)
    spread_copy(near_start, near_pair_sem, partner).wait_recv()
    spread_copy(far_start, far_pair_sem, partner).wait_recv()
    scale = jnp.transpose(spread[...])[0:1]
    units = gate_sum.shape[0]
    for start in range(0, units, HEAD_WIDTH):
        stop = min(start + HEAD_WIDTH, units)
        gate = gate_sum[start:stop] * scale
        upward = up_sum[start:stop] * scale
        block = gate / (1.0 + jnp.exp(-gate)) * upward
        active[:, start:stop] = jnp.transpose(block).astype(jnp.bfloat16)

    near_chip = chip + 1 - 2 * side
    outer_chip = 3 * side
    other_outer = 3 - outer_chip
    other_inner = 3 - chip

    def rows_pair_copy(j):
        return remote(rows_pair_out.at[j], rows_pair_in.at[j], rows_pair_sem, j, partner)

    def rows_outer_copy(j):
        return remote(rows_outer_out.at[j], rows_outer_in.at[j], rows_outer_sem, j, near_device)

    def rows_cross_copy(j):
        return remote(rows_cross_out.at[j], rows_cross_in.at[j], rows_cross_sem, j, near_device)

    def rows_last_copy(j, device):
        return remote(rows_last_out.at[j], rows_last_in.at[j], rows_last_sem, j, device)

    lag_last = lag_cross + HOP_LAG

    def rows_step(t, carry):
        @pl.when(stage(t, lag_last, outer))
        def _():
            j = t - lag_last
            rows_last_copy(j, near_device).wait_recv()
            out_ref[:, columns(j)] = (
                rows_own[j, chip] + rows_last_in[j].astype(jnp.float32)
            ).astype(jnp.bfloat16)

        @pl.when(stage(t, lag_cross, inner))
        def _():
            j = t - lag_cross
            rows_cross_copy(j).wait_recv()
            rows_last_out[j] = (
                rows_own[j, outer_chip] + rows_cross_in[j, 1].astype(jnp.float32)
            ).astype(jnp.bfloat16)
            rows_last_copy(j, outer_device).start()
            out_ref[:, columns(j)] = (
                rows_own[j, chip] + rows_cross_in[j, 0].astype(jnp.float32)
            ).astype(jnp.bfloat16)

        @pl.when(stage(t, lag_outer, inner))
        def _():
            j = t - lag_outer
            rows_outer_copy(j).wait_recv()
            rows_cross_out[j, 0] = (
                rows_own[j, other_inner] + rows_outer_in[j, 1].astype(jnp.float32)
            ).astype(jnp.bfloat16)
            rows_cross_out[j, 1] = (
                rows_own[j, other_outer] + rows_outer_in[j, 2].astype(jnp.float32)
            ).astype(jnp.bfloat16)
            rows_cross_copy(j).start()
            rows_own[j, chip] += rows_outer_in[j, 0].astype(jnp.float32)

        @pl.when(stage(t, PAIR_LAG))
        def _():
            j = t - PAIR_LAG
            rows_pair_copy(j).wait_recv()
            for k in range(4):
                rows_own[j, k] += rows_pair_in[j, k].astype(jnp.float32)

            @pl.when(outer)
            def _():
                for k in range(3):
                    target = (1 - side) * (1 + k) + side * (2 - k)
                    rows_outer_out[j, k] = rows_own[j, target].astype(jnp.bfloat16)
                rows_outer_copy(j).start()

        @pl.when(t < n_chunks)
        def _():
            load_down(t).wait()
            product[...] = jnp.dot(active[...], w_down[t], preferred_element_type=jnp.float32)

            @pl.when(inner)
            def _():
                product[pl.ds(near_start, part)] += middle[t].astype(jnp.float32)

            for k in range(4):
                keep = pl.ds(pl.multiple_of((2 * k + core) * own_rows, own_rows), own_rows)
                give = pl.ds(pl.multiple_of((2 * k + 1 - core) * own_rows, own_rows), own_rows)
                rows_own[t, k] = product[keep]
                rows_pair_out[t, k] = product[give].astype(jnp.bfloat16)
            rows_pair_copy(t).start()

        return carry

    lax.fori_loop(0, n_chunks + lag_last, rows_step, 0)

    def finish(j, carry):
        pair_copy(j).wait_send()
        rows_pair_copy(j).wait_send()
        x_copy(j, near_start, near_pair_sem, partner).wait_send()
        x_copy(j, far_start, far_pair_sem, partner).wait_send()

        @pl.when(outer)
        def _():
            outer_copy(j).wait_send()
            rows_outer_copy(j).wait_send()

        @pl.when(inner)
        def _():
            cross_copy(j).wait_send()
            x_copy(j, near_start, near_sem, outer_device).wait_send()
            x_copy(j, near_start, far_sem, near_device).wait_send()
            x_copy(j, far_start, far_out_sem, outer_device).wait_send()
            rows_cross_copy(j).wait_send()
            rows_last_copy(j, outer_device).wait_send()

        return carry

    lax.fori_loop(0, n_chunks, finish, 0)
    spread_copy(near_start, near_pair_sem, partner).wait_send()
    spread_copy(far_start, far_pair_sem, partner).wait_send()

    @pl.when(inner)
    def _():
        spread_copy(near_start, near_sem, outer_device).wait_send()
        spread_copy(near_start, far_sem, near_device).wait_send()
        spread_copy(far_start, far_out_sem, outer_device).wait_send()


def tail(attn, hidden, gain, w_out, w_gate, w_up, w_down, collective_id):
    tokens, inner = attn.shape
    own_rows, model = hidden.shape
    units = w_down.shape[0]
    chunk = TAIL_CHUNK
    n_chunks = model // chunk
    slots = 3
    part = tokens // 4
    bf16, f32 = jnp.bfloat16, jnp.float32
    vmem = pl.BlockSpec(memory_space=pltpu.VMEM)
    hbm = pl.BlockSpec(memory_space=pl.ANY)

    def remote_sem(count):
        return pltpu.SemaphoreType.DMA((2, count))

    return pl.pallas_call(
        functools.partial(tail_kernel, n_chunks),
        out_shape=jax.ShapeDtypeStruct((own_rows, model), bf16),
        in_specs=[vmem, vmem, vmem, hbm, hbm, hbm, hbm],
        out_specs=vmem,
        scratch_shapes=[
            pltpu.VMEM((n_chunks, inner, chunk), bf16),
            pltpu.VMEM((slots, units, FEED_GROUP * chunk), bf16),
            pltpu.VMEM((slots, units, FEED_GROUP * chunk), bf16),
            pltpu.VMEM((n_chunks, units, chunk), bf16),
            pltpu.VMEM((tokens, chunk), f32),
            pltpu.VMEM((n_chunks, 2, part, chunk), f32),
            pltpu.VMEM((n_chunks, 2, part, chunk), bf16),
            pltpu.VMEM((n_chunks, 2, part, chunk), bf16),
            pltpu.VMEM((n_chunks, 2, part, chunk), bf16),
            pltpu.VMEM((n_chunks, 2, part, chunk), bf16),
            pltpu.VMEM((n_chunks, part, chunk), bf16),
            pltpu.VMEM((n_chunks, part, chunk), bf16),
            pltpu.VMEM((n_chunks, part, chunk), bf16),
            pltpu.VMEM((part, HEAD_WIDTH), f32),
            pltpu.VMEM((n_chunks // FEED_GROUP, tokens, FEED_GROUP * chunk), bf16),
            pltpu.VMEM((tokens, HEAD_WIDTH), f32),
            pltpu.VMEM((units, tokens), f32),
            pltpu.VMEM((units, tokens), f32),
            pltpu.VMEM((tokens, units), bf16),
            pltpu.VMEM((n_chunks, 4, own_rows, chunk), f32),
            pltpu.VMEM((n_chunks, 4, own_rows, chunk), bf16),
            pltpu.VMEM((n_chunks, 4, own_rows, chunk), bf16),
            pltpu.VMEM((n_chunks, 3, own_rows, chunk), bf16),
            pltpu.VMEM((n_chunks, 3, own_rows, chunk), bf16),
            pltpu.VMEM((n_chunks, 2, own_rows, chunk), bf16),
            pltpu.VMEM((n_chunks, 2, own_rows, chunk), bf16),
            pltpu.VMEM((n_chunks, own_rows, chunk), bf16),
            pltpu.VMEM((n_chunks, own_rows, chunk), bf16),
            pltpu.SemaphoreType.DMA((4, n_chunks)),
        ]
        + [remote_sem(n_chunks)] * 3
        + [remote_sem(n_chunks + 1)] * 5
        + [remote_sem(n_chunks)] * 4,
        compiler_params=pltpu.CompilerParams(
            collective_id=collective_id, has_side_effects=True, vmem_limit_bytes=62 << 20
        ),
        name="tail%d" % collective_id,
    )(
        attn,
        hidden,
        gain.reshape(1, model),
        w_out,
        jnp.transpose(w_gate),
        jnp.transpose(w_up),
        w_down,
    )


def attend_pair(key, value, new_key, new_value, query, limit, row_start, tokens):
    length = key.shape[0]
    fresh = new_key.shape[0]
    width = query.shape[0]
    last = (((1,), (1,)), ((), ()))
    first = (((0,), (0,)), ((), ()))
    old = lax.dot_general(key, query, last, preferred_element_type=jnp.float32)
    new = lax.dot_general(new_key, query, last, preferred_element_type=jnp.float32)
    old_ids = lax.broadcasted_iota(jnp.int32, (length, 1), 0)
    old = jnp.where(old_ids < limit, old, -1e30)
    new_ids = lax.broadcasted_iota(jnp.int32, (fresh, width), 0) + row_start
    token_ids = lax.broadcasted_iota(jnp.int32, (fresh, width), 1) % tokens
    new = jnp.where(new_ids <= token_ids, new, -1e30)
    top = jnp.maximum(jnp.max(old, axis=0, keepdims=True), jnp.max(new, axis=0, keepdims=True))
    top = jnp.maximum(top, -1e29)
    old = jnp.exp((old - top) * SCALE)
    new = jnp.exp((new - top) * SCALE)
    total = jnp.sum(old, axis=0, keepdims=True) + jnp.sum(new, axis=0, keepdims=True)
    sums = lax.dot_general(
        value, old.astype(jnp.bfloat16), first, preferred_element_type=jnp.float32
    ) + lax.dot_general(
        new_value, new.astype(jnp.bfloat16), first, preferred_element_type=jnp.float32
    )
    return pack_sums(sums, total, top).astype(jnp.bfloat16)


def head_kernel(
    n_chunks,
    info_ref,
    hidden_ref,
    gain_ref,
    bias_ref,
    cos_half_ref,
    sin_half_ref,
    weight_hbm,
    key_hbm,
    value_hbm,
    attn_ref,
    new_key_ref,
    new_value_ref,
    weight,
    key_cache,
    value_cache,
    cos_ref,
    sin_ref,
    x,
    total,
    pairs,
    query,
    fresh_in,
    sums,
    pair_in,
    up_in,
    down_in,
    load_sem,
    x_up_sem,
    x_down_sem,
    x_recv,
    x_pair_sem,
    q_up_sem,
    q_down_sem,
    q_recv,
    q_pair_sem,
    fresh_send,
    fresh_recv,
    sums_pair_sem,
    sums_up_sem,
    sums_down_sem,
):
    me = lax.axis_index("head")
    chip = me // 2
    core = me % 2
    chips = 4
    size = 8
    partner = chip * 2 + (1 - core)
    tokens = x.shape[1]
    own_rows = hidden_ref.shape[0]
    chunk = x.shape[2]
    length = key_cache.shape[0]
    groups = 3
    n_pairs = QUERY_HEADS // 2
    width = 2 * HEAD_WIDTH
    first_kv = n_pairs // groups
    mine = pl.ds(pl.multiple_of(me * own_rows, own_rows), own_rows)

    def columns(j):
        return pl.ds(pl.multiple_of(j * chunk, chunk), chunk)

    def load_weight(j):
        return pltpu.make_async_copy(weight_hbm.at[columns(j)], weight.at[j], load_sem.at[j])

    def load_key():
        return pltpu.make_async_copy(key_hbm, key_cache, load_sem.at[n_chunks])

    def load_value():
        return pltpu.make_async_copy(value_hbm, value_cache, load_sem.at[n_chunks + 1])

    def remote(src, dst, send, recv, device):
        return pltpu.make_async_remote_copy(
            src_ref=src,
            dst_ref=dst,
            send_sem=send,
            recv_sem=recv,
            device_id={"head": device},
            device_id_type=MESH,
        )

    def begin(j, carry):
        load_weight(j).start()
        return carry

    lax.fori_loop(0, n_chunks, begin, 0)
    load_key().start()
    load_value().start()

    barrier = pltpu.get_barrier_semaphore()

    def greet(k, carry):
        pl.semaphore_signal(
            barrier, inc=1, device_id={"head": (me + k) % size}, device_id_type=MESH
        )
        return carry

    lax.fori_loop(1, size, greet, 0)
    data = hidden_ref[...].astype(jnp.float32)
    mean = jnp.mean(data * data, axis=-1, keepdims=True)
    normed = (data * lax.rsqrt(mean + 1e-06) * gain_ref[...]).astype(jnp.bfloat16)
    for j in range(n_chunks):
        x[j, mine] = normed[:, j * chunk : (j + 1) * chunk]
    total[...] = jnp.zeros_like(total)
    cosine = cos_half_ref[...]
    sine = sin_half_ref[...]
    cos_ref[...] = jnp.concatenate([cosine, cosine], axis=1)
    sin_ref[...] = jnp.concatenate([-sine, sine], axis=1)
    pl.semaphore_wait(barrier, size - 1)

    def x_block(j, owner_device):
        return x.at[j, pl.ds(pl.multiple_of(owner_device * own_rows, own_rows), own_rows)]

    def x_up(j, owner):
        block = x_block(j, owner * 2 + core)
        return remote(block, block, x_up_sem.at[owner, j], x_recv.at[owner, j], me + 2)

    def x_down(j, owner):
        block = x_block(j, owner * 2 + core)
        return remote(block, block, x_down_sem.at[owner, j], x_recv.at[owner, j], me - 2)

    def x_pair(j, owner):
        block = x_block(j, owner * 2 + core)
        return remote(block, block, x_pair_sem.at[0, owner, j], x_pair_sem.at[1, owner, j], partner)

    def send_x(j, carry):
        @pl.when(chip < chips - 1)
        def _():
            x_up(j, chip).start()

        @pl.when(chip > 0)
        def _():
            x_down(j, chip).start()

        x_pair(j, chip).start()
        return carry

    def gather_step(t, carry):
        s = 1 + t // n_chunks
        j = t % n_chunks

        @pl.when(chip - s >= 0)
        def _():
            x_up(j, chip - s).wait_recv()

            @pl.when(chip < chips - 1)
            def _():
                x_up(j, chip - s).start()

            x_pair(j, chip - s).start()

        @pl.when(chip + s <= chips - 1)
        def _():
            x_down(j, chip + s).wait_recv()

            @pl.when(chip > 0)
            def _():
                x_down(j, chip + s).start()

            x_pair(j, chip + s).start()

        done = t - (chips - 2) * n_chunks - 1

        @pl.when(done >= 0)
        def _():
            multiply(done)

        return carry

    def multiply(j):
        for owner in range(chips):
            x_pair(j, owner).wait_recv()
        load_weight(j).wait()
        total[...] += jnp.dot(x[j], weight[j], preferred_element_type=jnp.float32)

    lax.fori_loop(0, n_chunks, send_x, 0)
    lax.fori_loop(0, (chips - 1) * n_chunks, gather_step, 0)
    multiply(n_chunks - 1)

    def q_up(p):
        return remote(query.at[p], query.at[p], q_up_sem.at[p], q_recv.at[p], me + 2)

    def q_down(p):
        return remote(query.at[p], query.at[p], q_down_sem.at[p], q_recv.at[p], me - 2)

    def q_pair(p):
        return remote(query.at[p], query.at[p], q_pair_sem.at[0, p], q_pair_sem.at[1, p], partner)

    def fresh_copy(target):
        rows = pl.ds(pl.multiple_of(target * own_rows, own_rows), own_rows)
        source = me - first_kv
        return remote(
            pairs.at[:, rows], fresh_in.at[source], fresh_send.at[target], fresh_recv.at[source], target
        )

    def fresh_wait(source):
        return remote(
            pairs.at[:, pl.ds(0, own_rows)],
            fresh_in.at[source],
            fresh_send.at[0],
            fresh_recv.at[source],
            partner,
        ).wait_recv()

    def send_own(i):
        p = me * groups + i

        @pl.when(p < n_pairs)
        def _():
            @pl.when(chip < chips - 1)
            def _():
                q_up(p).start()

            @pl.when(chip > 0)
            def _():
                q_down(p).start()

            q_pair(p).start()

    def prepare(i, carry):
        piece = pl.ds(pl.multiple_of(i * width, width), width)
        raw = (total[:, piece] + bias_ref[:, piece].astype(jnp.float32)).astype(jnp.bfloat16)
        pairs[i] = raw

        @pl.when(me * groups + i < n_pairs)
        def _():
            for h in range(2):
                values = raw[:, h * HEAD_WIDTH : (h + 1) * HEAD_WIDTH].astype(jnp.float32)
                turned = pltpu.roll(values, HEAD_WIDTH // 2, 1)
                query[me * groups + i, h * tokens : (h + 1) * tokens] = (
                    values * cos_ref[...] + turned * sin_ref[...]
                ).astype(jnp.bfloat16)

        @pl.when((i == 0) | (chip != 1))
        def _():
            send_own(i)

        return carry

    lax.fori_loop(0, groups, prepare, 0)

    @pl.when(me >= first_kv)
    def _():
        for k in range(1, size):
            fresh_copy((me + k) % size).start()
        fresh_in[me - first_kv] = pairs[:, mine]

    load_key().wait()
    load_value().wait()

    def wait_fresh():
        for source in range(size - first_kv):
            @pl.when(me != first_kv + source)
            def _():
                fresh_wait(source)

        for k in range(n_pairs // 4):
            place = n_pairs + k
            block = fresh_in[place // groups - first_kv, place % groups].astype(jnp.float32)
            for h in range(2):
                values = block[:, h * HEAD_WIDTH : (h + 1) * HEAD_WIDTH]
                turned = pltpu.roll(values, HEAD_WIDTH // 2, 1)
                head = 2 * k + h
                new_key_ref[:, head * HEAD_WIDTH : (head + 1) * HEAD_WIDTH] = (
                    values * cos_ref[mine] + turned * sin_ref[mine]
                ).astype(jnp.bfloat16)
            place = n_pairs + n_pairs // 4 + k
            new_value_ref[:, k * width : (k + 1) * width] = fresh_in[
                place // groups - first_kv, place % groups
            ]

    def sums_pair(p):
        return remote(
            sums.at[p], pair_in.at[p], sums_pair_sem.at[0, p], sums_pair_sem.at[1, p], partner
        )

    def sums_up(src, p):
        return remote(src.at[p], up_in.at[p], sums_up_sem.at[0, p], sums_up_sem.at[1, p], me + 2)

    def sums_down(src, p):
        return remote(
            src.at[p], down_in.at[p], sums_down_sem.at[0, p], sums_down_sem.at[1, p], me - 2
        )

    def compute(p):
        head = pl.ds(pl.multiple_of((p // 2) * HEAD_WIDTH, HEAD_WIDTH), HEAD_WIDTH)
        sums[p] = attend_pair(
            key_cache[:, head],
            value_cache[:, head],
            new_key_ref[:, head],
            new_value_ref[:, head],
            query[p],
            info_ref[0],
            me * own_rows,
            tokens,
        )

        @pl.when((p // 2) % 2 != core)
        def _():
            sums_pair(p).start()

    def unit(k):
        after_two = (k + 5) // 8
        after_three = (k + 4) // 8
        after_six = (k + 1) // 8
        owner = 2 - after_two - after_three + after_six
        owner = owner + (2 - 2 * owner) * ((chips - 1 - chip) // (chips - 1))
        return owner, k - 3 * after_two - after_three - 2 * after_six

    def receive(k):
        owner, i = unit(k)
        receive_from(owner, i)

    def receive_from(owner, i):
        p = (owner * 2 + core) * groups + i

        @pl.when((p < n_pairs) & (owner < chip))
        def _():
            q_up(p).wait_recv()

            @pl.when(chip < chips - 1)
            def _():
                q_up(p).start()

            q_pair(p).start()

        @pl.when((p < n_pairs) & (owner > chip))
        def _():
            q_down(p).wait_recv()

            @pl.when(chip > 0)
            def _():
                q_down(p).start()

            q_pair(p).start()

    def attend_unit(k):
        owner, i = unit(k)

        def each(c, carry):
            p = (owner * 2 + c) * groups + i

            @pl.when(p < n_pairs)
            def _():
                @pl.when(c != core)
                def _():
                    q_pair(p).wait_recv()

                compute(p)

            return carry

        lax.fori_loop(0, 2, each, 0)

    def reduce(k, stage):
        owner, i = unit(k)

        def each(c, carry):
            p = (owner * 2 + c) * groups + i
            target = p // 4
            held = (p < n_pairs) & ((p // 2) % 2 == core)

            if stage == 0:

                @pl.when(held)
                def _():
                    sums_pair(p).wait_recv()
                    sums[p] = join_sums(sums[p], pair_in[p]).astype(jnp.bfloat16)

                    @pl.when((chip == 0) & (target > 0))
                    def _():
                        sums_up(sums, p).start()

                    @pl.when((chip == chips - 1) & (target < chips - 1))
                    def _():
                        sums_down(sums, p).start()
            else:

                @pl.when(held & (chip == stage) & (chip < target))
                def _():
                    sums_up(up_in, p).wait_recv()
                    up_in[p] = join_sums(up_in[p], sums[p]).astype(jnp.bfloat16)
                    sums_up(up_in, p).start()

                @pl.when(held & (chips - 1 - chip == stage) & (chip > target))
                def _():
                    sums_down(down_in, p).wait_recv()
                    down_in[p] = join_sums(down_in[p], sums[p]).astype(jnp.bfloat16)
                    sums_down(down_in, p).start()

            return carry

        lax.fori_loop(0, 2, each, 0)

    units = chips * groups - groups

    def attend_step(t, carry):
        @pl.when((chip == 1) & (t < groups))
        def _():
            receive_from(0, t)
            receive_from(2, t)

            @pl.when(t >= groups - 1)
            def _():
                send_own(1)
                send_own(2)

        @pl.when((chip == 2) & (t + ATTEND_LAG < units))
        def _():
            receive(t + ATTEND_LAG)

        @pl.when((t < units) & ((chip == 0) | (chip == chips - 1)))
        def _():
            receive(t)

        for stage in (2, 1, 0):
            k = t - 1 - stage * REDUCE_LAG

            @pl.when((k >= 0) & (k < units))
            def _():
                reduce(k, stage)

        @pl.when(t == 0)
        def _():
            wait_fresh()

        @pl.when(t < units)
        def _():
            attend_unit(t)

        return carry

    lax.fori_loop(0, units + 1 + 2 * REDUCE_LAG, attend_step, 0)

    for k in range(2):
        p = me * 2 + k

        @pl.when(chip > 0)
        def _():
            sums_up(up_in, p).wait_recv()
            sums[p] = join_sums(sums[p], up_in[p]).astype(jnp.bfloat16)

        @pl.when(chip < chips - 1)
        def _():
            sums_down(down_in, p).wait_recv()

        @pl.when(chip == chips - 1)
        def _():
            down_in[p] = sums[p]

        block = down_in[p]

        @pl.when(chip < chips - 1)
        def _():
            down_in[p] = join_sums(sums[p], block).astype(jnp.bfloat16)

        mixed = down_in[p].astype(jnp.float32)
        bottom = mixed[HEAD_WIDTH : HEAD_WIDTH + 1] + mixed[HEAD_WIDTH + 1 : HEAD_WIDTH + 2]
        result = jnp.transpose(mixed[:HEAD_WIDTH] / bottom).astype(jnp.bfloat16)
        for h in range(2):
            head = 2 * k + h
            attn_ref[:, head * HEAD_WIDTH : (head + 1) * HEAD_WIDTH] = result[
                h * tokens : (h + 1) * tokens
            ]

    def finish_x(n, carry):
        owner = n // n_chunks
        j = n % n_chunks
        x_pair(j, owner).wait_send()

        @pl.when((chip < chips - 1) & (owner <= chip))
        def _():
            x_up(j, owner).wait_send()

        @pl.when((chip > 0) & (owner >= chip))
        def _():
            x_down(j, owner).wait_send()

        return carry

    lax.fori_loop(0, chips * n_chunks, finish_x, 0)

    def finish_pairs(p, carry):
        device = p // groups
        owner = device // 2

        @pl.when(device % 2 == core)
        def _():
            q_pair(p).wait_send()

            @pl.when((chip < chips - 1) & (owner <= chip))
            def _():
                q_up(p).wait_send()

            @pl.when((chip > 0) & (owner >= chip))
            def _():
                q_down(p).wait_send()

        target = p // 4

        @pl.when((p // 2) % 2 != core)
        def _():
            sums_pair(p).wait_send()

        @pl.when((p // 2) % 2 == core)
        def _():
            @pl.when(chip < target)
            def _():
                sums_up(sums, p).wait_send()

            @pl.when(chip > target)
            def _():
                sums_down(sums, p).wait_send()

        return carry

    lax.fori_loop(0, n_pairs, finish_pairs, 0)

    @pl.when(me >= first_kv)
    def _():
        for k in range(1, size):
            fresh_copy((me + k) % size).wait_send()


def head(info, hidden, gain, bias, cosine, sine, weight, key_cache, value_cache, collective_id):
    own_rows, model = hidden.shape
    tokens = cosine.shape[0]
    columns = weight.shape[1]
    length, cached = key_cache.shape
    chunk = HEAD_CHUNK
    n_chunks = model // chunk
    n_pairs = QUERY_HEADS // 2
    groups = 3
    width = 2 * HEAD_WIDTH
    bf16, f32 = jnp.bfloat16, jnp.float32
    vmem = pl.BlockSpec(memory_space=pltpu.VMEM)
    smem = pl.BlockSpec(memory_space=pltpu.SMEM)
    hbm = pl.BlockSpec(memory_space=pl.ANY)
    dma = pltpu.SemaphoreType.DMA
    block = pltpu.VMEM((n_pairs, HEAD_WIDTH + TAIL, 2 * tokens), bf16)
    return pl.pallas_call(
        functools.partial(head_kernel, n_chunks),
        out_shape=[
            jax.ShapeDtypeStruct((tokens, 4 * HEAD_WIDTH), bf16),
            jax.ShapeDtypeStruct((own_rows, cached), bf16),
            jax.ShapeDtypeStruct((own_rows, cached), bf16),
        ],
        in_specs=[smem, vmem, vmem, vmem, vmem, vmem, hbm, hbm, hbm],
        out_specs=[vmem, vmem, vmem],
        scratch_shapes=[
            pltpu.VMEM((n_chunks, chunk, columns), bf16),
            pltpu.VMEM((length, cached), bf16),
            pltpu.VMEM((length, cached), bf16),
            pltpu.VMEM((tokens, HEAD_WIDTH), f32),
            pltpu.VMEM((tokens, HEAD_WIDTH), f32),
            pltpu.VMEM((n_chunks, tokens, chunk), bf16),
            pltpu.VMEM((tokens, columns), f32),
            pltpu.VMEM((groups, tokens, width), bf16),
            pltpu.VMEM((n_pairs, 2 * tokens, HEAD_WIDTH), bf16),
            pltpu.VMEM((3, groups, own_rows, width), bf16),
            block,
            block,
            block,
            block,
            dma((n_chunks + 2,)),
            dma((4, n_chunks)),
            dma((4, n_chunks)),
            dma((4, n_chunks)),
            dma((2, 4, n_chunks)),
            dma((n_pairs,)),
            dma((n_pairs,)),
            dma((n_pairs,)),
            dma((2, n_pairs)),
            dma((8,)),
            dma((3,)),
            dma((2, n_pairs)),
            dma((2, n_pairs)),
            dma((2, n_pairs)),
        ],
        compiler_params=pltpu.CompilerParams(
            collective_id=collective_id, has_side_effects=True, vmem_limit_bytes=62 << 20
        ),
        name="head%d" % collective_id,
    )(
        info,
        hidden,
        gain.reshape(1, model),
        bias.astype(f32).reshape(1, columns),
        cosine,
        sine,
        weight,
        key_cache,
        value_cache,
    )


def pass_on_kernel(*refs):
    count = len(refs) // 2
    for source, target in zip(refs[:count], refs[count:]):
        target[...] = source[...]


def pass_on(*arrays):
    vmem = pl.BlockSpec(memory_space=pltpu.VMEM)
    return pl.pallas_call(
        pass_on_kernel,
        out_shape=[jax.ShapeDtypeStruct(a.shape, a.dtype) for a in arrays],
        in_specs=[vmem] * len(arrays),
        out_specs=[vmem] * len(arrays),
        name="pass_on",
    )(*arrays)


def on_device(
    hidden,
    cached_len,
    attn_gain,
    query_key_value_weight,
    b_qkv,
    key_cache,
    value_cache,
    w_out,
    ffn_gain,
    w_gate,
    w_up,
    w_down,
):
    size = lax.axis_size("head")
    index_here = lax.axis_index("head")
    own_rows = hidden[0]
    fresh, model = own_rows.shape
    tokens = fresh * size
    heads_here = QUERY_HEADS // size
    row_start = index_here * fresh
    cache_length = key_cache.shape[1]
    key_start = QUERY_HEADS * HEAD_WIDTH
    coarse = max(fresh // 16, 1)

    positions = cached_len[0] + jnp.arange(tokens, dtype=jnp.int32)

    if size == 8 and fresh == 32:
        cosine, sine = rope_halves(positions)
        info = jnp.reshape(cached_len[0] - index_here * cache_length, (1,)).astype(jnp.int32)
        attn, new_keys, new_values = head(
            info,
            own_rows,
            attn_gain,
            b_qkv,
            cosine,
            sine,
            query_key_value_weight,
            key_cache[0],
            value_cache[0],
            2,
        )
        result = tail(attn, own_rows, ffn_gain, w_out, w_gate, w_up, w_down, 7)
        result, new_keys, new_values = pass_on(result, new_keys, new_values)
    else:
        cosine, sine = rope_tables(positions)
        own_cosine = lax.dynamic_slice_in_dim(cosine, row_start, fresh, 0)[:, None, :]
        own_sine = lax.dynamic_slice_in_dim(sine, row_start, fresh, 0)[:, None, :]
        normed = gather(rms_norm(own_rows, attn_gain), size, coarse, 0).reshape(tokens, model)
        qkv_part = (
            jnp.dot(normed, query_key_value_weight, preferred_element_type=jnp.float32)
            + b_qkv.astype(jnp.float32)
        ).astype(jnp.bfloat16)
        qkv = jnp.transpose(gather(qkv_part, size, 4, 1), (1, 0, 2)).reshape(tokens, -1)
        own = lax.dynamic_slice(
            qkv, (row_start, key_start), (fresh, 2 * KEY_VALUE_HEADS * HEAD_WIDTH)
        )
        key_data = own[:, : KEY_VALUE_HEADS * HEAD_WIDTH].astype(jnp.float32)
        key_data = key_data.reshape(fresh, KEY_VALUE_HEADS, HEAD_WIDTH)
        turned = jnp.roll(key_data, HEAD_WIDTH // 2, axis=-1)
        new_keys = (key_data * own_cosine + turned * own_sine).astype(jnp.bfloat16)
        new_keys = new_keys.reshape(fresh, KEY_VALUE_HEADS * HEAD_WIDTH)
        new_values = own[:, KEY_VALUE_HEADS * HEAD_WIDTH :]

        info = jnp.stack([cached_len[0] - index_here * cache_length, row_start]).astype(jnp.int32)
        sums = attend(info, qkv, key_cache[0], value_cache[0], new_keys, new_values, cosine, sine)
        sums = sums.reshape(size, heads_here, HEAD_WIDTH + TAIL, tokens)
        mixed = scatter(sums, size, join_sums, 3)
        total = mixed[:, HEAD_WIDTH : HEAD_WIDTH + 1] + mixed[:, HEAD_WIDTH + 1 : HEAD_WIDTH + 2]
        attn = (mixed[:, :HEAD_WIDTH] / total).astype(jnp.bfloat16)
        attn = jnp.transpose(attn, (2, 0, 1)).reshape(tokens, heads_here * HEAD_WIDTH)
        projected = jnp.dot(attn, w_out, preferred_element_type=jnp.float32).astype(jnp.bfloat16)
        blocks = (size, coarse, fresh // coarse, model)
        projected = scatter(projected.reshape(blocks), size, add_blocks, 4).reshape(fresh, model)
        middle = (own_rows.astype(jnp.float32) + projected).astype(jnp.bfloat16)
        normed_two = gather(rms_norm(middle, ffn_gain), size, coarse, 5).reshape(tokens, model)
        ffn_part = feed(normed_two, w_gate, w_up, w_down)
        ffn_sum = scatter(ffn_part.reshape(blocks), size, add_blocks, 6).reshape(fresh, model)
        result = (middle.astype(jnp.float32) + ffn_sum).astype(jnp.bfloat16)
    return (result[None], new_keys[None], new_values[None])


def solution(mesh):
    in_specs = (
        P("req", "head", None),
        P("req"),
        P(),
        P(None, "head"),
        P("head"),
        P("req", "head", None),
        P("req", "head", None),
        P("head", None),
        P(),
        P(None, "head"),
        P(None, "head"),
        P("head", None),
    )
    out_specs = (P("req", "head", None), P("req", "head", None), P("req", "head", None))
    return jax.shard_map(
        on_device, mesh=mesh, in_specs=in_specs, out_specs=out_specs, check_vma=False
    )
```

```python
import functools
import math

import jax
import jax.numpy as jnp
from jax import lax
from jax.experimental import pallas as pl
from jax.experimental.pallas import tpu as pltpu
from jax.sharding import PartitionSpec as P

QUERY_HEADS = 32
KEY_VALUE_HEADS = 8
HEAD_WIDTH = 128
GROUP = QUERY_HEADS // KEY_VALUE_HEADS
SCALE = 1.0 / math.sqrt(HEAD_WIDTH)
TAIL = 16
FEED_TILE = 432
FEED_COLUMNS = 1024
TAIL_CHUNK = 512
FEED_GROUP = 1
HEAD_CHUNK = 1024
ATTEND_LAG = 1
REDUCE_LAG = 4
PAIR_LAG = 1
HOP_LAG = 2

rope_base = 1000000.0
MESH = pl.DeviceIdType.MESH


def rms_norm(values, gain):
    data = values.astype(jnp.float32)
    spread = jnp.mean(data * data, axis=-1, keepdims=True)
    return (data * lax.rsqrt(spread + 1e-06) * gain).astype(jnp.bfloat16)


def rope_halves(positions):
    half_dim = HEAD_WIDTH // 2
    inverse = rope_base ** (-(jnp.arange(half_dim, dtype=jnp.float32) * 2.0 / HEAD_WIDTH))
    angles = positions.astype(jnp.float32)[:, None] * inverse[None, :]
    return jnp.cos(angles), jnp.sin(angles)


def rope_tables(positions):
    cosine, sine = rope_halves(positions)
    return (
        jnp.concatenate([cosine, cosine], axis=-1),
        jnp.concatenate([-sine, sine], axis=-1),
    )


def chain_barrier(chips, me, chip, partner):
    barrier = pltpu.get_barrier_semaphore()
    pl.semaphore_signal(barrier, inc=1, device_id={"head": partner}, device_id_type=MESH)

    @pl.when(chip > 0)
    def _():
        pl.semaphore_signal(barrier, inc=1, device_id={"head": me - 2}, device_id_type=MESH)

    @pl.when(chip < chips - 1)
    def _():
        pl.semaphore_signal(barrier, inc=1, device_id={"head": me + 2}, device_id_type=MESH)

    below = (chip + chips - 1) // chips
    above = (2 * chips - 2 - chip) // chips
    pl.semaphore_wait(barrier, 1 + below + above)


def gather_kernel(
    chips, pieces, x_ref, out_ref, own_sem, up_send, down_send, chip_recv, pair_send, pair_recv
):
    me = lax.axis_index("head")
    chip = me // 2
    core = me % 2
    partner = chip * 2 + (1 - core)
    chain_barrier(chips, me, chip, partner)

    def to_up(src, owner, c):
        return pltpu.make_async_remote_copy(
            src_ref=src,
            dst_ref=out_ref.at[owner * 2 + core, c],
            send_sem=up_send.at[owner, c],
            recv_sem=chip_recv.at[owner, c],
            device_id={"head": me + 2},
            device_id_type=MESH,
        )

    def to_down(src, owner, c):
        return pltpu.make_async_remote_copy(
            src_ref=src,
            dst_ref=out_ref.at[owner * 2 + core, c],
            send_sem=down_send.at[owner, c],
            recv_sem=chip_recv.at[owner, c],
            device_id={"head": me - 2},
            device_id_type=MESH,
        )

    def to_partner(src, owner, c):
        return pltpu.make_async_remote_copy(
            src_ref=src,
            dst_ref=out_ref.at[owner * 2 + core, c],
            send_sem=pair_send.at[owner, c],
            recv_sem=pair_recv.at[owner, c],
            device_id={"head": partner},
            device_id_type=MESH,
        )

    def begin(c, carry):
        @pl.when(chip < chips - 1)
        def _():
            to_up(x_ref.at[c], chip, c).start()

        @pl.when(chip > 0)
        def _():
            to_down(x_ref.at[c], chip, c).start()

        to_partner(x_ref.at[c], chip, c).start()
        return carry

    lax.fori_loop(0, pieces, begin, 0)
    own = pltpu.make_async_copy(x_ref, out_ref.at[me], own_sem)
    own.start()

    def step(t, carry):
        s = 1 + t // pieces
        c = t % pieces

        @pl.when(chip - s >= 0)
        def _():
            owner = chip - s
            held = out_ref.at[owner * 2 + core, c]
            to_up(held, owner, c).wait_recv()

            @pl.when(chip < chips - 1)
            def _():
                to_up(held, owner, c).start()

            to_partner(held, owner, c).start()

        @pl.when(chip + s <= chips - 1)
        def _():
            owner = chip + s
            held = out_ref.at[owner * 2 + core, c]
            to_down(held, owner, c).wait_recv()

            @pl.when(chip > 0)
            def _():
                to_down(held, owner, c).start()

            to_partner(held, owner, c).start()

        return carry

    lax.fori_loop(0, (chips - 1) * pieces, step, 0)
    own.wait()

    def finish(t, carry):
        owner = t // pieces
        c = t % pieces
        to_partner(x_ref.at[c], owner, c).wait()

        @pl.when((chip < chips - 1) & (owner <= chip))
        def _():
            to_up(x_ref.at[c], owner, c).wait_send()

        @pl.when((chip > 0) & (owner >= chip))
        def _():
            to_down(x_ref.at[c], owner, c).wait_send()

        return carry

    lax.fori_loop(0, chips * pieces, finish, 0)


def gather(x, size, pieces, collective_id):
    chips = size // 2
    rows, width = x.shape
    x = x.reshape(pieces, rows // pieces, width)
    return pl.pallas_call(
        functools.partial(gather_kernel, chips, pieces),
        out_shape=jax.ShapeDtypeStruct((size,) + x.shape, x.dtype),
        in_specs=[pl.BlockSpec(memory_space=pltpu.VMEM)],
        out_specs=pl.BlockSpec(memory_space=pltpu.VMEM),
        scratch_shapes=[pltpu.SemaphoreType.DMA(())]
        + [pltpu.SemaphoreType.DMA((chips, pieces))] * 5,
        compiler_params=pltpu.CompilerParams(
            collective_id=collective_id, has_side_effects=True, vmem_limit_bytes=16 << 20
        ),
        name="gather%d" % collective_id,
    )(x).reshape(size, rows, width)


def add_blocks(a, b):
    return a.astype(jnp.float32) + b.astype(jnp.float32)


def pack_sums(sums, total, top):
    def narrow(v):
        return v.astype(jnp.bfloat16).astype(jnp.float32)

    total_high = narrow(total)
    top_high = narrow(top)
    top_middle = narrow(top - top_high)
    rows = [total_high, total - total_high, top_high, top_middle, top - top_high - top_middle]
    index = lax.broadcasted_iota(jnp.int32, (TAIL, sums.shape[1]), 0)
    tail = jnp.zeros((TAIL, sums.shape[1]), jnp.float32)
    for place, row in enumerate(rows):
        tail = jnp.where(index == place, row, tail)
    return jnp.concatenate([sums, tail], axis=0)


def join_sums(a, b):
    def unpack(block):
        block = block.astype(jnp.float32)
        tail = block[HEAD_WIDTH:]
        return block[:HEAD_WIDTH], tail[0:1] + tail[1:2], (tail[2:3] + tail[3:4]) + tail[4:5]

    sums_a, total_a, top_a = unpack(a)
    sums_b, total_b, top_b = unpack(b)
    top = jnp.maximum(top_a, top_b)
    scale_a = jnp.exp((top_a - top) * SCALE)
    scale_b = jnp.exp((top_b - top) * SCALE)
    return pack_sums(
        sums_a * scale_a + sums_b * scale_b, total_a * scale_a + total_b * scale_b, top
    )


def scatter_kernel(
    join,
    chips,
    pieces,
    x_ref,
    out_ref,
    pair,
    up,
    down,
    pair_send,
    pair_recv,
    up_send,
    up_recv,
    down_send,
    down_recv,
):
    me = lax.axis_index("head")
    chip = me // 2
    core = me % 2
    partner = chip * 2 + (1 - core)
    half = chip // (chips // 2)
    chain_barrier(chips, me, chip, partner)

    def to_partner(j, c):
        return pltpu.make_async_remote_copy(
            src_ref=x_ref.at[2 * j + (1 - core), c],
            dst_ref=pair.at[j, c],
            send_sem=pair_send.at[j, c],
            recv_sem=pair_recv.at[j, c],
            device_id={"head": partner},
            device_id_type=MESH,
        )

    def to_up(src, j, c):
        return pltpu.make_async_remote_copy(
            src_ref=src.at[j, c],
            dst_ref=up.at[j, c],
            send_sem=up_send.at[j, c],
            recv_sem=up_recv.at[j, c],
            device_id={"head": me + 2},
            device_id_type=MESH,
        )

    def to_down(src, j, c):
        return pltpu.make_async_remote_copy(
            src_ref=src.at[j, c],
            dst_ref=down.at[j, c],
            send_sem=down_send.at[j, c],
            recv_sem=down_recv.at[j, c],
            device_id={"head": me - 2},
            device_id_type=MESH,
        )

    def order(k):
        return (1 - half) * (chips - 1 - k) + half * k

    def first(t, carry):
        to_partner(order(t // pieces), t % pieces).start()
        return carry

    lax.fori_loop(0, chips * pieces, first, 0)

    def second(t, carry):
        j = order(t // pieces)
        c = t % pieces
        to_partner(j, c).wait_recv()
        pair[j, c] = join(pair[j, c], x_ref[2 * j + core, c]).astype(pair.dtype)

        @pl.when((chip == 0) & (j > 0))
        def _():
            to_up(pair, j, c).start()

        @pl.when((chip == chips - 1) & (j < chips - 1))
        def _():
            to_down(pair, j, c).start()

        return carry

    lax.fori_loop(0, chips * pieces, second, 0)

    def move_up(j, c):
        @pl.when((chip > 0) & (j > chip))
        def _():
            to_up(up, j, c).wait_recv()
            up[j, c] = join(up[j, c], pair[j, c]).astype(up.dtype)
            to_up(up, j, c).start()

    def move_down(j, c):
        @pl.when((chip < chips - 1) & (j < chip))
        def _():
            to_down(down, j, c).wait_recv()
            down[j, c] = join(down[j, c], pair[j, c]).astype(down.dtype)
            to_down(down, j, c).start()

    def third(t, carry):
        s = t // pieces
        c = t % pieces

        @pl.when(half == 0)
        def _():
            move_up(chips - 1 - s, c)

        move_down(s, c)

        @pl.when(half == 1)
        def _():
            move_up(chips - 1 - s, c)

        return carry

    lax.fori_loop(0, (chips - 1) * pieces, third, 0)

    def total(c, carry):
        out_ref[c] = pair[chip, c].astype(jnp.float32)

        @pl.when(chip > 0)
        def _():
            to_up(up, chip, c).wait_recv()
            out_ref[c] = join(out_ref[c], up[chip, c])

        @pl.when(chip < chips - 1)
        def _():
            to_down(down, chip, c).wait_recv()
            out_ref[c] = join(out_ref[c], down[chip, c])

        return carry

    lax.fori_loop(0, pieces, total, 0)

    def finish(t, carry):
        j = t // pieces
        c = t % pieces
        to_partner(j, c).wait_send()

        @pl.when(j > chip)
        def _():
            to_up(pair, j, c).wait_send()

        @pl.when(j < chip)
        def _():
            to_down(pair, j, c).wait_send()

        return carry

    lax.fori_loop(0, chips * pieces, finish, 0)


def scatter(x, size, join, collective_id):
    chips = size // 2
    shape = x.shape[1:]
    pieces = shape[0]
    return pl.pallas_call(
        functools.partial(scatter_kernel, join, chips, pieces),
        out_shape=jax.ShapeDtypeStruct(shape, jnp.float32),
        in_specs=[pl.BlockSpec(memory_space=pltpu.VMEM)],
        out_specs=pl.BlockSpec(memory_space=pltpu.VMEM),
        scratch_shapes=[pltpu.VMEM((chips,) + shape, x.dtype)] * 3
        + [pltpu.SemaphoreType.DMA((chips, pieces))] * 6,
        compiler_params=pltpu.CompilerParams(
            collective_id=collective_id, has_side_effects=True, vmem_limit_bytes=24 << 20
        ),
        name="scatter%d" % collective_id,
    )(x)


def attend_kernel(info_ref, q_ref, kc_ref, vc_ref, kn_ref, vn_ref, cos_ref, sin_ref, sum_ref):
    tokens = q_ref.shape[0]
    length = kc_ref.shape[0]
    fresh = kn_ref.shape[0]
    width = GROUP * tokens
    cosine = cos_ref[...]
    sine = sin_ref[...]
    parts = []
    for j in range(GROUP):
        data = q_ref[:, j * HEAD_WIDTH : (j + 1) * HEAD_WIDTH].astype(jnp.float32)
        turned = pltpu.roll(data, HEAD_WIDTH // 2, 1)
        parts.append((data * cosine + turned * sine).astype(jnp.bfloat16))
    query = jnp.concatenate(parts, axis=0)
    last = (((1,), (1,)), ((), ()))
    first = (((0,), (0,)), ((), ()))
    old = lax.dot_general(kc_ref[...], query, last, preferred_element_type=jnp.float32)
    new = lax.dot_general(kn_ref[...], query, last, preferred_element_type=jnp.float32)
    old_ids = lax.broadcasted_iota(jnp.int32, (length, 1), 0)
    old = jnp.where(old_ids < info_ref[0], old, -1e30)
    new_ids = lax.broadcasted_iota(jnp.int32, (fresh, width), 0) + info_ref[1]
    token_ids = lax.broadcasted_iota(jnp.int32, (fresh, width), 1) % tokens
    new = jnp.where(new_ids <= token_ids, new, -1e30)
    top = jnp.maximum(jnp.max(old, axis=0, keepdims=True), jnp.max(new, axis=0, keepdims=True))
    top = jnp.maximum(top, -1e29)
    old = jnp.exp((old - top) * SCALE)
    new = jnp.exp((new - top) * SCALE)
    total = jnp.sum(old, axis=0, keepdims=True) + jnp.sum(new, axis=0, keepdims=True)
    sums = lax.dot_general(
        vc_ref[...], old.astype(jnp.bfloat16), first, preferred_element_type=jnp.float32
    ) + lax.dot_general(
        vn_ref[...], new.astype(jnp.bfloat16), first, preferred_element_type=jnp.float32
    )
    packed = pack_sums(sums, total, top).astype(jnp.bfloat16)
    for j in range(GROUP):
        sum_ref[0, j] = packed[:, j * tokens : (j + 1) * tokens]


def attend(info, qkv, key_cache, value_cache, new_keys, new_values, cosine, sine):
    tokens = qkv.shape[0]
    length = key_cache.shape[0]
    fresh = new_keys.shape[0]

    def head_block(rows):
        return pl.BlockSpec((rows, HEAD_WIDTH), lambda g, info: (0, g))

    def whole_block(shape):
        return pl.BlockSpec(shape, lambda g, info: (0, 0))

    return pl.pallas_call(
        attend_kernel,
        grid_spec=pltpu.PrefetchScalarGridSpec(
            num_scalar_prefetch=1,
            grid=(KEY_VALUE_HEADS,),
            in_specs=[
                pl.BlockSpec((tokens, GROUP * HEAD_WIDTH), lambda g, info: (0, g)),
                head_block(length),
                head_block(length),
                head_block(fresh),
                head_block(fresh),
                whole_block((tokens, HEAD_WIDTH)),
                whole_block((tokens, HEAD_WIDTH)),
            ],
            out_specs=pl.BlockSpec(
                (1, GROUP, HEAD_WIDTH + TAIL, tokens), lambda g, info: (g, 0, 0, 0)
            ),
        ),
        out_shape=jax.ShapeDtypeStruct(
            (KEY_VALUE_HEADS, GROUP, HEAD_WIDTH + TAIL, tokens), jnp.bfloat16
        ),
        compiler_params=pltpu.CompilerParams(
            dimension_semantics=("arbitrary",), vmem_limit_bytes=32 << 20
        ),
        name="attend",
    )(info, qkv, key_cache, value_cache, new_keys, new_values, cosine, sine)


def feed_kernel(steps, x_ref, gate_ref, up_ref, down_ref, out_ref, turned, active):
    step = pl.program_id(0)
    tile = gate_ref.shape[0]

    @pl.when(step == 0)
    def _():
        turned[...] = jnp.transpose(x_ref[...])

    @pl.when(step < steps)
    def _():
        x = turned[...]
        gate = jnp.dot(gate_ref[...], x, preferred_element_type=jnp.float32)
        upward = jnp.dot(up_ref[...], x, preferred_element_type=jnp.float32)
        active[pl.ds(pl.multiple_of(step * tile, tile), tile), :] = (
            gate / (1.0 + jnp.exp(-gate)) * upward
        ).astype(jnp.bfloat16)

    @pl.when(step >= steps)
    def _():
        out_ref[...] = lax.dot_general(
            active[...],
            down_ref[...],
            (((0,), (0,)), ((), ())),
            preferred_element_type=jnp.float32,
        ).astype(jnp.bfloat16)


def feed(x, w_gate, w_up, w_down):
    tokens, model = x.shape
    units = w_down.shape[0]
    steps = units // FEED_TILE
    tile = units // steps
    weight = pl.BlockSpec((tile, model), lambda i: (jnp.minimum(i, steps - 1), 0))
    return pl.pallas_call(
        functools.partial(feed_kernel, steps),
        grid=(steps + model // FEED_COLUMNS,),
        in_specs=[
            pl.BlockSpec((tokens, model), lambda i: (0, 0)),
            weight,
            weight,
            pl.BlockSpec((units, FEED_COLUMNS), lambda i: (0, jnp.maximum(i - steps, 0))),
        ],
        out_specs=pl.BlockSpec((tokens, FEED_COLUMNS), lambda i: (0, jnp.maximum(i - steps, 0))),
        out_shape=jax.ShapeDtypeStruct((tokens, model), jnp.bfloat16),
        scratch_shapes=[
            pltpu.VMEM((model, tokens), jnp.bfloat16),
            pltpu.VMEM((units, tokens), jnp.bfloat16),
        ],
        compiler_params=pltpu.CompilerParams(
            dimension_semantics=("arbitrary",), vmem_limit_bytes=48 << 20
        ),
        name="feed",
    )(x, jnp.transpose(w_gate), jnp.transpose(w_up), w_down)


def tail_kernel(
    n_chunks,
    attn_ref,
    hidden_ref,
    gain_ref,
    w_out_hbm,
    gate_hbm,
    up_hbm,
    w_down_hbm,
    out_ref,
    w_out,
    gate_w,
    up_w,
    w_down,
    product,
    own,
    pair_out,
    pair_in,
    outer_out,
    outer_in,
    cross_out,
    cross_in,
    middle,
    squares,
    x,
    spread,
    gate_sum,
    up_sum,
    active,
    rows_own,
    rows_pair_out,
    rows_pair_in,
    rows_outer_out,
    rows_outer_in,
    rows_cross_out,
    rows_cross_in,
    rows_last_out,
    rows_last_in,
    weight_sem,
    pair_sem,
    outer_sem,
    cross_sem,
    near_sem,
    far_sem,
    far_out_sem,
    near_pair_sem,
    far_pair_sem,
    rows_pair_sem,
    rows_outer_sem,
    rows_cross_sem,
    rows_last_sem,
):
    me = lax.axis_index("head")
    chip = me // 2
    core = me % 2
    side = chip // 2
    partner = chip * 2 + (1 - core)
    inner = (chip == 1) | (chip == 2)
    outer = (chip == 0) | (chip == 3)
    toward = 2 - 4 * side
    near_device = me + toward
    outer_device = me - toward
    tokens = attn_ref.shape[0]
    half = tokens // 2
    part = half // 2
    own_rows = hidden_ref.shape[0]
    chunk = w_out.shape[2]
    slots = gate_w.shape[0]
    near_start = pl.multiple_of(side * half + core * part, part)
    far_start = pl.multiple_of((1 - side) * half + core * part, part)

    def columns(j):
        return pl.ds(pl.multiple_of(j * chunk, chunk), chunk)

    def group_columns(j):
        return pl.ds(pl.multiple_of((j % FEED_GROUP) * chunk, chunk), chunk)

    def group_all(j):
        return pl.ds(pl.multiple_of(j * FEED_GROUP * chunk, FEED_GROUP * chunk), FEED_GROUP * chunk)

    def load_out(j):
        return pltpu.make_async_copy(w_out_hbm.at[:, columns(j)], w_out.at[j], weight_sem.at[0, j])

    def load_gate(j):
        return pltpu.make_async_copy(
            gate_hbm.at[:, group_all(j)], gate_w.at[j % slots], weight_sem.at[1, j]
        )

    def load_up(j):
        return pltpu.make_async_copy(
            up_hbm.at[:, group_all(j)], up_w.at[j % slots], weight_sem.at[2, j]
        )

    def load_down(j):
        return pltpu.make_async_copy(
            w_down_hbm.at[:, columns(j)], w_down.at[j], weight_sem.at[3, j]
        )

    def remote(src, dst, sems, j, device):
        return pltpu.make_async_remote_copy(
            src_ref=src,
            dst_ref=dst,
            send_sem=sems.at[0, j],
            recv_sem=sems.at[1, j],
            device_id={"head": device},
            device_id_type=MESH,
        )

    def pair_copy(j):
        return remote(pair_out.at[j], pair_in.at[j], pair_sem, j, partner)

    def outer_copy(j):
        return remote(outer_out.at[j], outer_in.at[j], outer_sem, j, near_device)

    def cross_copy(j):
        return remote(cross_out.at[j], cross_in.at[j], cross_sem, j, near_device)

    def x_copy(j, start, sems, device):
        ref = x.at[j // FEED_GROUP, pl.ds(start, part), group_columns(j)]
        return remote(ref, ref, sems, j, device)

    def spread_copy(start, sems, device):
        ref = spread.at[pl.ds(start, part)]
        return remote(ref, ref, sems, n_chunks, device)

    def begin_out(j, carry):
        load_out(j).start()
        return carry

    def begin_feed(j, carry):
        load_gate(j).start()
        load_up(j).start()
        return carry

    lax.fori_loop(0, n_chunks, begin_out, 0)
    lax.fori_loop(0, slots, begin_feed, 0)
    chain_barrier(4, me, chip, partner)
    squares[...] = jnp.zeros_like(squares)
    gate_sum[...] = jnp.zeros_like(gate_sum)
    up_sum[...] = jnp.zeros_like(up_sum)

    def stage(t, lag, also=None):
        j = t - lag
        ready = (j >= 0) & (j < n_chunks)
        return ready if also is None else ready & also

    lag_outer = PAIR_LAG + HOP_LAG
    lag_cross = lag_outer + HOP_LAG
    lag_near = lag_cross + HOP_LAG
    lag_far = lag_near + HOP_LAG
    lag_feed = lag_far + PAIR_LAG

    def step(t, carry):
        @pl.when(stage(t, lag_far, outer))
        def _():
            j = t - lag_far
            x_copy(j, far_start, far_out_sem, near_device).wait_recv()
            x_copy(j, far_start, far_pair_sem, partner).start()

            @pl.when(j == n_chunks - 1)
            def _():
                spread_copy(far_start, far_out_sem, near_device).wait_recv()
                spread_copy(far_start, far_pair_sem, partner).start()

        @pl.when(stage(t, lag_near, inner))
        def _():
            j = t - lag_near
            x_copy(j, far_start, far_sem, near_device).wait_recv()
            x_copy(j, far_start, far_out_sem, outer_device).start()
            x_copy(j, far_start, far_pair_sem, partner).start()

            @pl.when(j == n_chunks - 1)
            def _():
                spread_copy(far_start, far_sem, near_device).wait_recv()
                spread_copy(far_start, far_out_sem, outer_device).start()
                spread_copy(far_start, far_pair_sem, partner).start()

        @pl.when(stage(t, lag_near, outer))
        def _():
            j = t - lag_near
            x_copy(j, near_start, near_sem, near_device).wait_recv()
            x_copy(j, near_start, near_pair_sem, partner).start()

            @pl.when(j == n_chunks - 1)
            def _():
                spread_copy(near_start, near_sem, near_device).wait_recv()
                spread_copy(near_start, near_pair_sem, partner).start()

        @pl.when(stage(t, lag_cross, inner))
        def _():
            j = t - lag_cross
            cross_copy(j).wait_recv()
            mid = (own[j, side] + cross_in[j].astype(jnp.float32)).astype(jnp.bfloat16)
            middle[j] = mid
            data = mid.astype(jnp.float32)
            square = data * data
            folded = square[:, :HEAD_WIDTH]
            for k in range(1, chunk // HEAD_WIDTH):
                folded = folded + square[:, k * HEAD_WIDTH : (k + 1) * HEAD_WIDTH]
            squares[...] += folded
            x[j // FEED_GROUP, pl.ds(near_start, part), group_columns(j)] = (
                data * gain_ref[:, columns(j)]
            ).astype(jnp.bfloat16)
            x_copy(j, near_start, near_sem, outer_device).start()
            x_copy(j, near_start, far_sem, near_device).start()
            x_copy(j, near_start, near_pair_sem, partner).start()

            @pl.when(j == n_chunks - 1)
            def _():
                mean = jnp.sum(squares[...], axis=1, keepdims=True) / (n_chunks * chunk)
                spread[pl.ds(near_start, part)] = jnp.broadcast_to(
                    lax.rsqrt(mean + 1e-06), (part, HEAD_WIDTH)
                )
                spread_copy(near_start, near_sem, outer_device).start()
                spread_copy(near_start, far_sem, near_device).start()
                spread_copy(near_start, near_pair_sem, partner).start()

        @pl.when(stage(t, lag_outer, inner))
        def _():
            j = t - lag_outer
            outer_copy(j).wait_recv()
            cross_out[j] = (own[j, 1 - side] + outer_in[j, 1 - side].astype(jnp.float32)).astype(
                jnp.bfloat16
            )
            cross_copy(j).start()
            own[j, side] += outer_in[j, side].astype(jnp.float32)

        @pl.when(stage(t, PAIR_LAG))
        def _():
            j = t - PAIR_LAG
            pair_copy(j).wait_recv()
            total = own[j] + pair_in[j].astype(jnp.float32)

            @pl.when(outer)
            def _():
                outer_out[j] = total.astype(jnp.bfloat16)
                outer_copy(j).start()

            @pl.when(inner)
            def _():
                own[j] = total

        @pl.when(t < n_chunks)
        def _():
            load_out(t).wait()
            product[...] = jnp.dot(attn_ref[...], w_out[t], preferred_element_type=jnp.float32)
            mine = pl.ds(pl.multiple_of(me * own_rows, own_rows), own_rows)
            product[mine] += hidden_ref[:, columns(t)].astype(jnp.float32)
            for f in range(2):
                keep = pl.ds(pl.multiple_of(f * half + core * part, part), part)
                give = pl.ds(pl.multiple_of(f * half + (1 - core) * part, part), part)
                own[t, f] = product[keep]
                pair_out[t, f] = product[give].astype(jnp.bfloat16)
            pair_copy(t).start()
            load_down(t).start()

        @pl.when(stage(t, lag_feed))
        def _():
            j = t - lag_feed
            x_copy(j, near_start, near_pair_sem, partner).wait_recv()
            x_copy(j, far_start, far_pair_sem, partner).wait_recv()

            @pl.when(j % FEED_GROUP == FEED_GROUP - 1)
            def _():
                g = j // FEED_GROUP
                load_gate(g).wait()
                load_up(g).wait()
                last = (((1,), (1,)), ((), ()))
                gate_sum[...] += lax.dot_general(
                    gate_w[g % slots], x[g], last, preferred_element_type=jnp.float32
                )
                up_sum[...] += lax.dot_general(
                    up_w[g % slots], x[g], last, preferred_element_type=jnp.float32
                )

                @pl.when(g + slots < n_chunks // FEED_GROUP)
                def _():
                    load_gate(g + slots).start()
                    load_up(g + slots).start()

        return carry

    lax.fori_loop(0, n_chunks + lag_feed, step, 0)
    spread_copy(near_start, near_pair_sem, partner).wait_recv()
    spread_copy(far_start, far_pair_sem, partner).wait_recv()
    scale = jnp.transpose(spread[...])[0:1]
    units = gate_sum.shape[0]
    for start in range(0, units, HEAD_WIDTH):
        stop = min(start + HEAD_WIDTH, units)
        gate = gate_sum[start:stop] * scale
        upward = up_sum[start:stop] * scale
        block = gate / (1.0 + jnp.exp(-gate)) * upward
        active[:, start:stop] = jnp.transpose(block).astype(jnp.bfloat16)

    near_chip = chip + 1 - 2 * side
    outer_chip = 3 * side
    other_outer = 3 - outer_chip
    other_inner = 3 - chip

    def rows_pair_copy(j):
        return remote(rows_pair_out.at[j], rows_pair_in.at[j], rows_pair_sem, j, partner)

    def rows_outer_copy(j):
        return remote(rows_outer_out.at[j], rows_outer_in.at[j], rows_outer_sem, j, near_device)

    def rows_cross_copy(j):
        return remote(rows_cross_out.at[j], rows_cross_in.at[j], rows_cross_sem, j, near_device)

    def rows_last_copy(j, device):
        return remote(rows_last_out.at[j], rows_last_in.at[j], rows_last_sem, j, device)

    lag_last = lag_cross + HOP_LAG

    def rows_step(t, carry):
        @pl.when(stage(t, lag_last, outer))
        def _():
            j = t - lag_last
            rows_last_copy(j, near_device).wait_recv()
            out_ref[:, columns(j)] = (
                rows_own[j, chip] + rows_last_in[j].astype(jnp.float32)
            ).astype(jnp.bfloat16)

        @pl.when(stage(t, lag_cross, inner))
        def _():
            j = t - lag_cross
            rows_cross_copy(j).wait_recv()
            rows_last_out[j] = (
                rows_own[j, outer_chip] + rows_cross_in[j, 1].astype(jnp.float32)
            ).astype(jnp.bfloat16)
            rows_last_copy(j, outer_device).start()
            out_ref[:, columns(j)] = (
                rows_own[j, chip] + rows_cross_in[j, 0].astype(jnp.float32)
            ).astype(jnp.bfloat16)

        @pl.when(stage(t, lag_outer, inner))
        def _():
            j = t - lag_outer
            rows_outer_copy(j).wait_recv()
            rows_cross_out[j, 0] = (
                rows_own[j, other_inner] + rows_outer_in[j, 1].astype(jnp.float32)
            ).astype(jnp.bfloat16)
            rows_cross_out[j, 1] = (
                rows_own[j, other_outer] + rows_outer_in[j, 2].astype(jnp.float32)
            ).astype(jnp.bfloat16)
            rows_cross_copy(j).start()
            rows_own[j, chip] += rows_outer_in[j, 0].astype(jnp.float32)

        @pl.when(stage(t, PAIR_LAG))
        def _():
            j = t - PAIR_LAG
            rows_pair_copy(j).wait_recv()
            for k in range(4):
                rows_own[j, k] += rows_pair_in[j, k].astype(jnp.float32)

            @pl.when(outer)
            def _():
                for k in range(3):
                    target = (1 - side) * (1 + k) + side * (2 - k)
                    rows_outer_out[j, k] = rows_own[j, target].astype(jnp.bfloat16)
                rows_outer_copy(j).start()

        @pl.when(t < n_chunks)
        def _():
            load_down(t).wait()
            product[...] = jnp.dot(active[...], w_down[t], preferred_element_type=jnp.float32)

            @pl.when(inner)
            def _():
                product[pl.ds(near_start, part)] += middle[t].astype(jnp.float32)

            for k in range(4):
                keep = pl.ds(pl.multiple_of((2 * k + core) * own_rows, own_rows), own_rows)
                give = pl.ds(pl.multiple_of((2 * k + 1 - core) * own_rows, own_rows), own_rows)
                rows_own[t, k] = product[keep]
                rows_pair_out[t, k] = product[give].astype(jnp.bfloat16)
            rows_pair_copy(t).start()

        return carry

    lax.fori_loop(0, n_chunks + lag_last, rows_step, 0)

    def finish(j, carry):
        pair_copy(j).wait_send()
        rows_pair_copy(j).wait_send()
        x_copy(j, near_start, near_pair_sem, partner).wait_send()
        x_copy(j, far_start, far_pair_sem, partner).wait_send()

        @pl.when(outer)
        def _():
            outer_copy(j).wait_send()
            rows_outer_copy(j).wait_send()

        @pl.when(inner)
        def _():
            cross_copy(j).wait_send()
            x_copy(j, near_start, near_sem, outer_device).wait_send()
            x_copy(j, near_start, far_sem, near_device).wait_send()
            x_copy(j, far_start, far_out_sem, outer_device).wait_send()
            rows_cross_copy(j).wait_send()
            rows_last_copy(j, outer_device).wait_send()

        return carry

    lax.fori_loop(0, n_chunks, finish, 0)
    spread_copy(near_start, near_pair_sem, partner).wait_send()
    spread_copy(far_start, far_pair_sem, partner).wait_send()

    @pl.when(inner)
    def _():
        spread_copy(near_start, near_sem, outer_device).wait_send()
        spread_copy(near_start, far_sem, near_device).wait_send()
        spread_copy(far_start, far_out_sem, outer_device).wait_send()


def tail(attn, hidden, gain, w_out, w_gate, w_up, w_down, collective_id):
    tokens, inner = attn.shape
    own_rows, model = hidden.shape
    units = w_down.shape[0]
    chunk = TAIL_CHUNK
    n_chunks = model // chunk
    slots = 3
    part = tokens // 4
    bf16, f32 = jnp.bfloat16, jnp.float32
    vmem = pl.BlockSpec(memory_space=pltpu.VMEM)
    hbm = pl.BlockSpec(memory_space=pl.ANY)

    def remote_sem(count):
        return pltpu.SemaphoreType.DMA((2, count))

    return pl.pallas_call(
        functools.partial(tail_kernel, n_chunks),
        out_shape=jax.ShapeDtypeStruct((own_rows, model), bf16),
        in_specs=[vmem, vmem, vmem, hbm, hbm, hbm, hbm],
        out_specs=vmem,
        scratch_shapes=[
            pltpu.VMEM((n_chunks, inner, chunk), bf16),
            pltpu.VMEM((slots, units, FEED_GROUP * chunk), bf16),
            pltpu.VMEM((slots, units, FEED_GROUP * chunk), bf16),
            pltpu.VMEM((n_chunks, units, chunk), bf16),
            pltpu.VMEM((tokens, chunk), f32),
            pltpu.VMEM((n_chunks, 2, part, chunk), f32),
            pltpu.VMEM((n_chunks, 2, part, chunk), bf16),
            pltpu.VMEM((n_chunks, 2, part, chunk), bf16),
            pltpu.VMEM((n_chunks, 2, part, chunk), bf16),
            pltpu.VMEM((n_chunks, 2, part, chunk), bf16),
            pltpu.VMEM((n_chunks, part, chunk), bf16),
            pltpu.VMEM((n_chunks, part, chunk), bf16),
            pltpu.VMEM((n_chunks, part, chunk), bf16),
            pltpu.VMEM((part, HEAD_WIDTH), f32),
            pltpu.VMEM((n_chunks // FEED_GROUP, tokens, FEED_GROUP * chunk), bf16),
            pltpu.VMEM((tokens, HEAD_WIDTH), f32),
            pltpu.VMEM((units, tokens), f32),
            pltpu.VMEM((units, tokens), f32),
            pltpu.VMEM((tokens, units), bf16),
            pltpu.VMEM((n_chunks, 4, own_rows, chunk), f32),
            pltpu.VMEM((n_chunks, 4, own_rows, chunk), bf16),
            pltpu.VMEM((n_chunks, 4, own_rows, chunk), bf16),
            pltpu.VMEM((n_chunks, 3, own_rows, chunk), bf16),
            pltpu.VMEM((n_chunks, 3, own_rows, chunk), bf16),
            pltpu.VMEM((n_chunks, 2, own_rows, chunk), bf16),
            pltpu.VMEM((n_chunks, 2, own_rows, chunk), bf16),
            pltpu.VMEM((n_chunks, own_rows, chunk), bf16),
            pltpu.VMEM((n_chunks, own_rows, chunk), bf16),
            pltpu.SemaphoreType.DMA((4, n_chunks)),
        ]
        + [remote_sem(n_chunks)] * 3
        + [remote_sem(n_chunks + 1)] * 5
        + [remote_sem(n_chunks)] * 4,
        compiler_params=pltpu.CompilerParams(
            collective_id=collective_id, has_side_effects=True, vmem_limit_bytes=62 << 20
        ),
        name="tail%d" % collective_id,
    )(
        attn,
        hidden,
        gain.reshape(1, model),
        w_out,
        jnp.transpose(w_gate),
        jnp.transpose(w_up),
        w_down,
    )


def attend_pair(key, value, new_key, new_value, query, limit, row_start, tokens):
    length = key.shape[0]
    fresh = new_key.shape[0]
    width = query.shape[0]
    last = (((1,), (1,)), ((), ()))
    first = (((0,), (0,)), ((), ()))
    old = lax.dot_general(key, query, last, preferred_element_type=jnp.float32)
    new = lax.dot_general(new_key, query, last, preferred_element_type=jnp.float32)
    old_ids = lax.broadcasted_iota(jnp.int32, (length, 1), 0)
    old = jnp.where(old_ids < limit, old, -1e30)
    new_ids = lax.broadcasted_iota(jnp.int32, (fresh, width), 0) + row_start
    token_ids = lax.broadcasted_iota(jnp.int32, (fresh, width), 1) % tokens
    new = jnp.where(new_ids <= token_ids, new, -1e30)
    top = jnp.maximum(jnp.max(old, axis=0, keepdims=True), jnp.max(new, axis=0, keepdims=True))
    top = jnp.maximum(top, -1e29)
    old = jnp.exp((old - top) * SCALE)
    new = jnp.exp((new - top) * SCALE)
    total = jnp.sum(old, axis=0, keepdims=True) + jnp.sum(new, axis=0, keepdims=True)
    sums = lax.dot_general(
        value, old.astype(jnp.bfloat16), first, preferred_element_type=jnp.float32
    ) + lax.dot_general(
        new_value, new.astype(jnp.bfloat16), first, preferred_element_type=jnp.float32
    )
    return pack_sums(sums, total, top).astype(jnp.bfloat16)


def head_kernel(
    n_chunks,
    info_ref,
    hidden_ref,
    gain_ref,
    bias_ref,
    cos_half_ref,
    sin_half_ref,
    weight_hbm,
    key_hbm,
    value_hbm,
    attn_ref,
    new_key_ref,
    new_value_ref,
    weight,
    key_cache,
    value_cache,
    cos_ref,
    sin_ref,
    x,
    total,
    pairs,
    query,
    fresh_in,
    sums,
    pair_in,
    up_in,
    down_in,
    load_sem,
    x_up_sem,
    x_down_sem,
    x_recv,
    x_pair_sem,
    q_up_sem,
    q_down_sem,
    q_recv,
    q_pair_sem,
    fresh_send,
    fresh_recv,
    sums_pair_sem,
    sums_up_sem,
    sums_down_sem,
):
    me = lax.axis_index("head")
    chip = me // 2
    core = me % 2
    chips = 4
    size = 8
    partner = chip * 2 + (1 - core)
    tokens = x.shape[1]
    own_rows = hidden_ref.shape[0]
    chunk = x.shape[2]
    length = key_cache.shape[0]
    groups = 3
    n_pairs = QUERY_HEADS // 2
    width = 2 * HEAD_WIDTH
    first_kv = n_pairs // groups
    mine = pl.ds(pl.multiple_of(me * own_rows, own_rows), own_rows)

    def columns(j):
        return pl.ds(pl.multiple_of(j * chunk, chunk), chunk)

    def load_weight(j):
        return pltpu.make_async_copy(weight_hbm.at[columns(j)], weight.at[j], load_sem.at[j])

    def load_key():
        return pltpu.make_async_copy(key_hbm, key_cache, load_sem.at[n_chunks])

    def load_value():
        return pltpu.make_async_copy(value_hbm, value_cache, load_sem.at[n_chunks + 1])

    def remote(src, dst, send, recv, device):
        return pltpu.make_async_remote_copy(
            src_ref=src,
            dst_ref=dst,
            send_sem=send,
            recv_sem=recv,
            device_id={"head": device},
            device_id_type=MESH,
        )

    def begin(j, carry):
        load_weight(j).start()
        return carry

    lax.fori_loop(0, n_chunks, begin, 0)
    load_key().start()
    load_value().start()

    barrier = pltpu.get_barrier_semaphore()

    def greet(k, carry):
        pl.semaphore_signal(
            barrier, inc=1, device_id={"head": (me + k) % size}, device_id_type=MESH
        )
        return carry

    lax.fori_loop(1, size, greet, 0)
    data = hidden_ref[...].astype(jnp.float32)
    mean = jnp.mean(data * data, axis=-1, keepdims=True)
    normed = (data * lax.rsqrt(mean + 1e-06) * gain_ref[...]).astype(jnp.bfloat16)
    for j in range(n_chunks):
        x[j, mine] = normed[:, j * chunk : (j + 1) * chunk]
    total[...] = jnp.zeros_like(total)
    cosine = cos_half_ref[...]
    sine = sin_half_ref[...]
    cos_ref[...] = jnp.concatenate([cosine, cosine], axis=1)
    sin_ref[...] = jnp.concatenate([-sine, sine], axis=1)
    pl.semaphore_wait(barrier, size - 1)

    def x_block(j, owner_device):
        return x.at[j, pl.ds(pl.multiple_of(owner_device * own_rows, own_rows), own_rows)]

    def x_up(j, owner):
        block = x_block(j, owner * 2 + core)
        return remote(block, block, x_up_sem.at[owner, j], x_recv.at[owner, j], me + 2)

    def x_down(j, owner):
        block = x_block(j, owner * 2 + core)
        return remote(block, block, x_down_sem.at[owner, j], x_recv.at[owner, j], me - 2)

    def x_pair(j, owner):
        block = x_block(j, owner * 2 + core)
        return remote(block, block, x_pair_sem.at[0, owner, j], x_pair_sem.at[1, owner, j], partner)

    def send_x(j, carry):
        @pl.when(chip < chips - 1)
        def _():
            x_up(j, chip).start()

        @pl.when(chip > 0)
        def _():
            x_down(j, chip).start()

        x_pair(j, chip).start()
        return carry

    def gather_step(t, carry):
        s = 1 + t // n_chunks
        j = t % n_chunks

        @pl.when(chip - s >= 0)
        def _():
            x_up(j, chip - s).wait_recv()

            @pl.when(chip < chips - 1)
            def _():
                x_up(j, chip - s).start()

            x_pair(j, chip - s).start()

        @pl.when(chip + s <= chips - 1)
        def _():
            x_down(j, chip + s).wait_recv()

            @pl.when(chip > 0)
            def _():
                x_down(j, chip + s).start()

            x_pair(j, chip + s).start()

        done = t - (chips - 2) * n_chunks - 1

        @pl.when(done >= 0)
        def _():
            multiply(done)

        return carry

    def multiply(j):
        for owner in range(chips):
            x_pair(j, owner).wait_recv()
        load_weight(j).wait()
        total[...] += jnp.dot(x[j], weight[j], preferred_element_type=jnp.float32)

    lax.fori_loop(0, n_chunks, send_x, 0)
    lax.fori_loop(0, (chips - 1) * n_chunks, gather_step, 0)
    multiply(n_chunks - 1)

    def q_up(p):
        return remote(query.at[p], query.at[p], q_up_sem.at[p], q_recv.at[p], me + 2)

    def q_down(p):
        return remote(query.at[p], query.at[p], q_down_sem.at[p], q_recv.at[p], me - 2)

    def q_pair(p):
        return remote(query.at[p], query.at[p], q_pair_sem.at[0, p], q_pair_sem.at[1, p], partner)

    def fresh_copy(target):
        rows = pl.ds(pl.multiple_of(target * own_rows, own_rows), own_rows)
        source = me - first_kv
        return remote(
            pairs.at[:, rows], fresh_in.at[source], fresh_send.at[target], fresh_recv.at[source], target
        )

    def fresh_wait(source):
        return remote(
            pairs.at[:, pl.ds(0, own_rows)],
            fresh_in.at[source],
            fresh_send.at[0],
            fresh_recv.at[source],
            partner,
        ).wait_recv()

    def send_own(i):
        p = me * groups + i

        @pl.when(p < n_pairs)
        def _():
            @pl.when(chip < chips - 1)
            def _():
                q_up(p).start()

            @pl.when(chip > 0)
            def _():
                q_down(p).start()

            q_pair(p).start()

    def prepare(i, carry):
        piece = pl.ds(pl.multiple_of(i * width, width), width)
        raw = (total[:, piece] + bias_ref[:, piece].astype(jnp.float32)).astype(jnp.bfloat16)
        pairs[i] = raw

        @pl.when(me * groups + i < n_pairs)
        def _():
            for h in range(2):
                values = raw[:, h * HEAD_WIDTH : (h + 1) * HEAD_WIDTH].astype(jnp.float32)
                turned = pltpu.roll(values, HEAD_WIDTH // 2, 1)
                query[me * groups + i, h * tokens : (h + 1) * tokens] = (
                    values * cos_ref[...] + turned * sin_ref[...]
                ).astype(jnp.bfloat16)

        @pl.when((i == 0) | (chip != 1))
        def _():
            send_own(i)

        return carry

    lax.fori_loop(0, groups, prepare, 0)

    @pl.when(me >= first_kv)
    def _():
        for k in range(1, size):
            fresh_copy((me + k) % size).start()
        fresh_in[me - first_kv] = pairs[:, mine]

    load_key().wait()
    load_value().wait()

    def wait_fresh():
        for source in range(size - first_kv):
            @pl.when(me != first_kv + source)
            def _():
                fresh_wait(source)

        for k in range(n_pairs // 4):
            place = n_pairs + k
            block = fresh_in[place // groups - first_kv, place % groups].astype(jnp.float32)
            for h in range(2):
                values = block[:, h * HEAD_WIDTH : (h + 1) * HEAD_WIDTH]
                turned = pltpu.roll(values, HEAD_WIDTH // 2, 1)
                head = 2 * k + h
                new_key_ref[:, head * HEAD_WIDTH : (head + 1) * HEAD_WIDTH] = (
                    values * cos_ref[mine] + turned * sin_ref[mine]
                ).astype(jnp.bfloat16)
            place = n_pairs + n_pairs // 4 + k
            new_value_ref[:, k * width : (k + 1) * width] = fresh_in[
                place // groups - first_kv, place % groups
            ]

    def sums_pair(p):
        return remote(
            sums.at[p], pair_in.at[p], sums_pair_sem.at[0, p], sums_pair_sem.at[1, p], partner
        )

    def sums_up(src, p):
        return remote(src.at[p], up_in.at[p], sums_up_sem.at[0, p], sums_up_sem.at[1, p], me + 2)

    def sums_down(src, p):
        return remote(
            src.at[p], down_in.at[p], sums_down_sem.at[0, p], sums_down_sem.at[1, p], me - 2
        )

    def compute(p):
        head = pl.ds(pl.multiple_of((p // 2) * HEAD_WIDTH, HEAD_WIDTH), HEAD_WIDTH)
        sums[p] = attend_pair(
            key_cache[:, head],
            value_cache[:, head],
            new_key_ref[:, head],
            new_value_ref[:, head],
            query[p],
            info_ref[0],
            me * own_rows,
            tokens,
        )

        @pl.when((p // 2) % 2 != core)
        def _():
            sums_pair(p).start()

    def unit(k):
        after_two = (k + 5) // 8
        after_three = (k + 4) // 8
        after_six = (k + 1) // 8
        owner = 2 - after_two - after_three + after_six
        owner = owner + (2 - 2 * owner) * ((chips - 1 - chip) // (chips - 1))
        return owner, k - 3 * after_two - after_three - 2 * after_six

    def receive(k):
        owner, i = unit(k)
        receive_from(owner, i)

    def receive_from(owner, i):
        p = (owner * 2 + core) * groups + i

        @pl.when((p < n_pairs) & (owner < chip))
        def _():
            q_up(p).wait_recv()

            @pl.when(chip < chips - 1)
            def _():
                q_up(p).start()

            q_pair(p).start()

        @pl.when((p < n_pairs) & (owner > chip))
        def _():
            q_down(p).wait_recv()

            @pl.when(chip > 0)
            def _():
                q_down(p).start()

            q_pair(p).start()

    def attend_unit(k):
        owner, i = unit(k)

        def each(c, carry):
            p = (owner * 2 + c) * groups + i

            @pl.when(p < n_pairs)
            def _():
                @pl.when(c != core)
                def _():
                    q_pair(p).wait_recv()

                compute(p)

            return carry

        lax.fori_loop(0, 2, each, 0)

    def reduce(k, stage):
        owner, i = unit(k)

        def each(c, carry):
            p = (owner * 2 + c) * groups + i
            target = p // 4
            held = (p < n_pairs) & ((p // 2) % 2 == core)

            if stage == 0:

                @pl.when(held)
                def _():
                    sums_pair(p).wait_recv()
                    sums[p] = join_sums(sums[p], pair_in[p]).astype(jnp.bfloat16)

                    @pl.when((chip == 0) & (target > 0))
                    def _():
                        sums_up(sums, p).start()

                    @pl.when((chip == chips - 1) & (target < chips - 1))
                    def _():
                        sums_down(sums, p).start()
            else:

                @pl.when(held & (chip == stage) & (chip < target))
                def _():
                    sums_up(up_in, p).wait_recv()
                    up_in[p] = join_sums(up_in[p], sums[p]).astype(jnp.bfloat16)
                    sums_up(up_in, p).start()

                @pl.when(held & (chips - 1 - chip == stage) & (chip > target))
                def _():
                    sums_down(down_in, p).wait_recv()
                    down_in[p] = join_sums(down_in[p], sums[p]).astype(jnp.bfloat16)
                    sums_down(down_in, p).start()

            return carry

        lax.fori_loop(0, 2, each, 0)

    units = chips * groups - groups

    def attend_step(t, carry):
        @pl.when((chip == 1) & (t < groups))
        def _():
            receive_from(0, t)
            receive_from(2, t)

            @pl.when(t >= groups - 1)
            def _():
                send_own(1)
                send_own(2)

        @pl.when((chip == 2) & (t + ATTEND_LAG < units))
        def _():
            receive(t + ATTEND_LAG)

        @pl.when((t < units) & ((chip == 0) | (chip == chips - 1)))
        def _():
            receive(t)

        for stage in (2, 1, 0):
            k = t - 1 - stage * REDUCE_LAG

            @pl.when((k >= 0) & (k < units))
            def _():
                reduce(k, stage)

        @pl.when(t == 0)
        def _():
            wait_fresh()

        @pl.when(t < units)
        def _():
            attend_unit(t)

        return carry

    lax.fori_loop(0, units + 1 + 2 * REDUCE_LAG, attend_step, 0)

    for k in range(2):
        p = me * 2 + k

        @pl.when(chip > 0)
        def _():
            sums_up(up_in, p).wait_recv()
            sums[p] = join_sums(sums[p], up_in[p]).astype(jnp.bfloat16)

        @pl.when(chip < chips - 1)
        def _():
            sums_down(down_in, p).wait_recv()

        @pl.when(chip == chips - 1)
        def _():
            down_in[p] = sums[p]

        block = down_in[p]

        @pl.when(chip < chips - 1)
        def _():
            down_in[p] = join_sums(sums[p], block).astype(jnp.bfloat16)

        mixed = down_in[p].astype(jnp.float32)
        bottom = mixed[HEAD_WIDTH : HEAD_WIDTH + 1] + mixed[HEAD_WIDTH + 1 : HEAD_WIDTH + 2]
        result = jnp.transpose(mixed[:HEAD_WIDTH] / bottom).astype(jnp.bfloat16)
        for h in range(2):
            head = 2 * k + h
            attn_ref[:, head * HEAD_WIDTH : (head + 1) * HEAD_WIDTH] = result[
                h * tokens : (h + 1) * tokens
            ]

    def finish_x(n, carry):
        owner = n // n_chunks
        j = n % n_chunks
        x_pair(j, owner).wait_send()

        @pl.when((chip < chips - 1) & (owner <= chip))
        def _():
            x_up(j, owner).wait_send()

        @pl.when((chip > 0) & (owner >= chip))
        def _():
            x_down(j, owner).wait_send()

        return carry

    lax.fori_loop(0, chips * n_chunks, finish_x, 0)

    def finish_pairs(p, carry):
        device = p // groups
        owner = device // 2

        @pl.when(device % 2 == core)
        def _():
            q_pair(p).wait_send()

            @pl.when((chip < chips - 1) & (owner <= chip))
            def _():
                q_up(p).wait_send()

            @pl.when((chip > 0) & (owner >= chip))
            def _():
                q_down(p).wait_send()

        target = p // 4

        @pl.when((p // 2) % 2 != core)
        def _():
            sums_pair(p).wait_send()

        @pl.when((p // 2) % 2 == core)
        def _():
            @pl.when(chip < target)
            def _():
                sums_up(sums, p).wait_send()

            @pl.when(chip > target)
            def _():
                sums_down(sums, p).wait_send()

        return carry

    lax.fori_loop(0, n_pairs, finish_pairs, 0)

    @pl.when(me >= first_kv)
    def _():
        for k in range(1, size):
            fresh_copy((me + k) % size).wait_send()


def head(info, hidden, gain, bias, cosine, sine, weight, key_cache, value_cache, collective_id):
    own_rows, model = hidden.shape
    tokens = cosine.shape[0]
    columns = weight.shape[1]
    length, cached = key_cache.shape
    chunk = HEAD_CHUNK
    n_chunks = model // chunk
    n_pairs = QUERY_HEADS // 2
    groups = 3
    width = 2 * HEAD_WIDTH
    bf16, f32 = jnp.bfloat16, jnp.float32
    vmem = pl.BlockSpec(memory_space=pltpu.VMEM)
    smem = pl.BlockSpec(memory_space=pltpu.SMEM)
    hbm = pl.BlockSpec(memory_space=pl.ANY)
    dma = pltpu.SemaphoreType.DMA
    block = pltpu.VMEM((n_pairs, HEAD_WIDTH + TAIL, 2 * tokens), bf16)
    return pl.pallas_call(
        functools.partial(head_kernel, n_chunks),
        out_shape=[
            jax.ShapeDtypeStruct((tokens, 4 * HEAD_WIDTH), bf16),
            jax.ShapeDtypeStruct((own_rows, cached), bf16),
            jax.ShapeDtypeStruct((own_rows, cached), bf16),
        ],
        in_specs=[smem, vmem, vmem, vmem, vmem, vmem, hbm, hbm, hbm],
        out_specs=[vmem, vmem, vmem],
        scratch_shapes=[
            pltpu.VMEM((n_chunks, chunk, columns), bf16),
            pltpu.VMEM((length, cached), bf16),
            pltpu.VMEM((length, cached), bf16),
            pltpu.VMEM((tokens, HEAD_WIDTH), f32),
            pltpu.VMEM((tokens, HEAD_WIDTH), f32),
            pltpu.VMEM((n_chunks, tokens, chunk), bf16),
            pltpu.VMEM((tokens, columns), f32),
            pltpu.VMEM((groups, tokens, width), bf16),
            pltpu.VMEM((n_pairs, 2 * tokens, HEAD_WIDTH), bf16),
            pltpu.VMEM((3, groups, own_rows, width), bf16),
            block,
            block,
            block,
            block,
            dma((n_chunks + 2,)),
            dma((4, n_chunks)),
            dma((4, n_chunks)),
            dma((4, n_chunks)),
            dma((2, 4, n_chunks)),
            dma((n_pairs,)),
            dma((n_pairs,)),
            dma((n_pairs,)),
            dma((2, n_pairs)),
            dma((8,)),
            dma((3,)),
            dma((2, n_pairs)),
            dma((2, n_pairs)),
            dma((2, n_pairs)),
        ],
        compiler_params=pltpu.CompilerParams(
            collective_id=collective_id, has_side_effects=True, vmem_limit_bytes=62 << 20
        ),
        name="head%d" % collective_id,
    )(
        info,
        hidden,
        gain.reshape(1, model),
        bias.astype(f32).reshape(1, columns),
        cosine,
        sine,
        weight,
        key_cache,
        value_cache,
    )


def pass_on_kernel(*refs):
    count = len(refs) // 2
    for source, target in zip(refs[:count], refs[count:]):
        target[...] = source[...]


def pass_on(*arrays):
    vmem = pl.BlockSpec(memory_space=pltpu.VMEM)
    return pl.pallas_call(
        pass_on_kernel,
        out_shape=[jax.ShapeDtypeStruct(a.shape, a.dtype) for a in arrays],
        in_specs=[vmem] * len(arrays),
        out_specs=[vmem] * len(arrays),
        name="pass_on",
    )(*arrays)


def on_device(
    hidden,
    cached_len,
    attn_gain,
    query_key_value_weight,
    b_qkv,
    key_cache,
    value_cache,
    w_out,
    ffn_gain,
    w_gate,
    w_up,
    w_down,
):
    size = lax.axis_size("head")
    index_here = lax.axis_index("head")
    own_rows = hidden[0]
    fresh, model = own_rows.shape
    tokens = fresh * size
    heads_here = QUERY_HEADS // size
    row_start = index_here * fresh
    cache_length = key_cache.shape[1]
    key_start = QUERY_HEADS * HEAD_WIDTH
    coarse = max(fresh // 16, 1)

    positions = cached_len[0] + jnp.arange(tokens, dtype=jnp.int32)

    if size == 8 and fresh == 32:
        cosine, sine = rope_halves(positions)
        info = jnp.reshape(cached_len[0] - index_here * cache_length, (1,)).astype(jnp.int32)
        attn, new_keys, new_values = head(
            info,
            own_rows,
            attn_gain,
            b_qkv,
            cosine,
            sine,
            query_key_value_weight,
            key_cache[0],
            value_cache[0],
            2,
        )
        result = tail(attn, own_rows, ffn_gain, w_out, w_gate, w_up, w_down, 7)
        result, new_keys, new_values = pass_on(result, new_keys, new_values)
    else:
        cosine, sine = rope_tables(positions)
        own_cosine = lax.dynamic_slice_in_dim(cosine, row_start, fresh, 0)[:, None, :]
        own_sine = lax.dynamic_slice_in_dim(sine, row_start, fresh, 0)[:, None, :]
        normed = gather(rms_norm(own_rows, attn_gain), size, coarse, 0).reshape(tokens, model)
        qkv_part = (
            jnp.dot(normed, query_key_value_weight, preferred_element_type=jnp.float32)
            + b_qkv.astype(jnp.float32)
        ).astype(jnp.bfloat16)
        qkv = jnp.transpose(gather(qkv_part, size, 4, 1), (1, 0, 2)).reshape(tokens, -1)
        own = lax.dynamic_slice(
            qkv, (row_start, key_start), (fresh, 2 * KEY_VALUE_HEADS * HEAD_WIDTH)
        )
        key_data = own[:, : KEY_VALUE_HEADS * HEAD_WIDTH].astype(jnp.float32)
        key_data = key_data.reshape(fresh, KEY_VALUE_HEADS, HEAD_WIDTH)
        turned = jnp.roll(key_data, HEAD_WIDTH // 2, axis=-1)
        new_keys = (key_data * own_cosine + turned * own_sine).astype(jnp.bfloat16)
        new_keys = new_keys.reshape(fresh, KEY_VALUE_HEADS * HEAD_WIDTH)
        new_values = own[:, KEY_VALUE_HEADS * HEAD_WIDTH :]

        info = jnp.stack([cached_len[0] - index_here * cache_length, row_start]).astype(jnp.int32)
        sums = attend(info, qkv, key_cache[0], value_cache[0], new_keys, new_values, cosine, sine)
        sums = sums.reshape(size, heads_here, HEAD_WIDTH + TAIL, tokens)
        mixed = scatter(sums, size, join_sums, 3)
        total = mixed[:, HEAD_WIDTH : HEAD_WIDTH + 1] + mixed[:, HEAD_WIDTH + 1 : HEAD_WIDTH + 2]
        attn = (mixed[:, :HEAD_WIDTH] / total).astype(jnp.bfloat16)
        attn = jnp.transpose(attn, (2, 0, 1)).reshape(tokens, heads_here * HEAD_WIDTH)
        projected = jnp.dot(attn, w_out, preferred_element_type=jnp.float32).astype(jnp.bfloat16)
        blocks = (size, coarse, fresh // coarse, model)
        projected = scatter(projected.reshape(blocks), size, add_blocks, 4).reshape(fresh, model)
        middle = (own_rows.astype(jnp.float32) + projected).astype(jnp.bfloat16)
        normed_two = gather(rms_norm(middle, ffn_gain), size, coarse, 5).reshape(tokens, model)
        ffn_part = feed(normed_two, w_gate, w_up, w_down)
        ffn_sum = scatter(ffn_part.reshape(blocks), size, add_blocks, 6).reshape(fresh, model)
        result = (middle.astype(jnp.float32) + ffn_sum).astype(jnp.bfloat16)
    return (result[None], new_keys[None], new_values[None])


def solution(mesh):
    in_specs = (
        P("req", "head", None),
        P("req"),
        P(),
        P(None, "head"),
        P("head"),
        P("req", "head", None),
        P("req", "head", None),
        P("head", None),
        P(),
        P(None, "head"),
        P(None, "head"),
        P("head", None),
    )
    out_specs = (P("req", "head", None), P("req", "head", None), P("req", "head", None))
    return jax.shard_map(
        on_device, mesh=mesh, in_specs=in_specs, out_specs=out_specs, check_vma=False
    )
```
